32 devices in a mesh: grp: 4 (over z), dev: 8 (over y, x, core).
Axes of the slice: x: 2, y: 2, z: 4, core: 2. Of those that a mesh axis runs over, the one named last changes fastest.
Arguments:
- atoms: bfloat16 [8192, 768], P(('grp', 'dev')), may hold values from -6 to 6
- positions: float32 [3, 8192], P(None, ('grp', 'dev')), may hold values from -6 to 6
- segment: int32 [8192], P(('grp', 'dev')), may hold values from 0 to 8191, as said below
- item_time: float32 [8192], P(('grp', 'dev')), may hold values from 0 to 1, as said below
- time_weight: bfloat16 [128, 768], P(None, ('grp', 'dev')), may hold values from -0.5 to 0.5
- norm1_gain: bfloat16 [768], P(('grp', 'dev')), may hold values from 0.5 to 1.5
- norm1_bias: bfloat16 [768], P(('grp', 'dev')), may hold values from -3 to 3
- qkv_weight: bfloat16 [768, 2304], P(('grp', 'dev')), may hold values from -0.21875 to 0.21875
- out_weight: bfloat16 [768, 768], P(('grp', 'dev')), may hold values from -1.75 to 1.75
- norm2_gain: bfloat16 [768], P(('grp', 'dev')), may hold values from 0.5 to 1.5
- norm2_bias: bfloat16 [768], P(('grp', 'dev')), may hold values from -3 to 3
- ffn_in: bfloat16 [768, 3072], P(('grp', 'dev')), may hold values from -0.21875 to 0.21875
- ffn_in_bias: bfloat16 [3072], P(('grp', 'dev')), may hold values from -3 to 3
- ffn_out: bfloat16 [3072, 768], P(('grp', 'dev')), may hold values from -0.109375 to 0.109375
- ffn_out_bias: bfloat16 [768], P(('grp', 'dev')), may hold values from -3 to 3
- pair_weight: bfloat16 [128, 32], replicated, may hold values from -4 to 4
- kernel_mean: float32 [128], replicated, may hold values from 0 to 12
- kernel_width: float32 [128], replicated, may hold values from 0.5 to 3
- cotangent: bfloat16 [8192, 768], P(('grp', 'dev')), may hold values from -6 to 6
Outputs:
- output: bfloat16 [8192, 768], P(('grp', 'dev'))
- grad_atoms: float32 [8192, 768], P(('grp', 'dev'))
- grad_time_weight: float32 [128, 768], P(None, ('grp', 'dev'))
- grad_norm1_gain: float32 [768], P(('grp', 'dev'))
- grad_norm1_bias: float32 [768], P(('grp', 'dev'))
- grad_qkv_weight: float32 [768, 2304], P(('grp', 'dev'))
- grad_out_weight: float32 [768, 768], P(('grp', 'dev'))
- grad_norm2_gain: float32 [768], P(('grp', 'dev'))
- grad_norm2_bias: float32 [768], P(('grp', 'dev'))
- grad_ffn_in: float32 [768, 3072], P(('grp', 'dev'))
- grad_ffn_in_bias: float32 [3072], P(('grp', 'dev'))
- grad_ffn_out: float32 [3072, 768], P(('grp', 'dev'))
- grad_ffn_out_bias: float32 [768], P(('grp', 'dev'))
- grad_pair_weight: float32 [128, 32], replicated
- grad_kernel_mean: float32 [128], replicated
- grad_kernel_width: float32 [128], replicated
The draws below stay inside these ranges and needn't reach their ends.
Inputs may be any that keep to these rules, and one draw needn't show every extreme that they name: `segment`: an atom's item number is the index of the last atom of its item; numbers never fall along the atoms; each item is a run of equal numbers inside one aligned block of 1024 atoms and holds 1 to 1024 atoms; in every draw some block is one item of 1024 atoms. `item_time`: equal for all atoms of one item.
All inputs are finite; a program needn't handle non-finite values.
Results may differ from the reference program's by a relative error of at most 0.012.
The reference program's roundings to bfloat16 on the way count: a program that leaves them out, or rounds other values in their place, can miss the bound.
Values may be sent and summed in bfloat16 or wider, within the bound.
A program may use at most 256 MiB of HBM per device.

```python
import math
import jax
import jax.numpy as jnp
from jax import lax

D = 768
HEADS = 32
HDIM = 24
FF = 3072
KERN = 128
TFREQ = 128
BIN = 1024
TOKENS = 8192


def item_labels(key):
    bin_total = TOKENS // BIN
    key_kind, key_force, key_cuts = jax.random.split(jax.random.fold_in(key, 7), 3)
    bin_index = jnp.arange(bin_total)
    is_protein = jax.random.randint(key_kind, (bin_total,), 0, 4) == 0
    forced_bin = jax.random.randint(key_force, (), 1, bin_total)
    is_protein = (is_protein | (bin_index == forced_bin)) & (bin_index != 0)
    slot_index = jnp.arange(BIN)
    cut_marks = jax.random.randint(key_cuts, (bin_total, BIN), 0, max(BIN // 8, 2)) == 0
    forced_cut = (bin_index[:, None] == 0) & (slot_index[None, :] == 1)
    cut_marks = (cut_marks | forced_cut) & jnp.logical_not(is_protein[:, None]) & (slot_index[None, :] != 0)
    next_cut = jnp.concatenate([cut_marks[:, 1:], jnp.ones((bin_total, 1), dtype=bool)], axis=1)
    end_slot = jnp.where(next_cut, slot_index[None, :], BIN).astype(jnp.int32)
    item_end = lax.cummin(end_slot, axis=1, reverse=True)
    labels = bin_index.astype(jnp.int32)[:, None] * BIN + item_end
    return labels.reshape(-1).astype(jnp.int32)


def draw_segment(key, part):
    return item_labels(key)


def draw_item_time(key, part):
    labels = item_labels(key)
    time_table = jax.random.uniform(jax.random.fold_in(key, 11), (TOKENS,), jnp.float32)
    return time_table[labels]


def block_scale(stream_key, extent, cuts, low, largest):
    level, own = 1.0, jax.random.fold_in(stream_key, 6)
    for axis_at, parts in cuts:
        draws = jnp.exp(jax.random.uniform(jax.random.fold_in(own, axis_at), (parts,), jnp.float32, low / len(cuts), largest / len(cuts)))
        level = level * jnp.repeat(draws, extent[axis_at] // parts).reshape([-1 if axis == axis_at else 1 for axis in range(len(extent))])
    return level


def bell_draw(rng, extent, deviation, most, cuts=(), kind=jnp.bfloat16):
    level = block_scale(rng, extent, cuts, -0.22, 0.18) if cuts else 1.0
    entries = jax.random.normal(rng, extent, jnp.float32) * deviation * level
    return jnp.minimum(jnp.maximum(entries, -most), most).astype(kind)


def setup_inputs(seed: int = 0) -> dict:
    key_list = jax.random.split(jax.random.key(seed), 20)
    atoms = bell_draw(key_list[0], (TOKENS, D), 1.0, 6.0, ((0, 32),))
    positions = jnp.clip(jax.random.uniform(key_list[1], (3, TOKENS), jnp.float32, -6.0, 6.0) * block_scale(key_list[1], (3, TOKENS), ((1, 32),), -0.4, 0.0), -6.0, 6.0)
    segment = draw_segment(jax.random.fold_in(key_list[19], 71), 0)
    item_time = draw_item_time(jax.random.fold_in(key_list[19], 71), 0)
    time_weight = bell_draw(key_list[4], (TFREQ, D), TFREQ ** -0.5, 0.5, ((1, 32),))
    norm1_gain = jnp.clip(1.0 + 0.1 * jax.random.normal(key_list[5], (D,), jnp.float32), 0.5, 1.5).astype(jnp.bfloat16)
    norm1_bias = bell_draw(key_list[6], (D,), 0.5, 3.0, ((0, 32),))
    qkv_weight = bell_draw(key_list[7], (D, 3 * D), D ** -0.5, 0.21875, ((0, 32),))
    out_weight = bell_draw(key_list[8], (D, D), (D // 64) ** -0.5, 1.75, ((0, 32),))
    norm2_gain = jnp.clip(1.0 + 0.1 * jax.random.normal(key_list[9], (D,), jnp.float32), 0.5, 1.5).astype(jnp.bfloat16)
    norm2_bias = bell_draw(key_list[10], (D,), 0.5, 3.0, ((0, 32),))
    ffn_in = bell_draw(key_list[11], (D, FF), D ** -0.5, 0.21875, ((0, 32),))
    ffn_in_bias = bell_draw(key_list[12], (FF,), 0.5, 3.0, ((0, 32),))
    ffn_out = bell_draw(key_list[13], (FF, D), FF ** -0.5, 0.109375, ((0, 32),))
    ffn_out_bias = bell_draw(key_list[14], (D,), 0.5, 3.0, ((0, 32),))
    pair_weight = bell_draw(key_list[15], (KERN, HEADS), 1.0, 4.0)
    kernel_mean = jnp.clip(jax.random.uniform(key_list[16], (KERN,), jnp.float32, 0.0, 12.0), 0.0, 12.0)
    kernel_width = jnp.clip(jnp.exp(jax.random.uniform(key_list[17], (KERN,), jnp.float32, math.log(0.5), math.log(3.0))), 0.5, 3.0)
    cotangent = bell_draw(key_list[18], (TOKENS, D), 1.0, 6.0, ((0, 32),))
    return dict(atoms=atoms, positions=positions, segment=segment, item_time=item_time, time_weight=time_weight, norm1_gain=norm1_gain, norm1_bias=norm1_bias, qkv_weight=qkv_weight, out_weight=out_weight, norm2_gain=norm2_gain, norm2_bias=norm2_bias, ffn_in=ffn_in, ffn_in_bias=ffn_in_bias, ffn_out=ffn_out, ffn_out_bias=ffn_out_bias, pair_weight=pair_weight, kernel_mean=kernel_mean, kernel_width=kernel_width, cotangent=cotangent)


@jax.custom_vjp
def low(v):
    return lax.optimization_barrier(v.astype(jnp.bfloat16)).astype(jnp.float32)

@jax.custom_vjp
def low_back(v):
    return v

def low_keep(v):
    return (low(v), None)

def low_pass(kept, grad):
    return (grad,)

def back_keep(v):
    return (v, None)

def back_low(kept, grad):
    return (low(grad),)
low.defvjp(low_keep, low_pass)
low_back.defvjp(back_keep, back_low)
highest = lax.Precision.HIGHEST
norm_eps = 1e-05
mask_fill = -1e+30

def layer_norm(values, norm_gain, norm_offset):
    center = values - lax.optimization_barrier(jnp.mean(values, axis=-1, keepdims=True))
    spread = lax.optimization_barrier(jnp.mean(center * center, axis=-1, keepdims=True))
    return center * lax.rsqrt(spread + norm_eps) * norm_gain + norm_offset

def time_features(time_values):
    half_count = TFREQ // 2
    frequency = jnp.exp(jnp.arange(half_count, dtype=jnp.float32) * (-math.log(10000.0) / half_count))
    angles = (1000.0 * time_values)[:, None] * frequency[None, :]
    return jnp.concatenate([jnp.sin(angles), jnp.cos(angles)], axis=1)

def distances(place_rows, place_keys):
    differ = place_rows[:, :, None] - place_keys[:, None, :]
    return jnp.sqrt(lax.optimization_barrier(jnp.sum(differ * differ, axis=0)))

def gaussian(distance, kern_mean, kern_width):
    scaled = (distance[None] - kern_mean[:, None, None]) / kern_width[:, None, None]
    return jnp.exp(-0.5 * scaled * scaled) / (math.sqrt(2.0 * math.pi) * kern_width[:, None, None])

def bin_layer(params, atoms_bin, places_bin, labels_bin, times_bin):
    w_time, gain_one, shift_one, w_qkv, w_out, gain_two, shift_two, w_in, bias_in, w_back, bias_back, w_pair, kern_mean, kern_width = params
    features = low(time_features(times_bin))
    stream_zero = atoms_bin + low_back(jnp.dot(features, w_time, precision=highest))
    normed = low(layer_norm(stream_zero, gain_one, shift_one))
    packed = low(low_back(jnp.dot(normed, w_qkv, precision=highest)))
    query = packed[:, :D].reshape(BIN, HEADS, HDIM)
    key_heads = packed[:, D:2 * D].reshape(BIN, HEADS, HDIM)
    value_heads = packed[:, 2 * D:].reshape(BIN, HEADS, HDIM)
    kernels = low(gaussian(distances(places_bin, places_bin), kern_mean, kern_width))
    bias_heads = jnp.einsum('kij,kh->hij', kernels, w_pair, precision=highest)
    scores = jnp.einsum('ihd,jhd->hij', query, key_heads, precision=highest) * HDIM ** (-0.5) + bias_heads
    scores = low_back(scores)
    same_item = labels_bin[:, None] == labels_bin[None, :]
    scores = jnp.where(same_item[None], scores, mask_fill)
    weights = low(jax.nn.softmax(scores, axis=-1))
    mixed_rows = jnp.einsum('hij,jhd->ihd', weights, value_heads, precision=highest).reshape(BIN, D)
    mixed_rows = low(low_back(mixed_rows))
    stream_one = stream_zero + low_back(jnp.dot(mixed_rows, w_out, precision=highest))
    second = low(layer_norm(stream_one, gain_two, shift_two))
    hidden_pre = low_back(jnp.dot(second, w_in, precision=highest) + bias_in)
    hidden_act = low(jax.nn.gelu(hidden_pre, approximate=False))
    return stream_one + low_back(jnp.dot(hidden_act, w_back, precision=highest) + bias_back)

def reference(atoms, positions, segment, item_time, time_weight, norm1_gain, norm1_bias, qkv_weight, out_weight, norm2_gain, norm2_bias, ffn_in, ffn_in_bias, ffn_out, ffn_out_bias, pair_weight, kernel_mean, kernel_width, cotangent):
    bin_total = TOKENS // BIN
    params = tuple((tensor.astype(jnp.float32) for tensor in (time_weight, norm1_gain, norm1_bias, qkv_weight, out_weight, norm2_gain, norm2_bias, ffn_in, ffn_in_bias, ffn_out, ffn_out_bias, pair_weight, kernel_mean, kernel_width)))
    atoms_input = atoms.astype(jnp.float32).reshape(bin_total, BIN, D)
    places = positions.reshape(3, bin_total, BIN).transpose(1, 0, 2)
    labels = segment.reshape(bin_total, BIN)
    time_bins = item_time.reshape(bin_total, BIN)

    def forward(atoms_in, param_in):

        def one_bin(pieces):
            return bin_layer(param_in, pieces[0], pieces[1], pieces[2], pieces[3])
        return lax.map(jax.checkpoint(one_bin), (atoms_in, places, labels, time_bins))
    result, pullback = jax.vjp(forward, atoms_input, params)
    grad_input, grads = pullback(cotangent.astype(jnp.float32).reshape(bin_total, BIN, D))
    return (result.reshape(TOKENS, D).astype(jnp.bfloat16), grad_input.reshape(TOKENS, D), grads[0], grads[1], grads[2], grads[3], grads[4], grads[5], grads[6], grads[7], grads[8], grads[9], grads[10], grads[11], grads[12], grads[13])
```

```python
import math

import jax
import jax.numpy as jnp
from jax import lax
from jax.experimental import pallas as pl
from jax.experimental.pallas import tpu as pltpu
from jax.sharding import PartitionSpec as P

D = 768
HEADS = 32
HDIM = 24
KERN = 128
TFREQ = 128
BIN = 1024
GROUPS = 4
GHEADS = HEADS // GROUPS
GWIDTH = GHEADS * HDIM
PAIR_ROWS = 8
ATT_ROWS = 128

norm_eps = 1e-05
mask_fill = -1e30
log2e = math.log2(math.e)
center = 6.0
f32 = jnp.float32
bf16 = jnp.bfloat16
VMEM_LIMIT = 56 * 1024 * 1024


def lanes_dot(left, right):
    return lax.dot_general(left, right, (((1,), (1,)), ((), ())), preferred_element_type=f32)


def dot(left, right):
    return jnp.dot(left, right, preferred_element_type=f32)


def pair_block(places_i, segs_i, places_j, segs_j, coef, weight_t, dist_ref, phi_ref, bias_ref, mask_scr):
    square = None
    for axis in range(3):
        gap = places_i[:, axis : axis + 1] - places_j[axis : axis + 1, :]
        square = gap * gap if square is None else square + gap * gap
    dist_ref[...] = jnp.sqrt(square)
    mask_scr[...] = jnp.where(segs_i == segs_j, 0.0, mask_fill).astype(f32)
    for u in range(PAIR_ROWS):
        for kg in range(KERN // 16):
            rows = slice(kg * 16, kg * 16 + 16)
            mean, inv, shift = coef[0, rows, :], coef[1, rows, :], coef[2, rows, :]
            for jv in range(BIN // 128):
                dist = dist_ref[u : u + 1, jv * 128 : jv * 128 + 128]
                z = (dist - mean) * inv
                lanes = slice(u * BIN + jv * 128, u * BIN + jv * 128 + 128)
                phi_ref[rows, lanes] = jnp.exp2(shift - z * z).astype(bf16)
    bias = dot(weight_t[...], phi_ref[...])
    for u in range(PAIR_ROWS):
        part = bias[:, u * BIN : u * BIN + BIN] * log2e + mask_scr[u : u + 1, :]
        for g in range(GROUPS):
            bias_ref[g, u * GHEADS : u * GHEADS + GHEADS, :] = part[g * GHEADS : g * GHEADS + GHEADS, :]


def pair_kernel(places_i, segs_i, places_j, segs_j, coef, weight_t, dist_ref, phi_ref, bias_ref, mask_scr):
    pair_block(
        places_i[...], segs_i[...], places_j[...], segs_j[...], coef, weight_t, dist_ref, phi_ref.at[0], bias_ref, mask_scr
    )


def pair_call(places_i, segs_i, places_j, segs_j, coef, weight_t):
    rows = places_i.shape[0]
    steps = rows // PAIR_ROWS
    return pl.pallas_call(
        pair_kernel,
        grid=(steps,),
        in_specs=[
            pl.BlockSpec((PAIR_ROWS, 3), lambda i: (i, 0)),
            pl.BlockSpec((PAIR_ROWS, 1), lambda i: (i, 0)),
            pl.BlockSpec((3, BIN), lambda i: (0, 0)),
            pl.BlockSpec((1, BIN), lambda i: (0, 0)),
            pl.BlockSpec((3, KERN, 128), lambda i: (0, 0, 0)),
            pl.BlockSpec((HEADS, KERN), lambda i: (0, 0)),
        ],
        out_specs=[
            pl.BlockSpec((PAIR_ROWS, BIN), lambda i: (i, 0)),
            pl.BlockSpec((1, KERN, PAIR_ROWS * BIN), lambda i: (i, 0, 0)),
            pl.BlockSpec((GROUPS, PAIR_ROWS * GHEADS, BIN), lambda i: (0, i, 0)),
        ],
        out_shape=[
            jax.ShapeDtypeStruct((rows, BIN), f32),
            jax.ShapeDtypeStruct((steps, KERN, PAIR_ROWS * BIN), bf16),
            jax.ShapeDtypeStruct((GROUPS, rows * GHEADS, BIN), f32),
        ],
        scratch_shapes=[pltpu.VMEM((PAIR_ROWS, BIN), f32)],
        compiler_params=pltpu.CompilerParams(vmem_limit_bytes=VMEM_LIMIT),
        name="pair_forward",
    )(places_i, segs_i, places_j, segs_j, coef, weight_t)


def spread_tables():
    rows = ATT_ROWS * GHEADS
    spread = (lax.broadcasted_iota(jnp.int32, (rows, ATT_ROWS), 0) // GHEADS) == lax.broadcasted_iota(
        jnp.int32, (rows, ATT_ROWS), 1
    )
    gather = (lax.broadcasted_iota(jnp.int32, (ATT_ROWS, rows), 1) // GHEADS) == lax.broadcasted_iota(
        jnp.int32, (ATT_ROWS, rows), 0
    )
    head = (lax.broadcasted_iota(jnp.int32, (rows, GWIDTH), 0) % GHEADS) == (
        lax.broadcasted_iota(jnp.int32, (rows, GWIDTH), 1) // HDIM
    )
    head_t = (lax.broadcasted_iota(jnp.int32, (GWIDTH, rows), 1) % GHEADS) == (
        lax.broadcasted_iota(jnp.int32, (GWIDTH, rows), 0) // HDIM
    )
    return spread.astype(bf16), gather.astype(bf16), head.astype(bf16), head_t.astype(bf16)


def forward_kernel(q_ref, k_ref, v_ref, bias_ref, spread, gather, head, head_t, out_ref, prob_ref, s_scr):
    rows = ATT_ROWS * GHEADS
    query = (lanes_dot(spread[...], q_ref[...]).astype(bf16)) * head[...]
    s_scr[...] = dot(query, k_ref[...])
    chunk = 32

    def soft(t, carry):
        at = pl.ds(pl.multiple_of(t * chunk, chunk), chunk)
        score = s_scr[at, :] * (HDIM**-0.5 * log2e) + bias_ref[0, at, :]
        top = jnp.max(score, axis=-1, keepdims=True)
        weight = jnp.exp2(score - top)
        total = jnp.sum(weight, axis=-1, keepdims=True)
        prob_ref[0, at, :] = (weight * (1.0 / total)).astype(bf16)
        return carry

    lax.fori_loop(0, rows // chunk, soft, 0)
    mixed = lanes_dot(v_ref[...], prob_ref[0])
    mixed = mixed.astype(bf16) * head_t[...]
    out_ref[...] = lanes_dot(mixed, gather[...]).astype(bf16)


def forward_call(q_t, k_t, v_t, bias, tables):
    rows = q_t.shape[1]
    blocks = rows // ATT_ROWS
    wide = ATT_ROWS * GHEADS
    whole = lambda g, i: (0, 0)
    return pl.pallas_call(
        forward_kernel,
        grid=(GROUPS, blocks),
        in_specs=[
            pl.BlockSpec((GWIDTH, ATT_ROWS), lambda g, i: (g, i)),
            pl.BlockSpec((GWIDTH, BIN), lambda g, i: (g, 0)),
            pl.BlockSpec((GWIDTH, BIN), lambda g, i: (g, 0)),
            pl.BlockSpec((1, wide, BIN), lambda g, i: (g, i, 0)),
            pl.BlockSpec((wide, ATT_ROWS), whole),
            pl.BlockSpec((ATT_ROWS, wide), whole),
            pl.BlockSpec((wide, GWIDTH), whole),
            pl.BlockSpec((GWIDTH, wide), whole),
        ],
        out_specs=[
            pl.BlockSpec((GWIDTH, ATT_ROWS), lambda g, i: (g, i)),
            pl.BlockSpec((1, wide, BIN), lambda g, i: (g, i, 0)),
        ],
        out_shape=[
            jax.ShapeDtypeStruct((D, rows), bf16),
            jax.ShapeDtypeStruct((GROUPS, rows * GHEADS, BIN), bf16),
        ],
        scratch_shapes=[pltpu.VMEM((wide, BIN), f32)],
        compiler_params=pltpu.CompilerParams(vmem_limit_bytes=VMEM_LIMIT),
        name="attention_forward",
    )(q_t, k_t, v_t, bias, *tables)


def backward_kernel(
    q_ref, go_ref, k_ref, v_ref, prob_ref, spread, gather, head, head_t, gs_ref, gq_ref, gk_ref, gv_ref, s_scr
):
    rows = ATT_ROWS * GHEADS
    step = pl.program_id(1)
    last = pl.num_programs(1) - 1
    grad_out = (lanes_dot(spread[...], go_ref[...]).astype(bf16)) * head[...]
    s_scr[...] = dot(grad_out, v_ref[...])
    chunk = 32

    def soft(t, carry):
        at = pl.ds(pl.multiple_of(t * chunk, chunk), chunk)
        prob = prob_ref[0, at, :].astype(f32)
        grad_prob = s_scr[at, :]
        inner = jnp.sum(prob * grad_prob, axis=-1, keepdims=True)
        gs_ref[0, at, :] = (prob * (grad_prob - inner)).astype(bf16)
        return carry

    lax.fori_loop(0, rows // chunk, soft, 0)
    grad_query = lanes_dot(k_ref[...], gs_ref[0]) * (HDIM**-0.5)
    grad_query = grad_query.astype(bf16) * head_t[...]
    gq_ref[...] = lanes_dot(grad_query, gather[...]).astype(bf16)
    query_t = lanes_dot(q_ref[...], spread[...]).astype(bf16) * head_t[...]
    grad_out_t = lanes_dot(go_ref[...], spread[...]).astype(bf16) * head_t[...]
    grad_key = dot(query_t, gs_ref[0]) * (HDIM**-0.5)
    grad_value = dot(grad_out_t, prob_ref[0])

    @pl.when(step == 0)
    def _():
        gk_ref[...] = grad_key
        gv_ref[...] = grad_value

    @pl.when(step > 0)
    def _():
        gk_ref[...] += grad_key
        gv_ref[...] += grad_value


def backward_call(q_t, go_t, k_t, v_t, prob, tables):
    rows = q_t.shape[1]
    blocks = rows // ATT_ROWS
    wide = ATT_ROWS * GHEADS
    whole = lambda g, i: (0, 0)
    return pl.pallas_call(
        backward_kernel,
        grid=(GROUPS, blocks),
        in_specs=[
            pl.BlockSpec((GWIDTH, ATT_ROWS), lambda g, i: (g, i)),
            pl.BlockSpec((GWIDTH, ATT_ROWS), lambda g, i: (g, i)),
            pl.BlockSpec((GWIDTH, BIN), lambda g, i: (g, 0)),
            pl.BlockSpec((GWIDTH, BIN), lambda g, i: (g, 0)),
            pl.BlockSpec((1, wide, BIN), lambda g, i: (g, i, 0)),
            pl.BlockSpec((wide, ATT_ROWS), whole),
            pl.BlockSpec((ATT_ROWS, wide), whole),
            pl.BlockSpec((wide, GWIDTH), whole),
            pl.BlockSpec((GWIDTH, wide), whole),
        ],
        out_specs=[
            pl.BlockSpec((1, wide, BIN), lambda g, i: (g, i, 0)),
            pl.BlockSpec((GWIDTH, ATT_ROWS), lambda g, i: (g, i)),
            pl.BlockSpec((GWIDTH, BIN), lambda g, i: (g, 0)),
            pl.BlockSpec((GWIDTH, BIN), lambda g, i: (g, 0)),
        ],
        out_shape=[
            jax.ShapeDtypeStruct((GROUPS, rows * GHEADS, BIN), bf16),
            jax.ShapeDtypeStruct((D, rows), bf16),
            jax.ShapeDtypeStruct((D, BIN), f32),
            jax.ShapeDtypeStruct((D, BIN), f32),
        ],
        scratch_shapes=[pltpu.VMEM((wide, BIN), f32)],
        compiler_params=pltpu.CompilerParams(vmem_limit_bytes=VMEM_LIMIT),
        name="attention_backward",
    )(q_t, go_t, k_t, v_t, prob, *tables)


def pair_grad_kernel(gs_ref, dist_ref, phi_ref, sum_ref, terms):
    @pl.when(pl.program_id(0) == 0)
    def _():
        sum_ref[...] = jnp.zeros_like(sum_ref)

    for u in range(PAIR_ROWS):
        lanes = slice(u * BIN, u * BIN + BIN)
        dist = dist_ref[u : u + 1, :] - center
        for g in range(0, GROUPS, 2):
            low = gs_ref[g, u * GHEADS : u * GHEADS + GHEADS, :].astype(f32)
            high = gs_ref[g + 1, u * GHEADS : u * GHEADS + GHEADS, :].astype(f32)
            grad = jnp.concatenate([low, high], axis=0)
            once = grad * dist
            twice = once * dist
            once_top = once.astype(bf16)
            twice_top = twice.astype(bf16)
            pieces = (
                grad.astype(bf16),
                once_top,
                (once - once_top.astype(f32)).astype(bf16),
                twice_top,
                (twice - twice_top.astype(f32)).astype(bf16),
            )
            for at, piece in enumerate(pieces):
                terms[at * HEADS + g * GHEADS : at * HEADS + (g + 2) * GHEADS, lanes] = piece
    sum_ref[...] += lanes_dot(terms[...], phi_ref[0])


def pair_grad_call(gs, dist, phi):
    rows = dist.shape[0]
    steps = rows // PAIR_ROWS
    return pl.pallas_call(
        pair_grad_kernel,
        grid=(steps,),
        in_specs=[
            pl.BlockSpec((GROUPS, PAIR_ROWS * GHEADS, BIN), lambda i: (0, i, 0)),
            pl.BlockSpec((PAIR_ROWS, BIN), lambda i: (i, 0)),
            pl.BlockSpec((1, KERN, PAIR_ROWS * BIN), lambda i: (i, 0, 0)),
        ],
        out_specs=pl.BlockSpec((5 * HEADS, KERN), lambda i: (0, 0)),
        out_shape=jax.ShapeDtypeStruct((5 * HEADS, KERN), f32),
        scratch_shapes=[pltpu.VMEM((5 * HEADS, PAIR_ROWS * BIN), bf16)],
        compiler_params=pltpu.CompilerParams(vmem_limit_bytes=VMEM_LIMIT),
        name="pair_gradient",
    )(gs, dist, phi)


def layer_norm(values, norm_gain, norm_offset):
    middle = values - jnp.mean(values, axis=-1, keepdims=True)
    spread = jnp.mean(middle * middle, axis=-1, keepdims=True)
    return middle * lax.rsqrt(spread + norm_eps) * norm_gain + norm_offset


def time_features(time_values):
    half_count = TFREQ // 2
    frequency = jnp.exp(jnp.arange(half_count, dtype=f32) * (-math.log(10000.0) / half_count))
    angles = (1000.0 * time_values)[:, None] * frequency[None, :]
    return jnp.concatenate([jnp.sin(angles), jnp.cos(angles)], axis=1)


def from_partner(block, bit):
    count = lax.axis_size("dev")
    return lax.ppermute(block, "dev", [(at, at ^ bit) for at in range(count)])


def of_block(own):
    across = from_partner(own, 2)
    beside = from_partner(own, 1)
    diagonal = from_partner(across, 1)
    return own, beside, across, diagonal


def outer_sum(left_rows, right_rows):
    return lax.dot_general(left_rows, right_rows, (((0,), (0,)), ((), ())), preferred_element_type=f32)


def times_transposed(left_rows, weight_matrix):
    return lax.dot_general(left_rows, weight_matrix, (((1,), (1,)), ((), ())), preferred_element_type=f32)


def shards(
    atoms,
    positions,
    segment,
    item_time,
    time_weight,
    norm1_gain,
    norm1_bias,
    qkv_weight,
    out_weight,
    norm2_gain,
    norm2_bias,
    ffn_in,
    ffn_in_bias,
    ffn_out,
    ffn_out_bias,
    pair_weight,
    kernel_mean,
    kernel_width,
    cotangent,
):
    axes = ("grp", "dev")
    gather = lambda array, axis: lax.all_gather(array, axes, axis=axis, tiled=True)
    w_time = gather(time_weight, 1)
    gain_one, shift_one = gather(norm1_gain, 0).astype(f32), gather(norm1_bias, 0).astype(f32)
    w_qkv = gather(qkv_weight, 0)
    w_out = gather(out_weight, 0)
    gain_two, shift_two = gather(norm2_gain, 0).astype(f32), gather(norm2_bias, 0).astype(f32)
    w_in = gather(ffn_in, 0)
    bias_in = gather(ffn_in_bias, 0).astype(f32)
    w_back = gather(ffn_out, 0)
    bias_back = gather(ffn_out_bias, 0).astype(f32)

    places = jnp.concatenate([positions, segment.astype(f32)[None]], axis=0)
    places_all = jnp.concatenate(of_block(places), axis=1)
    places_i = places.T
    column = lambda values: jnp.broadcast_to(values[:, None], (KERN, 128))
    coef = jnp.stack(
        [
            column(kernel_mean),
            column(math.sqrt(0.5 * log2e) / kernel_width),
            column(-jnp.log2(math.sqrt(2.0 * math.pi) * kernel_width)),
        ]
    )
    dist, phi, bias = pair_call(places_i[:, :3], places_i[:, 3:], places_all[:3], places_all[3:], coef, pair_weight.T)
    tables = spread_tables()

    features = time_features(item_time).astype(bf16)
    stream_zero = atoms.astype(f32) + dot(features, w_time)
    normed = layer_norm(stream_zero, gain_one, shift_one).astype(bf16)
    packed_t = lax.dot_general(w_qkv, normed, (((0,), (1,)), ((), ())), preferred_element_type=f32).astype(bf16)
    q_t = packed_t[:D]
    kv_t = jnp.concatenate(of_block(packed_t[D:]), axis=1)
    k_t, v_t = kv_t[:D], kv_t[D:]
    mixed_t, prob = forward_call(q_t, k_t, v_t, bias, tables)

    stream_one = stream_zero + lax.dot_general(mixed_t, w_out, (((0,), (0,)), ((), ())), preferred_element_type=f32)
    second = layer_norm(stream_one, gain_two, shift_two).astype(bf16)
    hidden_pre = dot(second, w_in) + bias_in
    hidden_act = jax.nn.gelu(hidden_pre, approximate=False).astype(bf16)
    output = (stream_one + dot(hidden_act, w_back) + bias_back).astype(bf16)

    grad_output = cotangent.astype(f32)
    grad_branch = cotangent
    grad_back = outer_sum(hidden_act, grad_branch)
    grad_bias_back = jnp.sum(grad_output, axis=0)
    grad_act = times_transposed(grad_branch, w_back)
    _, gelu_pull = jax.vjp(lambda pre: jax.nn.gelu(pre, approximate=False), hidden_pre)
    grad_pre = gelu_pull(grad_act)[0].astype(bf16)
    grad_in = outer_sum(second, grad_pre)
    grad_bias_in = jnp.sum(grad_pre.astype(f32), axis=0)
    grad_second = times_transposed(grad_pre, w_in)
    _, norm_two_pull = jax.vjp(layer_norm, stream_one, gain_two, shift_two)
    grad_stream_part, grad_gain_two, grad_shift_two = norm_two_pull(grad_second)
    grad_stream_one = grad_output + grad_stream_part
    grad_attn = grad_stream_one.astype(bf16)
    grad_out_weight = dot(mixed_t, grad_attn)
    grad_mixed_t = times_transposed(w_out, grad_attn).astype(bf16)

    gs, grad_query_t, grad_key_t, grad_value_t = backward_call(q_t, grad_mixed_t, k_t, v_t, prob, tables)
    sums = pair_grad_call(gs, dist, phi)

    rows = atoms.shape[0]
    grad_kv = jnp.concatenate([grad_key_t, grad_value_t], axis=0)
    part = [grad_kv[:, at * rows : at * rows + rows] for at in range(BIN // rows)]
    own = part[0] + from_partner(part[1].astype(bf16), 1).astype(f32)
    far = part[2] + from_partner(part[3].astype(bf16), 1).astype(f32)
    own = own + from_partner(far.astype(bf16), 2).astype(f32)
    grad_packed_t = jnp.concatenate([grad_query_t, own.astype(bf16)], axis=0)
    grad_qkv = lax.dot_general(normed, grad_packed_t, (((0,), (1,)), ((), ())), preferred_element_type=f32)
    grad_normed = lax.dot_general(grad_packed_t, w_qkv, (((0,), (1,)), ((), ())), preferred_element_type=f32)
    _, norm_one_pull = jax.vjp(layer_norm, stream_zero, gain_one, shift_one)
    grad_zero_part, grad_gain_one, grad_shift_one = norm_one_pull(grad_normed)
    grad_input = grad_stream_one + grad_zero_part
    grad_time = outer_sum(features, grad_input.astype(bf16))

    scatter = lambda array, axis: lax.psum_scatter(array, axes, scatter_dimension=axis, tiled=True)
    sums = lax.psum(sums, axes)
    weight_t = pair_weight.astype(f32).T
    low = sums[:HEADS]
    once = sums[HEADS : 2 * HEADS] + sums[2 * HEADS : 3 * HEADS]
    twice = sums[3 * HEADS : 4 * HEADS] + sums[4 * HEADS :]
    zeroth, first, square = (jnp.sum(weight_t * part_sum, axis=0) for part_sum in (low, once, twice))
    mean = kernel_mean - center
    grad_mean = (first - mean * zeroth) / (kernel_width * kernel_width)
    grad_width = (square - 2.0 * mean * first + mean * mean * zeroth) / (
        kernel_width * kernel_width * kernel_width
    ) - zeroth / kernel_width
    return (
        output,
        grad_input,
        scatter(grad_time, 1),
        scatter(grad_gain_one, 0),
        scatter(grad_shift_one, 0),
        scatter(grad_qkv, 0),
        scatter(grad_out_weight, 0),
        scatter(grad_gain_two, 0),
        scatter(grad_shift_two, 0),
        scatter(grad_in, 0),
        scatter(grad_bias_in, 0),
        scatter(grad_back, 0),
        scatter(grad_bias_back, 0),
        low.T,
        grad_mean,
        grad_width,
    )


def solution(mesh):
    in_specs = (
        P(("grp", "dev"), None),
        P(None, ("grp", "dev")),
        P(("grp", "dev")),
        P(("grp", "dev")),
        P(None, ("grp", "dev")),
        P(("grp", "dev")),
        P(("grp", "dev")),
        P(("grp", "dev"), None),
        P(("grp", "dev"), None),
        P(("grp", "dev")),
        P(("grp", "dev")),
        P(("grp", "dev"), None),
        P(("grp", "dev")),
        P(("grp", "dev"), None),
        P(("grp", "dev")),
        P(),
        P(),
        P(),
        P(("grp", "dev"), None),
    )
    out_specs = (
        P(("grp", "dev"), None),
        P(("grp", "dev"), None),
        P(None, ("grp", "dev")),
        P(("grp", "dev")),
        P(("grp", "dev")),
        P(("grp", "dev"), None),
        P(("grp", "dev"), None),
        P(("grp", "dev")),
        P(("grp", "dev")),
        P(("grp", "dev"), None),
        P(("grp", "dev")),
        P(("grp", "dev"), None),
        P(("grp", "dev")),
        P(),
        P(),
        P(),
    )
    return jax.shard_map(shards, mesh=mesh, in_specs=in_specs, out_specs=out_specs, check_vma=False)
```

```python
from functools import partial
import math

import jax
import jax.numpy as jnp
from jax import lax
from jax.experimental import pallas as pl
from jax.experimental.pallas import tpu as pltpu
from jax.sharding import PartitionSpec as P

D = 768
HEADS = 32
HDIM = 24
KERN = 128
TFREQ = 128
BIN = 1024
GROUPS = 4
GHEADS = HEADS // GROUPS
GWIDTH = GHEADS * HDIM
PAIR_ROWS = 8
ATT_ROWS = 128

norm_eps = 1e-05
mask_fill = -1e30
log2e = math.log2(math.e)
center = 6.0
f32 = jnp.float32
bf16 = jnp.bfloat16
VMEM_LIMIT = 56 * 1024 * 1024


def lanes_dot(left, right):
    return lax.dot_general(left, right, (((1,), (1,)), ((), ())), preferred_element_type=f32)


def dot(left, right):
    return jnp.dot(left, right, preferred_element_type=f32)


def pair_block(places_i, segs_i, places_j, segs_j, coef, weight_t, dist_ref, phi_ref, bias_ref, mask_scr):
    square = None
    for axis in range(3):
        gap = places_i[:, axis : axis + 1] - places_j[axis : axis + 1, :]
        square = gap * gap if square is None else square + gap * gap
    dist_ref[...] = jnp.sqrt(square)
    mask_scr[...] = jnp.where(segs_i == segs_j, 0.0, mask_fill).astype(f32)
    for u in range(PAIR_ROWS):
        for kg in range(KERN // 16):
            rows = slice(kg * 16, kg * 16 + 16)
            mean, inv, shift = coef[0, rows, :], coef[1, rows, :], coef[2, rows, :]
            for jv in range(BIN // 128):
                dist = dist_ref[u : u + 1, jv * 128 : jv * 128 + 128]
                z = (dist - mean) * inv
                lanes = slice(u * BIN + jv * 128, u * BIN + jv * 128 + 128)
                phi_ref[rows, lanes] = jnp.exp2(shift - z * z).astype(bf16)
    bias = dot(weight_t[...], phi_ref[...])
    for u in range(PAIR_ROWS):
        part = bias[:, u * BIN : u * BIN + BIN] * log2e + mask_scr[u : u + 1, :]
        for g in range(GROUPS):
            bias_ref[g, u * GHEADS : u * GHEADS + GHEADS, :] = part[g * GHEADS : g * GHEADS + GHEADS, :]


def pair_kernel(places_i, segs_i, places_j, segs_j, coef, weight_t, dist_ref, phi_ref, bias_ref, mask_scr):
    pair_block(
        places_i[...], segs_i[...], places_j[...], segs_j[...], coef, weight_t, dist_ref, phi_ref.at[0], bias_ref, mask_scr
    )


def pair_call(places_i, segs_i, places_j, segs_j, coef, weight_t):
    rows = places_i.shape[0]
    steps = rows // PAIR_ROWS
    return pl.pallas_call(
        pair_kernel,
        grid=(steps,),
        in_specs=[
            pl.BlockSpec((PAIR_ROWS, 3), lambda i: (i, 0)),
            pl.BlockSpec((PAIR_ROWS, 1), lambda i: (i, 0)),
            pl.BlockSpec((3, BIN), lambda i: (0, 0)),
            pl.BlockSpec((1, BIN), lambda i: (0, 0)),
            pl.BlockSpec((3, KERN, 128), lambda i: (0, 0, 0)),
            pl.BlockSpec((HEADS, KERN), lambda i: (0, 0)),
        ],
        out_specs=[
            pl.BlockSpec((PAIR_ROWS, BIN), lambda i: (i, 0)),
            pl.BlockSpec((1, KERN, PAIR_ROWS * BIN), lambda i: (i, 0, 0)),
            pl.BlockSpec((GROUPS, PAIR_ROWS * GHEADS, BIN), lambda i: (0, i, 0)),
        ],
        out_shape=[
            jax.ShapeDtypeStruct((rows, BIN), f32),
            jax.ShapeDtypeStruct((steps, KERN, PAIR_ROWS * BIN), bf16),
            jax.ShapeDtypeStruct((GROUPS, rows * GHEADS, BIN), f32),
        ],
        scratch_shapes=[pltpu.VMEM((PAIR_ROWS, BIN), f32)],
        compiler_params=pltpu.CompilerParams(vmem_limit_bytes=VMEM_LIMIT),
        name="pair_forward",
    )(places_i, segs_i, places_j, segs_j, coef, weight_t)


def spread_tables():
    rows = ATT_ROWS * GHEADS
    spread = (lax.broadcasted_iota(jnp.int32, (rows, ATT_ROWS), 0) // GHEADS) == lax.broadcasted_iota(
        jnp.int32, (rows, ATT_ROWS), 1
    )
    gather = (lax.broadcasted_iota(jnp.int32, (ATT_ROWS, rows), 1) // GHEADS) == lax.broadcasted_iota(
        jnp.int32, (ATT_ROWS, rows), 0
    )
    head = (lax.broadcasted_iota(jnp.int32, (rows, GWIDTH), 0) % GHEADS) == (
        lax.broadcasted_iota(jnp.int32, (rows, GWIDTH), 1) // HDIM
    )
    head_t = (lax.broadcasted_iota(jnp.int32, (GWIDTH, rows), 1) % GHEADS) == (
        lax.broadcasted_iota(jnp.int32, (GWIDTH, rows), 0) // HDIM
    )
    return spread.astype(bf16), gather.astype(bf16), head.astype(bf16), head_t.astype(bf16)


def forward_kernel(q_ref, k_ref, v_ref, bias_ref, spread, gather, head, head_t, out_ref, prob_ref, s_scr):
    rows = ATT_ROWS * GHEADS
    query = (lanes_dot(spread[...], q_ref[...]).astype(bf16)) * head[...]
    s_scr[...] = dot(query, k_ref[...])
    chunk = 32

    def soft(t, carry):
        at = pl.ds(pl.multiple_of(t * chunk, chunk), chunk)
        score = s_scr[at, :] * (HDIM**-0.5 * log2e) + bias_ref[0, at, :]
        top = jnp.max(score, axis=-1, keepdims=True)
        weight = jnp.exp2(score - top)
        total = jnp.sum(weight, axis=-1, keepdims=True)
        prob_ref[0, at, :] = (weight * (1.0 / total)).astype(bf16)
        return carry

    lax.fori_loop(0, rows // chunk, soft, 0)
    mixed = lanes_dot(v_ref[...], prob_ref[0])
    mixed = mixed.astype(bf16) * head_t[...]
    out_ref[...] = lanes_dot(mixed, gather[...]).astype(bf16)


def forward_call(q_t, k_t, v_t, bias, tables):
    rows = q_t.shape[1]
    blocks = rows // ATT_ROWS
    wide = ATT_ROWS * GHEADS
    whole = lambda g, i: (0, 0)
    return pl.pallas_call(
        forward_kernel,
        grid=(GROUPS, blocks),
        in_specs=[
            pl.BlockSpec((GWIDTH, ATT_ROWS), lambda g, i: (g, i)),
            pl.BlockSpec((GWIDTH, BIN), lambda g, i: (g, 0)),
            pl.BlockSpec((GWIDTH, BIN), lambda g, i: (g, 0)),
            pl.BlockSpec((1, wide, BIN), lambda g, i: (g, i, 0)),
            pl.BlockSpec((wide, ATT_ROWS), whole),
            pl.BlockSpec((ATT_ROWS, wide), whole),
            pl.BlockSpec((wide, GWIDTH), whole),
            pl.BlockSpec((GWIDTH, wide), whole),
        ],
        out_specs=[
            pl.BlockSpec((GWIDTH, ATT_ROWS), lambda g, i: (g, i)),
            pl.BlockSpec((1, wide, BIN), lambda g, i: (g, i, 0)),
        ],
        out_shape=[
            jax.ShapeDtypeStruct((D, rows), bf16),
            jax.ShapeDtypeStruct((GROUPS, rows * GHEADS, BIN), bf16),
        ],
        scratch_shapes=[pltpu.VMEM((wide, BIN), f32)],
        compiler_params=pltpu.CompilerParams(vmem_limit_bytes=VMEM_LIMIT),
        name="attention_forward",
    )(q_t, k_t, v_t, bias, *tables)


def backward_kernel(
    q_ref, go_ref, k_ref, v_ref, prob_ref, spread, gather, head, head_t, gs_ref, gq_ref, gk_ref, gv_ref, s_scr
):
    rows = ATT_ROWS * GHEADS
    step = pl.program_id(1)
    last = pl.num_programs(1) - 1
    grad_out = (lanes_dot(spread[...], go_ref[...]).astype(bf16)) * head[...]
    s_scr[...] = dot(grad_out, v_ref[...])
    chunk = 32

    def soft(t, carry):
        at = pl.ds(pl.multiple_of(t * chunk, chunk), chunk)
        prob = prob_ref[0, at, :].astype(f32)
        grad_prob = s_scr[at, :]
        inner = jnp.sum(prob * grad_prob, axis=-1, keepdims=True)
        gs_ref[0, at, :] = (prob * (grad_prob - inner)).astype(bf16)
        return carry

    lax.fori_loop(0, rows // chunk, soft, 0)
    grad_query = lanes_dot(k_ref[...], gs_ref[0]) * (HDIM**-0.5)
    grad_query = grad_query.astype(bf16) * head_t[...]
    gq_ref[...] = lanes_dot(grad_query, gather[...]).astype(bf16)
    query_t = lanes_dot(q_ref[...], spread[...]).astype(bf16) * head_t[...]
    grad_out_t = lanes_dot(go_ref[...], spread[...]).astype(bf16) * head_t[...]
    grad_key = dot(query_t, gs_ref[0]) * (HDIM**-0.5)
    grad_value = dot(grad_out_t, prob_ref[0])

    @pl.when(step == 0)
    def _():
        gk_ref[...] = grad_key
        gv_ref[...] = grad_value

    @pl.when(step > 0)
    def _():
        gk_ref[...] += grad_key
        gv_ref[...] += grad_value


def backward_call(q_t, go_t, k_t, v_t, prob, tables):
    rows = q_t.shape[1]
    blocks = rows // ATT_ROWS
    wide = ATT_ROWS * GHEADS
    whole = lambda g, i: (0, 0)
    return pl.pallas_call(
        backward_kernel,
        grid=(GROUPS, blocks),
        in_specs=[
            pl.BlockSpec((GWIDTH, ATT_ROWS), lambda g, i: (g, i)),
            pl.BlockSpec((GWIDTH, ATT_ROWS), lambda g, i: (g, i)),
            pl.BlockSpec((GWIDTH, BIN), lambda g, i: (g, 0)),
            pl.BlockSpec((GWIDTH, BIN), lambda g, i: (g, 0)),
            pl.BlockSpec((1, wide, BIN), lambda g, i: (g, i, 0)),
            pl.BlockSpec((wide, ATT_ROWS), whole),
            pl.BlockSpec((ATT_ROWS, wide), whole),
            pl.BlockSpec((wide, GWIDTH), whole),
            pl.BlockSpec((GWIDTH, wide), whole),
        ],
        out_specs=[
            pl.BlockSpec((1, wide, BIN), lambda g, i: (g, i, 0)),
            pl.BlockSpec((GWIDTH, ATT_ROWS), lambda g, i: (g, i)),
            pl.BlockSpec((GWIDTH, BIN), lambda g, i: (g, 0)),
            pl.BlockSpec((GWIDTH, BIN), lambda g, i: (g, 0)),
        ],
        out_shape=[
            jax.ShapeDtypeStruct((GROUPS, rows * GHEADS, BIN), bf16),
            jax.ShapeDtypeStruct((D, rows), bf16),
            jax.ShapeDtypeStruct((D, BIN), f32),
            jax.ShapeDtypeStruct((D, BIN), f32),
        ],
        scratch_shapes=[pltpu.VMEM((wide, BIN), f32)],
        compiler_params=pltpu.CompilerParams(vmem_limit_bytes=VMEM_LIMIT),
        name="attention_backward",
    )(q_t, go_t, k_t, v_t, prob, *tables)


def pair_grad_kernel(gs_ref, dist_ref, phi_ref, sum_ref, terms):
    @pl.when(pl.program_id(0) == 0)
    def _():
        sum_ref[...] = jnp.zeros_like(sum_ref)

    for u in range(PAIR_ROWS):
        lanes = slice(u * BIN, u * BIN + BIN)
        dist = dist_ref[u : u + 1, :] - center
        for g in range(0, GROUPS, 2):
            low = gs_ref[g, u * GHEADS : u * GHEADS + GHEADS, :].astype(f32)
            high = gs_ref[g + 1, u * GHEADS : u * GHEADS + GHEADS, :].astype(f32)
            grad = jnp.concatenate([low, high], axis=0)
            once = grad * dist
            twice = once * dist
            once_top = once.astype(bf16)
            twice_top = twice.astype(bf16)
            pieces = (
                grad.astype(bf16),
                once_top,
                (once - once_top.astype(f32)).astype(bf16),
                twice_top,
                (twice - twice_top.astype(f32)).astype(bf16),
            )
            for at, piece in enumerate(pieces):
                terms[at * HEADS + g * GHEADS : at * HEADS + (g + 2) * GHEADS, lanes] = piece
    sum_ref[...] += lanes_dot(terms[...], phi_ref[0])


def pair_grad_call(gs, dist, phi):
    rows = dist.shape[0]
    steps = rows // PAIR_ROWS
    return pl.pallas_call(
        pair_grad_kernel,
        grid=(steps,),
        in_specs=[
            pl.BlockSpec((GROUPS, PAIR_ROWS * GHEADS, BIN), lambda i: (0, i, 0)),
            pl.BlockSpec((PAIR_ROWS, BIN), lambda i: (i, 0)),
            pl.BlockSpec((1, KERN, PAIR_ROWS * BIN), lambda i: (i, 0, 0)),
        ],
        out_specs=pl.BlockSpec((5 * HEADS, KERN), lambda i: (0, 0)),
        out_shape=jax.ShapeDtypeStruct((5 * HEADS, KERN), f32),
        scratch_shapes=[pltpu.VMEM((5 * HEADS, PAIR_ROWS * BIN), bf16)],
        compiler_params=pltpu.CompilerParams(vmem_limit_bytes=VMEM_LIMIT),
        name="pair_gradient",
    )(gs, dist, phi)


def grid_of_mesh(mesh):
    count = mesh.shape["dev"] // 2
    wide = 1
    while wide * wide < count:
        wide *= 2
    return mesh.shape["grp"], count // wide, wide, 2


def my_place(sizes):
    _, _, wide, cores = sizes
    dev = lax.axis_index("dev")
    return (lax.axis_index("grp"), dev // (wide * cores), lax.rem(dev // cores, wide), lax.rem(dev, cores))


def device_at(place, sizes):
    _, _, wide, cores = sizes
    return (place[0], (place[1] * wide + place[2]) * cores + place[3])


def other_place(place, axis, shift, sizes):
    moved = list(place)
    moved[axis] = lax.rem(place[axis] + shift, sizes[axis])
    return tuple(moved)


def partner_list(place, sizes):
    return [other_place(place, axis, shift, sizes) for axis in range(4) for shift in range(1, sizes[axis])]


def meet(place, sizes):
    barrier = pltpu.get_barrier_semaphore()
    partners = partner_list(place, sizes)
    for partner in partners:
        pl.semaphore_signal(
            barrier, inc=1, device_id=device_at(partner, sizes), device_id_type=pl.DeviceIdType.MESH
        )
    pl.semaphore_wait(barrier, len(partners))


class GatherPart:
    def __init__(self, source, full, lanes, order, at, send_sem, recv_sem, place, sizes):
        self.source, self.full, self.lanes = source, full, lanes
        self.order = order
        self.at = at
        self.send_sem, self.recv_sem = send_sem, recv_sem
        self.place, self.sizes = place, sizes
        self.base = [0]
        for axis in order:
            self.base.append(self.base[-1] + sizes[axis] - 1)

    def view(self, stage):
        done = self.order[:stage]
        where = tuple(slice(None) if axis in done else self.place[axis] for axis in range(4))
        return self.full.at[where + (slice(None), self.lanes)]

    def copies(self, stage):
        axis = self.order[stage]
        found = []
        for shift in range(1, self.sizes[axis]):
            sem = self.base[stage] + shift - 1
            found.append(
                pltpu.make_async_remote_copy(
                    src_ref=self.source.at[:, self.lanes] if stage == 0 else self.view(stage),
                    dst_ref=self.view(stage),
                    send_sem=self.send_sem.at[self.at, sem],
                    recv_sem=self.recv_sem.at[self.at, sem],
                    device_id=device_at(other_place(self.place, axis, shift, self.sizes), self.sizes),
                    device_id_type=pl.DeviceIdType.MESH,
                )
            )
        return found

    def start(self, stage):
        for copy in self.copies(stage):
            copy.start()

    def arrive(self, stage):
        for copy in self.copies(stage):
            copy.wait_recv()

    def finish(self):
        for stage in range(len(self.order)):
            for copy in self.copies(stage):
                copy.wait_send()


def gather_plan(shapes):
    plan = []
    for at, (rows, lanes) in enumerate(shapes):
        half = lanes // 256 * 128
        group = [(at, half, lanes - half, (0, 1, 2, 3))]
        if half:
            group.insert(0, (at, 0, half, (0, 2, 1, 3)))
        plan.append(group)
    return plan


def run_stages(groups, stages=4):
    for part in groups[0]:
        part.start(0)
    for turn in range(len(groups) + stages - 1):
        if turn + 1 < len(groups):
            for part in groups[turn + 1]:
                part.start(0)
        for stage in range(stages - 1, -1, -1):
            index = turn - stage
            if 0 <= index < len(groups):
                for part in groups[index]:
                    part.arrive(stage)
                    if stage + 1 < stages:
                        part.start(stage + 1)
    for group in groups:
        for part in group:
            part.finish()


def gather_kernel(sizes, plan, count, *refs):
    sources, fulls = refs[:count], refs[count : 2 * count]
    send_sem, recv_sem, own_sem = refs[2 * count :]
    place = my_place(sizes)
    own = []
    for at in range(count):
        own.append(pltpu.make_async_copy(sources[at], fulls[at].at[place], own_sem.at[at]))
        own[at].start()
    meet(place, sizes)
    groups, index = [], 0
    for group in plan:
        groups.append([])
        for at, first, lanes, order in group:
            groups[-1].append(
                GatherPart(sources[at], fulls[at], pl.ds(first, lanes), order, index, send_sem, recv_sem, place, sizes)
            )
            index += 1
    for copy in own:
        copy.wait()
    run_stages(groups)


def gather_call(sizes, arrays, collective):
    count = len(arrays)
    plan = gather_plan([array.shape for array in arrays])
    slots = sum(size - 1 for size in sizes)
    fulls = pl.pallas_call(
        lambda *refs: gather_kernel(sizes, plan, count, *refs),
        in_specs=[pl.BlockSpec(memory_space=pl.ANY)] * count,
        out_specs=[pl.BlockSpec(memory_space=pl.ANY)] * count,
        out_shape=[jax.ShapeDtypeStruct(sizes + array.shape, array.dtype) for array in arrays],
        scratch_shapes=[
            pltpu.SemaphoreType.DMA((sum(map(len, plan)), slots)),
            pltpu.SemaphoreType.DMA((sum(map(len, plan)), slots)),
            pltpu.SemaphoreType.DMA((count,)),
        ],
        compiler_params=pltpu.CompilerParams(
            collective_id=collective, has_side_effects=True, vmem_limit_bytes=VMEM_LIMIT
        ),
        name="gather_weights",
    )(*arrays)
    return [full.reshape((-1,) + full.shape[4:]) for full in fulls]


class ScatterPart:
    def __init__(self, source, result, lanes, order, buffers, at, send_sem, recv_sem, own_sem, place, sizes):
        self.source, self.result, self.lanes = source, result, lanes
        self.order, self.place, self.sizes = order, place, sizes
        self.first, self.slots = buffers[0], buffers[1:]
        self.at, self.send_sem, self.recv_sem, self.own_sem = at, send_sem, recv_sem, own_sem
        self.base = [0]
        for axis in order:
            self.base.append(self.base[-1] + sizes[axis] - 1)

    def pick(self, stage, index):
        if stage == 0:
            where = tuple(index if axis == self.order[0] else slice(None) for axis in range(4))
            return self.source.at[where + (slice(None), self.lanes)]
        holder = self.first if stage == 1 else self.slots[stage - 1].at[0]
        left = [axis for axis in range(4) if axis not in self.order[:stage]]
        where = tuple(index if axis == self.order[stage] else slice(None) for axis in left)
        return holder.at[where]

    def own_copy(self):
        return pltpu.make_async_copy(self.pick(0, self.place[self.order[0]]), self.first, self.own_sem.at[self.at])

    def copies(self, stage):
        axis = self.order[stage]
        found = []
        for shift in range(1, self.sizes[axis]):
            target = other_place(self.place, axis, shift, self.sizes)
            sem = self.base[stage] + shift - 1
            found.append(
                pltpu.make_async_remote_copy(
                    src_ref=self.pick(stage, target[axis]),
                    dst_ref=self.slots[stage].at[shift - 1],
                    send_sem=self.send_sem.at[self.at, sem],
                    recv_sem=self.recv_sem.at[self.at, sem],
                    device_id=device_at(target, self.sizes),
                    device_id_type=pl.DeviceIdType.MESH,
                )
            )
        return found

    def start(self, stage):
        if stage == 0:
            self.own_copy().start()
        for copy in self.copies(stage):
            copy.start()

    def arrive(self, stage):
        if stage == 0:
            self.own_copy().wait()
        for copy in self.copies(stage):
            copy.wait_recv()
        slots = self.slots[stage]
        count = self.sizes[self.order[stage]] - 1
        mine = self.first if stage == 0 else self.pick(stage, self.place[self.order[stage]])
        lead = slots.shape[1:-2]
        if not lead:
            total = mine[...].astype(f32)
            for slot in range(count):
                total = total + slots[slot].astype(f32)
            self.result[:, self.lanes] = total
            return
        blocks = math.prod(lead)

        def add(step, carry):
            where = []
            for size in reversed(lead):
                where.insert(0, lax.rem(step, size))
                step = step // size
            where = tuple(where)
            total = mine[where].astype(f32)
            for slot in range(count):
                total = total + slots[(slot,) + where].astype(f32)
            if stage == 0:
                self.first[where] = total.astype(bf16)
            else:
                slots[(0,) + where] = total.astype(bf16)
            return carry

        lax.fori_loop(0, blocks, add, 0)

    def finish(self):
        for stage in range(len(self.order)):
            for copy in self.copies(stage):
                copy.wait_send()


class TotalPart:
    def __init__(self, source, result, slots, send_sem, recv_sem, place, sizes):
        self.source, self.result, self.slots = source, result, slots
        self.order, self.place, self.sizes = (3, 2, 1, 0), place, sizes
        self.send_sem, self.recv_sem = send_sem, recv_sem
        self.base = [0]
        for axis in self.order:
            self.base.append(self.base[-1] + sizes[axis] - 1)

    def copies(self, stage):
        axis = self.order[stage]
        mine = self.slots[stage].at[self.place[axis]]
        found = []
        for shift in range(1, self.sizes[axis]):
            sem = self.base[stage] + shift - 1
            found.append(
                pltpu.make_async_remote_copy(
                    src_ref=mine,
                    dst_ref=mine,
                    send_sem=self.send_sem.at[sem],
                    recv_sem=self.recv_sem.at[sem],
                    device_id=device_at(other_place(self.place, axis, shift, self.sizes), self.sizes),
                    device_id_type=pl.DeviceIdType.MESH,
                )
            )
        return found

    def start(self, stage):
        if stage == 0:
            self.slots[0][self.place[3]] = self.source[...]
        for copy in self.copies(stage):
            copy.start()

    def arrive(self, stage):
        for copy in self.copies(stage):
            copy.wait_recv()
        axis = self.order[stage]
        total = self.slots[stage][0]
        for at in range(1, self.sizes[axis]):
            total = total + self.slots[stage][at]
        if stage == 3:
            self.result[...] = total
        else:
            self.slots[stage + 1][self.place[self.order[stage + 1]]] = total

    def finish(self):
        for stage in range(4):
            for copy in self.copies(stage):
                copy.wait_send()


def scatter_plan(shapes):
    plan = []
    for at, (rows, lanes) in enumerate(shapes):
        half = lanes // 256 * 128
        plan.append([(at, 0, half, (3, 2, 1, 0)), (at, half, lanes - half, (3, 1, 2, 0))])
    return plan


def scatter_buffers(sizes, plan, shapes):
    buffers = []
    for at, first, lanes, order in sum(plan, []):
        block = (shapes[at][0], lanes)
        left = [0, 1, 2, 3]
        for stage, axis in enumerate(order):
            left.remove(axis)
            lead = tuple(sizes[other] for other in left)
            if stage == 0:
                buffers.append(pltpu.VMEM(lead + block, bf16))
            buffers.append(pltpu.VMEM((sizes[axis] - 1,) + lead + block, bf16))
    return buffers


def scatter_kernel(sizes, plan, count, total_at, *refs):
    extra = 0 if total_at is None else 1
    sources, refs = refs[: count + extra], refs[count + extra :]
    results, refs = refs[: count + extra], refs[count + extra :]
    send_sem, recv_sem, own_sem = refs[:3]
    buffers = refs[3:]
    place = my_place(sizes)
    meet(place, sizes)
    groups, index = [], 0
    for group in plan:
        groups.append([])
        for at, first, lanes, order in group:
            held = buffers[5 * index : 5 * index + 5]
            lanes = pl.ds(first, lanes)
            groups[-1].append(
                ScatterPart(
                    sources[at], results[at], lanes, order, held, index, send_sem, recv_sem, own_sem, place, sizes
                )
            )
            index += 1
    if extra:
        slots = buffers[5 * index : 5 * index + 4]
        groups[total_at].insert(
            0, TotalPart(sources[count], results[count], slots, buffers[-2], buffers[-1], place, sizes)
        )
    run_stages(groups)


def scatter_call(sizes, arrays, collective, total=None, total_at=None):
    devices = math.prod(sizes)
    count = len(arrays)
    shapes = [(array.shape[0] // devices, array.shape[1]) for array in arrays]
    plan = scatter_plan(shapes)
    slots = sum(size - 1 for size in sizes)
    vmem = pl.BlockSpec(memory_space=pltpu.VMEM)
    operands = [array.reshape(sizes + shape) for array, shape in zip(arrays, shapes)]
    in_specs, out_specs = [pl.BlockSpec(memory_space=pl.ANY)] * count, [vmem] * count
    out_shape = [jax.ShapeDtypeStruct(shape, f32) for shape in shapes]
    parts = sum(map(len, plan))
    scratch = [
        pltpu.SemaphoreType.DMA((parts, slots)),
        pltpu.SemaphoreType.DMA((parts, slots)),
        pltpu.SemaphoreType.DMA((parts,)),
    ] + scatter_buffers(sizes, plan, shapes)
    if total is not None:
        operands.append(total)
        in_specs, out_specs = in_specs + [vmem], out_specs + [vmem]
        out_shape.append(jax.ShapeDtypeStruct(total.shape, f32))
        scratch += [pltpu.VMEM((sizes[axis],) + total.shape, f32) for axis in (3, 2, 1, 0)]
        scratch += [pltpu.SemaphoreType.DMA((slots,))] * 2
    return pl.pallas_call(
        lambda *refs: scatter_kernel(sizes, plan, count, total_at, *refs),
        in_specs=in_specs,
        out_specs=out_specs,
        out_shape=out_shape,
        scratch_shapes=scratch,
        compiler_params=pltpu.CompilerParams(
            collective_id=collective, has_side_effects=True, vmem_limit_bytes=VMEM_LIMIT
        ),
        name="sum_gradients",
    )(*operands)


def layer_norm(values, norm_gain, norm_offset):
    middle = values - jnp.mean(values, axis=-1, keepdims=True)
    spread = jnp.mean(middle * middle, axis=-1, keepdims=True)
    return middle * lax.rsqrt(spread + norm_eps) * norm_gain + norm_offset


def time_features(time_values):
    half_count = TFREQ // 2
    frequency = jnp.exp(jnp.arange(half_count, dtype=f32) * (-math.log(10000.0) / half_count))
    angles = (1000.0 * time_values)[:, None] * frequency[None, :]
    return jnp.concatenate([jnp.sin(angles), jnp.cos(angles)], axis=1)


def from_partner(block, bit):
    count = lax.axis_size("dev")
    return lax.ppermute(block, "dev", [(at, at ^ bit) for at in range(count)])


def of_block(own):
    across = from_partner(own, 2)
    beside = from_partner(own, 1)
    diagonal = from_partner(across, 1)
    return own, beside, across, diagonal


def outer_sum(left_rows, right_rows):
    return lax.dot_general(left_rows, right_rows, (((0,), (0,)), ((), ())), preferred_element_type=f32)


def times_transposed(left_rows, weight_matrix):
    return lax.dot_general(left_rows, weight_matrix, (((1,), (1,)), ((), ())), preferred_element_type=f32)


def shards(
    sizes,
    atoms,
    positions,
    segment,
    item_time,
    time_weight,
    norm1_gain,
    norm1_bias,
    qkv_weight,
    out_weight,
    norm2_gain,
    norm2_bias,
    ffn_in,
    ffn_in_bias,
    ffn_out,
    ffn_out_bias,
    pair_weight,
    kernel_mean,
    kernel_width,
    cotangent,
):
    axes = ("grp", "dev")
    own_rows, own_hidden = norm1_gain.shape[0], ffn_in_bias.shape[0]
    vectors = jnp.stack(
        [jnp.pad(v, (0, 128 - v.shape[0])) for v in (norm1_gain, norm1_bias, norm2_gain, norm2_bias, ffn_out_bias, ffn_in_bias)]
        + [jnp.zeros((128,), bf16)] * 2
    )
    small = jnp.concatenate([time_weight.T, vectors], axis=0)
    small, w_qkv, w_out, w_in, w_back = gather_call(sizes, (small, qkv_weight, out_weight, ffn_in, ffn_out), 1)
    w_qkv, w_out, w_in, w_back = (full.reshape(-1, full.shape[2]) for full in (w_qkv, w_out, w_in, w_back))
    w_time_t = small[:, :own_rows].reshape(-1, TFREQ)
    vectors = small[:, own_rows:].astype(f32).transpose(1, 0, 2)
    gain_one, shift_one, gain_two, shift_two, bias_back = (vectors[at, :, :own_rows].reshape(-1) for at in range(5))
    bias_in = vectors[5, :, :own_hidden].reshape(-1)

    places = jnp.concatenate([positions, segment.astype(f32)[None]], axis=0)
    places_all = jnp.concatenate(of_block(places), axis=1)
    places_i = places.T
    column = lambda values: jnp.broadcast_to(values[:, None], (KERN, 128))
    coef = jnp.stack(
        [
            column(kernel_mean),
            column(math.sqrt(0.5 * log2e) / kernel_width),
            column(-jnp.log2(math.sqrt(2.0 * math.pi) * kernel_width)),
        ]
    )
    dist, phi, bias = pair_call(places_i[:, :3], places_i[:, 3:], places_all[:3], places_all[3:], coef, pair_weight.T)
    tables = spread_tables()

    features = time_features(item_time).astype(bf16)
    stream_zero = atoms.astype(f32) + times_transposed(features, w_time_t)
    normed = layer_norm(stream_zero, gain_one, shift_one).astype(bf16)
    packed_t = lax.dot_general(w_qkv, normed, (((0,), (1,)), ((), ())), preferred_element_type=f32).astype(bf16)
    q_t = packed_t[:D]
    kv_t = jnp.concatenate(of_block(packed_t[D:]), axis=1)
    k_t, v_t = kv_t[:D], kv_t[D:]
    mixed_t, prob = forward_call(q_t, k_t, v_t, bias, tables)

    stream_one = stream_zero + lax.dot_general(mixed_t, w_out, (((0,), (0,)), ((), ())), preferred_element_type=f32)
    second = layer_norm(stream_one, gain_two, shift_two).astype(bf16)
    hidden_pre = dot(second, w_in) + bias_in
    hidden_act = jax.nn.gelu(hidden_pre, approximate=False).astype(bf16)
    output = (stream_one + dot(hidden_act, w_back) + bias_back).astype(bf16)

    grad_output = cotangent.astype(f32)
    grad_branch = cotangent
    grad_back = outer_sum(hidden_act, grad_branch).astype(bf16)
    grad_bias_back = jnp.sum(grad_output, axis=0)
    grad_act = times_transposed(grad_branch, w_back)
    _, gelu_pull = jax.vjp(lambda pre: jax.nn.gelu(pre, approximate=False), hidden_pre)
    grad_pre = gelu_pull(grad_act)[0].astype(bf16)
    grad_in = outer_sum(second, grad_pre).astype(bf16)
    grad_bias_in = jnp.sum(grad_pre.astype(f32), axis=0)
    grad_second = times_transposed(grad_pre, w_in)
    _, norm_two_pull = jax.vjp(layer_norm, stream_one, gain_two, shift_two)
    grad_stream_part, grad_gain_two, grad_shift_two = norm_two_pull(grad_second)
    grad_stream_one = grad_output + grad_stream_part
    grad_attn = grad_stream_one.astype(bf16)
    grad_out_weight = dot(mixed_t, grad_attn).astype(bf16)
    grad_mixed_t = times_transposed(w_out, grad_attn).astype(bf16)

    gs, grad_query_t, grad_key_t, grad_value_t = backward_call(q_t, grad_mixed_t, k_t, v_t, prob, tables)
    sums = pair_grad_call(gs, dist, phi)

    rows = atoms.shape[0]
    grad_kv = jnp.concatenate([grad_key_t, grad_value_t], axis=0)
    part = [grad_kv[:, at * rows : at * rows + rows] for at in range(BIN // rows)]
    own = part[0] + from_partner(part[1].astype(bf16), 1).astype(f32)
    far = part[2] + from_partner(part[3].astype(bf16), 1).astype(f32)
    own = own + from_partner(far.astype(bf16), 2).astype(f32)
    grad_packed_t = jnp.concatenate([grad_query_t, own.astype(bf16)], axis=0)
    grad_qkv = lax.dot_general(normed, grad_packed_t, (((0,), (1,)), ((), ())), preferred_element_type=f32).astype(bf16)
    grad_normed = lax.dot_general(grad_packed_t, w_qkv, (((0,), (1,)), ((), ())), preferred_element_type=f32)
    _, norm_one_pull = jax.vjp(layer_norm, stream_zero, gain_one, shift_one)
    grad_zero_part, grad_gain_one, grad_shift_one = norm_one_pull(grad_normed)
    grad_input = grad_stream_one + grad_zero_part
    grad_time_t = outer_sum(grad_input.astype(bf16), features).astype(bf16)

    vectors = jnp.stack([grad_gain_one, grad_shift_one, grad_gain_two, grad_shift_two, grad_bias_back], axis=1)
    vectors = jnp.concatenate([vectors, grad_bias_in.reshape(D, -1)], axis=1)
    vectors = jnp.pad(vectors, ((0, 0), (0, 128 - vectors.shape[1]))).astype(bf16)
    grad_small = jnp.concatenate([grad_time_t, vectors], axis=1)
    arrays = (grad_back, grad_in, grad_out_weight, grad_qkv, grad_small)
    sums = jnp.concatenate(
        [sums[:HEADS], sums[HEADS : 2 * HEADS] + sums[2 * HEADS : 3 * HEADS], sums[3 * HEADS : 4 * HEADS] + sums[4 * HEADS :]]
    )
    if own_rows % 8 == 0:
        grad_back, grad_in, grad_out_weight, grad_qkv, grad_small, sums = scatter_call(
            sizes, arrays, 2, total=sums, total_at=0
        )
    else:
        sums = lax.psum(sums, axes)
        grad_back, grad_in, grad_out_weight, grad_qkv, grad_small = (
            lax.psum_scatter(array.astype(f32), axes, scatter_dimension=0, tiled=True) for array in arrays
        )
    vectors = grad_small[:, TFREQ:]
    weight_t = pair_weight.astype(f32).T
    low, once, twice = sums[:HEADS], sums[HEADS : 2 * HEADS], sums[2 * HEADS :]
    zeroth, first, square = (jnp.sum(weight_t * part_sum, axis=0) for part_sum in (low, once, twice))
    mean = kernel_mean - center
    grad_mean = (first - mean * zeroth) / (kernel_width * kernel_width)
    grad_width = (square - 2.0 * mean * first + mean * mean * zeroth) / (
        kernel_width * kernel_width * kernel_width
    ) - zeroth / kernel_width
    return (
        output,
        grad_input,
        grad_small[:, :TFREQ].T,
        vectors[:, 0],
        vectors[:, 1],
        grad_qkv,
        grad_out_weight,
        vectors[:, 2],
        vectors[:, 3],
        grad_in,
        vectors[:, 5 : 5 + own_hidden // own_rows].reshape(-1),
        grad_back,
        vectors[:, 4],
        low.T,
        grad_mean,
        grad_width,
    )


def solution(mesh):
    in_specs = (
        P(("grp", "dev"), None),
        P(None, ("grp", "dev")),
        P(("grp", "dev")),
        P(("grp", "dev")),
        P(None, ("grp", "dev")),
        P(("grp", "dev")),
        P(("grp", "dev")),
        P(("grp", "dev"), None),
        P(("grp", "dev"), None),
        P(("grp", "dev")),
        P(("grp", "dev")),
        P(("grp", "dev"), None),
        P(("grp", "dev")),
        P(("grp", "dev"), None),
        P(("grp", "dev")),
        P(),
        P(),
        P(),
        P(("grp", "dev"), None),
    )
    out_specs = (
        P(("grp", "dev"), None),
        P(("grp", "dev"), None),
        P(None, ("grp", "dev")),
        P(("grp", "dev")),
        P(("grp", "dev")),
        P(("grp", "dev"), None),
        P(("grp", "dev"), None),
        P(("grp", "dev")),
        P(("grp", "dev")),
        P(("grp", "dev"), None),
        P(("grp", "dev")),
        P(("grp", "dev"), None),
        P(("grp", "dev")),
        P(),
        P(),
        P(),
    )
    return jax.shard_map(partial(shards, grid_of_mesh(mesh)), mesh=mesh, in_specs=in_specs, out_specs=out_specs, check_vma=False)
```

```python
from functools import partial
import itertools
import math

import jax
import jax.numpy as jnp
from jax import lax
from jax.experimental import pallas as pl
from jax.experimental.pallas import tpu as pltpu
from jax.sharding import PartitionSpec as P
import ml_dtypes
import numpy as np

D = 768
HEADS = 32
HDIM = 24
KERN = 128
TFREQ = 128
BIN = 1024
GROUPS = 4
GHEADS = HEADS // GROUPS
GWIDTH = GHEADS * HDIM
PAIR_ROWS = 16
GRAD_ROWS = 32
ATT_ROWS = 128
UNIT_LANES = 768
UNIT_ROWS = 32
SLACK = 2
LAST_TURNS = 5
VECTORS = 6

norm_eps = 1e-05
mask_fill = -1e30
log2e = math.log2(math.e)
center = 6.0
f32 = jnp.float32
bf16 = jnp.bfloat16
VMEM_LIMIT = 58 * 1024 * 1024
MESH = pl.DeviceIdType.MESH


def dot(left, right):
    return jnp.dot(left, right, preferred_element_type=f32)


def lanes_dot(left, right):
    return lax.dot_general(left, right, (((1,), (1,)), ((), ())), preferred_element_type=f32)


def rows_dot(left, right):
    return lax.dot_general(left, right, (((0,), (0,)), ((), ())), preferred_element_type=f32)


def grid_of_mesh(mesh):
    count = mesh.shape["dev"] // 2
    wide = 1
    while wide * wide < count:
        wide *= 2
    return mesh.shape["grp"], count // wide, wide, 2


def my_place(sizes):
    _, _, wide, cores = sizes
    dev = lax.axis_index("dev")
    return (lax.axis_index("grp"), dev // (wide * cores), lax.rem(dev // cores, wide), lax.rem(dev, cores))


def device_at(place, sizes):
    _, _, wide, cores = sizes
    return (place[0], (place[1] * wide + place[2]) * cores + place[3])


def other_place(place, axis, shift, sizes):
    moved = list(place)
    moved[axis] = lax.rem(place[axis] + shift, sizes[axis])
    return tuple(moved)


def block_partners(place):
    _, _, x, core = place
    beside, across = 1 - core, x + 1 - 2 * lax.rem(x, 2)
    return (
        place[:3] + (beside,),
        place[:2] + (across, core),
        place[:2] + (across, beside),
    )


def axis_partners(place, sizes):
    return [other_place(place, axis, shift, sizes) for axis in range(4) for shift in range(1, sizes[axis])]


def meet(partners, sizes):
    barrier = pltpu.get_barrier_semaphore()
    for partner in partners:
        pl.semaphore_signal(barrier, inc=1, device_id=device_at(partner, sizes), device_id_type=MESH)
    pl.semaphore_wait(barrier, len(partners))


def send(source, goal, sems, at, partner, sizes):
    return pltpu.make_async_remote_copy(
        src_ref=source,
        dst_ref=goal,
        send_sem=sems[0].at[at],
        recv_sem=sems[1].at[at],
        device_id=device_at(partner, sizes),
        device_id_type=MESH,
    )


class Staged:
    def place_stages(self, order, place, sizes):
        self.order, self.place, self.sizes = order, place, sizes
        self.base = [0]
        for axis in order:
            self.base.append(self.base[-1] + sizes[axis] - 1)

    def copies(self, stage):
        found = []
        for shift in range(1, self.sizes[self.order[stage]]):
            target = other_place(self.place, self.order[stage], shift, self.sizes)
            source, goal = self.ends(stage, shift, target)
            sem = self.base[stage] + shift - 1
            found.append(
                pltpu.make_async_remote_copy(
                    src_ref=source,
                    dst_ref=goal,
                    send_sem=self.send_sem.at[self.at, sem],
                    recv_sem=self.recv_sem.at[self.at, sem],
                    device_id=device_at(target, self.sizes),
                    device_id_type=MESH,
                )
            )
        return found

    def start(self, stage):
        for copy in self.copies(stage):
            copy.start()

    def arrive(self, stage):
        for copy in self.copies(stage):
            copy.wait_recv()

    def finish(self):
        for stage in range(len(self.order)):
            for copy in self.copies(stage):
                copy.wait_send()


class GatherPart(Staged):
    def __init__(self, source, full, rows, lanes, order, at, send_sem, recv_sem, place, sizes):
        self.source, self.full, self.rows, self.lanes = source, full, rows, lanes
        self.at, self.send_sem, self.recv_sem = at, send_sem, recv_sem
        self.place_stages(order, place, sizes)

    def ends(self, stage, shift, target):
        done = self.order[:stage]
        where = tuple(slice(None) if axis in done else self.place[axis] for axis in range(4))
        held = self.full.at[where + (self.rows, self.lanes)]
        return (self.source.at[self.rows, self.lanes] if stage == 0 else held), held


class ScatterPart(Staged):
    def __init__(self, source, result, rows, lanes, order, buffers, at, send_sem, recv_sem, own_sem, place, sizes):
        self.source, self.result, self.rows, self.lanes = source, result, rows, lanes
        self.first, self.slots = buffers[0], buffers[1:]
        self.at, self.send_sem, self.recv_sem, self.own_sem = at, send_sem, recv_sem, own_sem
        self.place_stages(order, place, sizes)

    def pick(self, stage, index):
        if stage == 0:
            where = tuple(index if axis == self.order[0] else slice(None) for axis in range(4))
            return self.source.at[where + (self.rows, self.lanes)]
        holder = self.first if stage == 1 else self.slots[stage - 1].at[0]
        left = [axis for axis in range(4) if axis not in self.order[:stage]]
        return holder.at[tuple(index if axis == self.order[stage] else slice(None) for axis in left)]

    def own_copy(self):
        return pltpu.make_async_copy(self.pick(0, self.place[self.order[0]]), self.first, self.own_sem.at[self.at])

    def ends(self, stage, shift, target):
        return self.pick(stage, target[self.order[stage]]), self.slots[stage].at[shift - 1]

    def start(self, stage):
        if stage == 0:
            self.own_copy().start()
        super().start(stage)

    def arrive(self, stage):
        if stage == 0:
            self.own_copy().wait()
        super().arrive(stage)
        slots = self.slots[stage]
        count = self.sizes[self.order[stage]] - 1
        mine = self.first if stage == 0 else self.pick(stage, self.place[self.order[stage]])
        lead = slots.shape[1:-2]
        if not lead:
            total = mine[...].astype(f32)
            for slot in range(count):
                total = total + slots[slot].astype(f32)
            self.result[self.rows, self.lanes] = total
            return

        def add(outer, carry):
            for inner in itertools.product(*map(range, lead[1:])):
                where = (outer,) + inner
                total = mine[where].astype(f32)
                for slot in range(count):
                    total = total + slots[(slot,) + where].astype(f32)
                if stage == 0:
                    self.first[where] = total.astype(bf16)
                else:
                    slots[(0,) + where] = total.astype(bf16)
            return carry

        lax.fori_loop(0, lead[0], add, 0)


class TotalPart(Staged):
    def __init__(self, source, result, slots, send_sem, recv_sem, place, sizes):
        self.source, self.result, self.slots = source, result, slots
        self.at, self.send_sem, self.recv_sem = 0, send_sem, recv_sem
        self.place_stages((3, 2, 1, 0), place, sizes)

    def ends(self, stage, shift, target):
        mine = self.slots[stage].at[self.place[self.order[stage]]]
        return mine, mine

    def start(self, stage):
        if stage == 0:
            self.slots[0][self.place[3]] = self.source[...]
        super().start(stage)

    def arrive(self, stage):
        super().arrive(stage)
        total = self.slots[stage][0]
        for at in range(1, self.sizes[self.order[stage]]):
            total = total + self.slots[stage][at]
        if stage == 3:
            self.result[...] = total
        else:
            self.slots[stage + 1][self.place[self.order[stage + 1]]] = total


def stage_turns(groups, stages=4, slack=SLACK):
    def opening():
        for group in groups[:slack]:
            for part in group:
                part.start(0)

    def turn(at):
        if at + slack < len(groups):
            for part in groups[at + slack]:
                part.start(0)
        for stage in range(stages - 1, -1, -1):
            index = at - slack * stage
            if 0 <= index < len(groups):
                for part in groups[index]:
                    part.arrive(stage)
                    if stage + 1 < stages:
                        part.start(stage + 1)

    def closing():
        for group in groups:
            for part in group:
                part.finish()

    return opening, [partial(turn, at) for at in range(len(groups) + slack * (stages - 1))], closing


def spread_turns(step, steps, turns, phase=0, phases=1):
    span = steps * phases - 1
    for at in range(steps):
        point = at * phases + phase - 1
        todo = turns[point * len(turns) // span : (point + 1) * len(turns) // span] if point >= 0 else []
        if todo:

            @pl.when(step == at)
            def _():
                for turn in todo:
                    turn()


def pieces(rows, lanes):
    if rows > UNIT_ROWS and rows % UNIT_ROWS == 0:
        return [(at, UNIT_ROWS, 0, lanes) for at in range(0, rows, UNIT_ROWS)]
    if lanes > UNIT_LANES and lanes % UNIT_LANES == 0:
        return [(0, rows, at, UNIT_LANES) for at in range(0, lanes, UNIT_LANES)]
    return [(0, rows, 0, lanes)]


def make_plan(shapes, first_order, second_order):
    plan = []
    for at, (rows, lanes) in enumerate(shapes):
        for row, height, lane, width in pieces(rows, lanes):
            half = width // 256 * 128
            group = [(at, (row, height), (lane + half, width - half), second_order)]
            if half:
                group.insert(0, (at, (row, height), (lane, half), first_order))
            plan.append(group)
    return plan


def part_count(plan):
    return sum(map(len, plan))


def slot_count(sizes):
    return sum(size - 1 for size in sizes)


def gather_plan(shapes):
    return make_plan(shapes, (0, 2, 1, 3), (0, 1, 2, 3))


def gather_groups(plan, sources, fulls, send_sem, recv_sem, place, sizes):
    groups, index = [], 0
    for group in plan:
        groups.append([])
        for at, rows, lanes, order in group:
            groups[-1].append(
                GatherPart(
                    sources[at], fulls[at], pl.ds(*rows), pl.ds(*lanes), order, index, send_sem, recv_sem, place, sizes
                )
            )
            index += 1
    return groups


def scatter_plan(shapes):
    return make_plan(shapes, (3, 2, 1, 0), (3, 1, 2, 0))


def scatter_scratch(sizes, plan):
    parts, slots = part_count(plan), slot_count(sizes)
    scratch = [
        pltpu.SemaphoreType.DMA((parts, slots)),
        pltpu.SemaphoreType.DMA((parts, slots)),
        pltpu.SemaphoreType.DMA((parts,)),
    ]
    for at, rows, lanes, order in sum(plan, []):
        block = (rows[1], lanes[1])
        left = [0, 1, 2, 3]
        for stage, axis in enumerate(order):
            left.remove(axis)
            lead = tuple(sizes[other] for other in left)
            if stage == 0:
                scratch.append(pltpu.VMEM(lead + block, bf16))
            scratch.append(pltpu.VMEM((sizes[axis] - 1,) + lead + block, bf16))
    return scratch


def scatter_groups(plan, sources, results, scratch, place, sizes):
    send_sem, recv_sem, own_sem = scratch[:3]
    groups, index = [], 0
    for group in plan:
        groups.append([])
        for at, rows, lanes, order in group:
            held = scratch[3 + 5 * index : 8 + 5 * index]
            groups[-1].append(
                ScatterPart(
                    sources[at],
                    results[at],
                    pl.ds(*rows),
                    pl.ds(*lanes),
                    order,
                    held,
                    index,
                    send_sem,
                    recv_sem,
                    own_sem,
                    place,
                    sizes,
                )
            )
            index += 1
    return groups


def scatter_shapes(sizes, arrays):
    return [(array.shape[0] // math.prod(sizes), array.shape[1]) for array in arrays]


anywhere = pl.BlockSpec(memory_space=pl.ANY)
in_vmem = pl.BlockSpec(memory_space=pltpu.VMEM)


def pair_block(places_i, keys, coef, weight_t, dist_ref, phi_ref, bias_ref, mask_scr, between):
    square = None
    for axis in range(3):
        gap = places_i[:, axis : axis + 1] - keys[axis : axis + 1, :]
        square = gap * gap if square is None else square + gap * gap
    dist_ref[...] = jnp.sqrt(square)
    mask_scr[...] = jnp.where(places_i[:, 3:4] == keys[3:4, :], 0.0, mask_fill).astype(f32)
    for u in range(PAIR_ROWS):
        if u == PAIR_ROWS // 2:
            between()
        for kg in range(KERN // 16):
            rows = slice(kg * 16, kg * 16 + 16)
            mean, inv, shift = coef[0, rows, :], coef[1, rows, :], coef[2, rows, :]
            for jv in range(BIN // 128):
                z = (dist_ref[u : u + 1, jv * 128 : jv * 128 + 128] - mean) * inv
                lanes = slice(u * BIN + jv * 128, u * BIN + jv * 128 + 128)
                phi_ref[rows, lanes] = jnp.exp2(shift - z * z).astype(bf16)
    bias = dot(weight_t[...], phi_ref[...])
    for u in range(PAIR_ROWS):
        part = bias[:, u * BIN : u * BIN + BIN] * log2e + mask_scr[u : u + 1, :]
        for g in range(GROUPS):
            bias_ref[g, u * GHEADS : u * GHEADS + GHEADS, :] = part[g * GHEADS : g * GHEADS + GHEADS, :]


def pair_kernel(sizes, plan, count, steps, positions, items, mean, width, weight_t, time_weight, *refs):
    vectors, refs = refs[:VECTORS], refs[VECTORS:]
    sources, refs = (refs[-1],) + refs[: count - 1], refs[count - 1 : -1]
    (dist_ref, phi_ref, bias_ref), refs = refs[:3], refs[3:]
    fulls, refs = refs[:count], refs[count:]
    mask_scr, keys, columns, coef, send_sem, recv_sem, own_sem, place_send, place_recv = refs
    step = pl.program_id(0)
    place = my_place(sizes)
    rows = positions.shape[1]
    opening, turns, closing = stage_turns(gather_groups(plan, sources, fulls, send_sem, recv_sem, place, sizes))
    own = [pltpu.make_async_copy(sources[at], fulls[at].at[place], own_sem.at[at]) for at in range(count)]
    shared = [
        send(
            keys.at[:, pl.ds(0, rows)],
            keys.at[:, pl.ds((at + 1) * rows, rows)],
            (place_send, place_recv),
            at,
            partner,
            sizes,
        )
        for at, partner in enumerate(block_partners(place))
    ]

    @pl.when(step == 0)
    def _():
        here = jnp.concatenate([positions[...], items[...], jnp.zeros((4, rows), f32)], axis=0)
        keys[:, pl.ds(0, rows)] = here
        columns[...] = here.T
        square = lambda values: jnp.broadcast_to(values, (KERN, KERN)).T
        coef[0] = square(mean[...])
        coef[1] = square(math.sqrt(0.5 * log2e) / width[...])
        coef[2] = square(-log2e * jnp.log(math.sqrt(2.0 * math.pi) * width[...]))
        mask_scr[...] = jnp.zeros_like(mask_scr)
        for at, vector in enumerate(vectors):
            mask_scr[at : at + 1, pl.ds(0, vector.shape[1])] = vector[...].astype(f32)
        rest = mask_scr[0 : sources[0].shape[0] - time_weight.shape[1], pl.ds(0, TFREQ)]
        sources[0][...] = jnp.concatenate([time_weight[...].astype(f32).T, rest], axis=0).astype(bf16)
        meet(axis_partners(place, sizes) + [block_partners(place)[2]], sizes)
        for copy in own:
            copy.start()
        for copy in shared:
            copy.start()
        opening()
        for copy in own:
            copy.wait()
        for copy in shared:
            copy.wait()

    spread_turns(step, steps, turns, 0, 2)
    pair_block(
        columns[pl.ds(pl.multiple_of(step * PAIR_ROWS, PAIR_ROWS), PAIR_ROWS), :],
        keys,
        coef,
        weight_t,
        dist_ref,
        phi_ref.at[0],
        bias_ref,
        mask_scr,
        lambda: spread_turns(step, steps, turns, 1, 2),
    )

    @pl.when(step == steps - 1)
    def _():
        closing()


def pair_call(sizes, positions, items, mean, width, weight_t, time_weight, vectors, arrays, collective):
    rows = positions.shape[1]
    count = 1 + len(arrays)
    steps = rows // PAIR_ROWS
    own = time_weight.shape[1]
    small = jax.ShapeDtypeStruct((own + 8, TFREQ), bf16)
    plan = gather_plan([array.shape for array in (small, *arrays)])
    parts, slots = part_count(plan), slot_count(sizes)
    outs = pl.pallas_call(
        partial(pair_kernel, sizes, plan, count, steps),
        grid=(steps,),
        in_specs=[in_vmem] * (6 + VECTORS) + [anywhere] * len(arrays),
        out_specs=[
            pl.BlockSpec((PAIR_ROWS, BIN), lambda i: (i, 0)),
            pl.BlockSpec((1, KERN, PAIR_ROWS * BIN), lambda i: (i, 0, 0)),
            pl.BlockSpec((GROUPS, PAIR_ROWS * GHEADS, BIN), lambda i: (0, i, 0)),
        ]
        + [anywhere] * count,
        out_shape=[
            jax.ShapeDtypeStruct((rows, BIN), f32),
            jax.ShapeDtypeStruct((steps, KERN, PAIR_ROWS * BIN), bf16),
            jax.ShapeDtypeStruct((GROUPS, rows * GHEADS, BIN), f32),
        ]
        + [jax.ShapeDtypeStruct(sizes + array.shape, array.dtype) for array in (small, *arrays)],
        scratch_shapes=[
            pltpu.VMEM((PAIR_ROWS, BIN), f32),
            pltpu.VMEM((8, BIN), f32),
            pltpu.VMEM((rows, 8), f32),
            pltpu.VMEM((3, KERN, KERN), f32),
            pltpu.SemaphoreType.DMA((parts, slots)),
            pltpu.SemaphoreType.DMA((parts, slots)),
            pltpu.SemaphoreType.DMA((count,)),
            pltpu.SemaphoreType.DMA((3,)),
            pltpu.SemaphoreType.DMA((3,)),
            pltpu.VMEM(small.shape, bf16),
        ],
        compiler_params=pltpu.CompilerParams(
            collective_id=collective, has_side_effects=True, vmem_limit_bytes=VMEM_LIMIT
        ),
        name="pair_bias_and_gather",
    )(positions, items, mean, width, weight_t, time_weight, *vectors, *arrays)
    return outs[0], outs[1], outs[2], [full.reshape((-1,) + full.shape[4:]) for full in outs[3:]]


def spread_tables():
    row = np.arange(ATT_ROWS * GHEADS)
    spread = row[:, None] // GHEADS == np.arange(ATT_ROWS)[None, :]
    head = row[:, None] % GHEADS == np.arange(GWIDTH)[None, :] // HDIM
    return tuple(jnp.asarray(table.astype(ml_dtypes.bfloat16)) for table in (spread, spread.T, head, head.T))


table_specs = [in_vmem] * 4


class BlockShare:
    def __init__(self, own, full, far, near, forward, place, sizes):
        self.own, self.full, self.sizes = own, full, sizes
        self.far_sems, self.near_sems, self.forward_sems = far, near, forward
        self.beside, self.across, _ = block_partners(place)
        self.width = own.shape[1]

    def rows(self, g, which):
        return pl.ds(which * D + g * GWIDTH, GWIDTH)

    def lanes(self, at):
        return pl.ds(at * self.width, self.width)

    def far(self, g):
        return [
            send(
                self.own.at[self.rows(g, which)],
                self.full.at[self.rows(g, which), self.lanes(2)],
                self.far_sems,
                g * 2 + which,
                self.across,
                self.sizes,
            )
            for which in range(2)
        ]

    def near(self, g):
        return [
            send(
                self.own.at[self.rows(g, which)],
                self.full.at[self.rows(g, which), self.lanes(1)],
                self.near_sems,
                g * 2 + which,
                self.beside,
                self.sizes,
            )
            for which in range(2)
        ]

    def forward(self, g):
        return [
            send(
                self.full.at[self.rows(g, which), self.lanes(2)],
                self.full.at[self.rows(g, which), self.lanes(3)],
                self.forward_sems,
                g * 2 + which,
                self.beside,
                self.sizes,
            )
            for which in range(2)
        ]

    def open(self):
        for copy in self.far(0) + self.far(1):
            copy.start()
        for g in range(GROUPS):
            for copy in self.near(g):
                copy.start()

    def pass_on(self, g):
        for copy in self.far(g):
            copy.wait_recv()
        for copy in self.forward(g) + (self.far(g + 2) if g + 2 < GROUPS else []):
            copy.start()

    def ready(self, g):
        for copy in self.near(g) + self.forward(g):
            copy.wait_recv()

    def close(self):
        for g in range(GROUPS):
            for copy in self.far(g) + self.near(g) + self.forward(g):
                copy.wait_send()


def forward_kernel(sizes, parts, q_ref, own_ref, bias_ref, spread, gather, head, head_t, out_ref, prob_ref, kv_out, kv_ref, out_sems, *sems):
    group, part = pl.program_id(0), pl.program_id(1)
    place = my_place(sizes)
    share = BlockShare(own_ref, kv_ref, sems[0:2], sems[2:4], sems[4:6], place, sizes)
    kept = [
        pltpu.make_async_copy(kv_ref.at[share.rows(g, which)], kv_out.at[share.rows(g, which)], out_sems.at[g * 2 + which])
        for g in range(GROUPS)
        for which in range(2)
    ]
    for g in range(GROUPS):

        @pl.when((group == g) & (part == 0))
        def _():
            if g == 0:
                kv_ref[:, pl.ds(0, share.width)] = own_ref[...]
                meet([share.beside, share.across], sizes)
                share.open()
                share.pass_on(0)
            share.ready(g)
            for copy in kept[2 * g : 2 * g + 2]:
                copy.start()

        if g + 1 < GROUPS:

            @pl.when((group == g) & (part == parts - 1))
            def _():
                share.pass_on(g + 1)

    first_row = pl.multiple_of(group * GWIDTH, GWIDTH)
    key_rows, value_rows = pl.ds(first_row, GWIDTH), pl.ds(pl.multiple_of(D + first_row, GWIDTH), GWIDTH)
    wide = ATT_ROWS * GHEADS
    query = lanes_dot(spread[...], q_ref[...]).astype(bf16) * head[...]
    chunk = 256
    for first in range(0, wide, chunk):
        at = slice(first, first + chunk)
        score = dot(query[at], kv_ref[key_rows, :]) * (HDIM**-0.5 * log2e) + bias_ref[0, at, :]
        top = jnp.max(score, axis=-1, keepdims=True)
        weight = jnp.exp2(score - top)
        total = jnp.sum(weight, axis=-1, keepdims=True)
        prob_ref[0, at, :] = (weight * (1.0 / total)).astype(bf16)
    mixed = lanes_dot(kv_ref[value_rows, :], prob_ref[0]).astype(bf16) * head_t[...]
    out_ref[...] = lanes_dot(mixed, gather[...]).astype(bf16)

    @pl.when((group == GROUPS - 1) & (part == parts - 1))
    def _():
        share.close()
        for copy in kept:
            copy.wait()


def forward_call(sizes, q_t, kv_t, bias, tables, collective):
    rows = q_t.shape[1]
    wide = ATT_ROWS * GHEADS
    parts = rows // ATT_ROWS
    return pl.pallas_call(
        partial(forward_kernel, sizes, parts),
        grid=(GROUPS, parts),
        in_specs=[
            pl.BlockSpec((GWIDTH, ATT_ROWS), lambda g, i: (g, i)),
            in_vmem,
            pl.BlockSpec((1, wide, BIN), lambda g, i: (g, i, 0)),
        ]
        + table_specs,
        out_specs=[
            pl.BlockSpec((GWIDTH, ATT_ROWS), lambda g, i: (g, i)),
            pl.BlockSpec((1, wide, BIN), lambda g, i: (g, i, 0)),
            anywhere,
        ],
        out_shape=[
            jax.ShapeDtypeStruct((D, rows), bf16),
            jax.ShapeDtypeStruct((GROUPS, rows * GHEADS, BIN), bf16),
            jax.ShapeDtypeStruct((2 * D, BIN), bf16),
        ],
        scratch_shapes=[pltpu.VMEM((2 * D, BIN), bf16)] + [pltpu.SemaphoreType.DMA((2 * GROUPS,))] * 7,
        compiler_params=pltpu.CompilerParams(
            collective_id=collective, has_side_effects=True, vmem_limit_bytes=VMEM_LIMIT
        ),
        name="attention_forward",
    )(q_t, kv_t, bias, *tables)


class BlockSum:
    def __init__(self, outbox, near, far, result, near_sems, far_sems, place, sizes):
        self.outbox, self.near, self.far, self.result = outbox, near, far, result
        self.near_sems, self.far_sems = near_sems, far_sems
        self.sizes = sizes
        self.beside, self.across, _ = block_partners(place)
        self.width = result.shape[1]

    def block(self, g, which, at):
        return self.outbox.at[g, which, :, pl.ds(at * self.width, self.width)]

    def near_copies(self, g):
        return [
            send(
                self.block(g, which, 2 * slot + 1),
                self.near.at[g, which, slot],
                self.near_sems,
                g * 4 + which * 2 + slot,
                self.beside,
                self.sizes,
            )
            for which in range(2)
            for slot in range(2)
        ]

    def far_copies(self, g):
        return [
            send(self.block(g, which, 2), self.far.at[g, which], self.far_sems, g * 2 + which, self.across, self.sizes)
            for which in range(2)
        ]

    def open(self, g):
        for copy in self.near_copies(g):
            copy.start()

    def middle(self, g):
        for copy in self.near_copies(g):
            copy.wait_recv()
        for which in range(2):
            here = self.block(g, which, 2)
            here[...] = (here[...].astype(f32) + self.near[g, which, 1].astype(f32)).astype(bf16)
        for copy in self.far_copies(g):
            copy.start()

    def close(self, g):
        for copy in self.far_copies(g):
            copy.wait_recv()
        for which in range(2):
            total = self.block(g, which, 0)[...].astype(f32) + self.near[g, which, 0].astype(f32)
            total = total + self.far[g, which].astype(f32)
            self.result[pl.ds(which * D + g * GWIDTH, GWIDTH), :] = total.astype(bf16)

    def finish(self):
        for g in range(GROUPS):
            for copy in self.near_copies(g) + self.far_copies(g):
                copy.wait_send()


def backward_kernel(
    sizes, plan, count, steps, q_ref, go_ref, k_ref, v_ref, prob_ref, spread, gather, head, head_t, *refs
):
    sources, refs = refs[:count], refs[count:]
    (gs_ref, gq_ref, own_ref), refs = refs[:3], refs[3:]
    results, refs = refs[:count], refs[count:]
    (key_sum, value_sum, outbox, near, far), refs = refs[:5], refs[5:]
    near_sems, far_sems, scratch = refs[:2], refs[2:4], refs[4:]
    group, part, parts = pl.program_id(0), pl.program_id(1), steps // GROUPS
    step = group * parts + part
    place = my_place(sizes)
    block = BlockSum(outbox, near, far, own_ref, near_sems, far_sems, place, sizes)
    if count:
        opening, turns, closing = stage_turns(scatter_groups(plan, sources, results, scratch, place, sizes))

    @pl.when(step == 0)
    def _():
        partners = axis_partners(place, sizes) if count else [block.beside, block.across]
        meet(partners, sizes)
        if count:
            opening()

    for g in range(1, GROUPS):

        @pl.when((group == g) & (part == 0))
        def _():
            block.middle(g - 1)
            if g >= 2:
                block.close(g - 2)

    if count:
        spread_turns(step, steps, turns, 0, 2)

    wide = ATT_ROWS * GHEADS
    grad_out = lanes_dot(spread[...], go_ref[...]).astype(bf16) * head[...]
    chunk = 256
    for first in range(0, wide, chunk):
        at = slice(first, first + chunk)
        prob = prob_ref[0, at, :].astype(f32)
        grad_prob = dot(grad_out[at], v_ref[...])
        inner = jnp.sum(prob * grad_prob, axis=-1, keepdims=True)
        gs_ref[0, at, :] = (prob * (grad_prob - inner)).astype(bf16)
    if count:
        spread_turns(step, steps, turns, 1, 2)

    grad_query = lanes_dot(k_ref[...], gs_ref[0]) * (HDIM**-0.5)
    gq_ref[...] = lanes_dot(grad_query.astype(bf16) * head_t[...], gather[...]).astype(bf16)
    query_t = lanes_dot(q_ref[...], spread[...]).astype(bf16) * head_t[...]
    grad_out_t = lanes_dot(go_ref[...], spread[...]).astype(bf16) * head_t[...]
    grad_key = dot(query_t, gs_ref[0])
    grad_value = dot(grad_out_t, prob_ref[0])

    @pl.when(part == 0)
    def _():
        key_sum[...] = grad_key
        value_sum[...] = grad_value

    @pl.when(part > 0)
    def _():
        key_sum[...] += grad_key
        value_sum[...] += grad_value

    for g in range(GROUPS):

        @pl.when((group == g) & (part == parts - 1))
        def _():
            outbox[g, 0] = (key_sum[...] * (HDIM**-0.5)).astype(bf16)
            outbox[g, 1] = value_sum[...].astype(bf16)
            block.open(g)

    @pl.when(step == steps - 1)
    def _():
        block.middle(GROUPS - 1)
        block.close(GROUPS - 2)
        if count:
            closing()
        block.close(GROUPS - 1)
        block.finish()


def backward_call(sizes, q_t, go_t, kv_t, prob, tables, arrays, collective):
    rows = q_t.shape[1]
    wide = ATT_ROWS * GHEADS
    parts = rows // ATT_ROWS
    count = len(arrays)
    shapes = scatter_shapes(sizes, arrays)
    plan = scatter_plan(shapes)
    return pl.pallas_call(
        partial(backward_kernel, sizes, plan, count, GROUPS * parts),
        grid=(GROUPS, parts),
        in_specs=[
            pl.BlockSpec((GWIDTH, ATT_ROWS), lambda g, i: (g, i)),
            pl.BlockSpec((GWIDTH, ATT_ROWS), lambda g, i: (g, i)),
            pl.BlockSpec((GWIDTH, BIN), lambda g, i: (g, 0)),
            pl.BlockSpec((GWIDTH, BIN), lambda g, i: (g + GROUPS, 0)),
            pl.BlockSpec((1, wide, BIN), lambda g, i: (g, i, 0)),
        ]
        + table_specs
        + [anywhere] * count,
        out_specs=[
            pl.BlockSpec((1, wide, BIN), lambda g, i: (g, i, 0)),
            pl.BlockSpec((GWIDTH, ATT_ROWS), lambda g, i: (g, i)),
            in_vmem,
        ]
        + [in_vmem] * count,
        out_shape=[
            jax.ShapeDtypeStruct((GROUPS, rows * GHEADS, BIN), bf16),
            jax.ShapeDtypeStruct((D, rows), bf16),
            jax.ShapeDtypeStruct((2 * D, rows), bf16),
        ]
        + [jax.ShapeDtypeStruct(shape, f32) for shape in shapes],
        scratch_shapes=[
            pltpu.VMEM((GWIDTH, BIN), f32),
            pltpu.VMEM((GWIDTH, BIN), f32),
            pltpu.VMEM((GROUPS, 2, GWIDTH, BIN), bf16),
            pltpu.VMEM((GROUPS, 2, 2, GWIDTH, rows), bf16),
            pltpu.VMEM((GROUPS, 2, GWIDTH, rows), bf16),
            pltpu.SemaphoreType.DMA((4 * GROUPS,)),
            pltpu.SemaphoreType.DMA((4 * GROUPS,)),
            pltpu.SemaphoreType.DMA((2 * GROUPS,)),
            pltpu.SemaphoreType.DMA((2 * GROUPS,)),
        ]
        + (scatter_scratch(sizes, plan) if count else []),
        compiler_params=pltpu.CompilerParams(
            collective_id=collective, has_side_effects=True, vmem_limit_bytes=VMEM_LIMIT
        ),
        name="attention_backward",
    )(q_t, go_t, kv_t, kv_t, prob, *tables, *[array.reshape(sizes + shape) for array, shape in zip(arrays, shapes)])


def kernel_gradients(sums, weight_t, mean, width):
    weight_t = weight_t.astype(f32)
    shifted = mean - center
    zeroth, once, twice = (
        jnp.sum(weight_t * sums[at * HEADS : at * HEADS + HEADS], axis=0, keepdims=True) for at in range(3)
    )
    grad_mean = (once - shifted * zeroth) / (width * width)
    grad_width = (twice - 2.0 * shifted * once + shifted * shifted * zeroth) / (width * width * width) - zeroth / width
    return sums[:HEADS], grad_mean, grad_width


def split_small(small, own_hidden):
    rows = small.shape[0]
    vectors = small[:, TFREQ:].T
    return (small[:, :TFREQ].T, *(vectors[at : at + 1] for at in range(5)), vectors[5 : 5 + own_hidden // rows])


def pair_grad_kernel(sizes, plan, count, steps, gs_ref, dist_ref, phi_ref, *refs):
    sources, refs = refs[:count], refs[count:]
    sum_ref, refs = refs[0], refs[1:]
    results, refs = refs[:count], refs[count:]
    (terms, sums), refs = refs[:2], refs[2:]
    step = pl.program_id(0)
    place = my_place(sizes)
    if count:
        total_slots, total_send, total_recv, scratch = refs[:4], refs[4], refs[5], refs[6:]
        total = TotalPart(sums, sum_ref, total_slots, total_send, total_recv, place, sizes)
        opening, turns, closing = stage_turns(scatter_groups(plan, sources, results, scratch, place, sizes))
        tail = min(LAST_TURNS, len(turns))

    @pl.when(step == 0)
    def _():
        sums[...] = jnp.zeros_like(sums)
        if count:
            meet(axis_partners(place, sizes), sizes)
            opening()

    if count:
        spread_turns(step, steps, turns[: len(turns) - tail], 0, 2)

    for u in range(GRAD_ROWS):
        lanes = slice(u * BIN, u * BIN + BIN)
        dist = dist_ref[u : u + 1, :] - center
        for g in range(0, GROUPS, 2):
            low = gs_ref[g, u * GHEADS : u * GHEADS + GHEADS, :].astype(f32)
            high = gs_ref[g + 1, u * GHEADS : u * GHEADS + GHEADS, :].astype(f32)
            grad = jnp.concatenate([low, high], axis=0)
            once = grad * dist
            twice = once * dist
            once_top = once.astype(bf16)
            twice_top = twice.astype(bf16)
            kinds = (
                grad.astype(bf16),
                once_top,
                (once - once_top.astype(f32)).astype(bf16),
                twice_top,
                (twice - twice_top.astype(f32)).astype(bf16),
            )
            for at, kind in enumerate(kinds):
                terms[at * HEADS + g * GHEADS : at * HEADS + (g + 2) * GHEADS, lanes] = kind
    if count:
        spread_turns(step, steps, turns[: len(turns) - tail], 1, 2)

    found = None
    for half in range(GRAD_ROWS // PAIR_ROWS):
        wide = PAIR_ROWS * BIN
        more = lanes_dot(terms[:, half * wide : half * wide + wide], phi_ref[half])
        found = more if found is None else found + more
    sums[:HEADS] += found[:HEADS]
    sums[HEADS : 2 * HEADS] += found[HEADS : 2 * HEADS] + found[2 * HEADS : 3 * HEADS]
    sums[2 * HEADS :] += found[3 * HEADS : 4 * HEADS] + found[4 * HEADS :]

    @pl.when(step == steps - 1)
    def _():
        if not count:
            sum_ref[...] = sums[...]
            return
        total.start(0)
        for at in range(max(tail, 4)):
            if at < tail:
                turns[len(turns) - tail + at]()
            if at < 4:
                total.arrive(at)
                if at < 3:
                    total.start(at + 1)
        closing()
        total.finish()


def pair_grad_call(sizes, gs, dist, phi, arrays, collective):
    rows = dist.shape[0]
    steps = rows // GRAD_ROWS
    count = len(arrays)
    shapes = scatter_shapes(sizes, arrays)
    plan = scatter_plan(shapes)
    total = (3 * HEADS, KERN)
    scratch = [pltpu.VMEM((5 * HEADS, GRAD_ROWS * BIN), bf16), pltpu.VMEM(total, f32)]
    remote = {}
    if count:
        scratch += [pltpu.VMEM((sizes[axis],) + total, f32) for axis in (3, 2, 1, 0)]
        scratch += [pltpu.SemaphoreType.DMA((1, slot_count(sizes)))] * 2
        scratch += scatter_scratch(sizes, plan)
        remote = dict(collective_id=collective, has_side_effects=True)
    return pl.pallas_call(
        partial(pair_grad_kernel, sizes, plan, count, steps),
        grid=(steps,),
        in_specs=[
            pl.BlockSpec((GROUPS, GRAD_ROWS * GHEADS, BIN), lambda i: (0, i, 0)),
            pl.BlockSpec((GRAD_ROWS, BIN), lambda i: (i, 0)),
            pl.BlockSpec((GRAD_ROWS // PAIR_ROWS, KERN, PAIR_ROWS * BIN), lambda i: (i, 0, 0)),
        ]
        + [anywhere] * count,
        out_specs=[in_vmem] * (count + 1),
        out_shape=[jax.ShapeDtypeStruct(total, f32)] + [jax.ShapeDtypeStruct(shape, f32) for shape in shapes],
        scratch_shapes=scratch,
        compiler_params=pltpu.CompilerParams(vmem_limit_bytes=VMEM_LIMIT, **remote),
        name="pair_gradient",
    )(gs, dist, phi, *[array.reshape(sizes + shape) for array, shape in zip(arrays, shapes)])


def settle_kernel(own_hidden, count, sums, weight_t, mean, width, small, *refs):
    values = list(kernel_gradients(sums[...], weight_t[...], mean[...], width[...]))
    values[0] = values[0].T
    values += split_small(small[...], own_hidden)
    for ref, value in zip(refs[count : count + len(values)], values):
        ref[...] = value
    for source, goal in zip(refs[:count], refs[count + len(values) :]):
        goal[...] = source[...]


def settle_call(sums, weight_t, mean, width, small, arrays, own_hidden):
    own = small.shape[0]
    shapes = [(KERN, HEADS), (1, KERN), (1, KERN), (TFREQ, own)] + [(1, own)] * 5 + [(own_hidden // own, own)]
    shapes += [array.shape for array in arrays]
    found = pl.pallas_call(
        partial(settle_kernel, own_hidden, len(arrays)),
        in_specs=[in_vmem] * (5 + len(arrays)),
        out_specs=[in_vmem] * len(shapes),
        out_shape=[jax.ShapeDtypeStruct(shape, f32) for shape in shapes],
        compiler_params=pltpu.CompilerParams(vmem_limit_bytes=VMEM_LIMIT),
        name="settle_gradients",
    )(sums, weight_t, mean, width, small, *arrays)
    return found[:3], found[3:10], found[10:]


def layer_norm(values, norm_gain, norm_offset):
    middle = values - jnp.mean(values, axis=-1, keepdims=True)
    spread = jnp.mean(middle * middle, axis=-1, keepdims=True)
    return middle * lax.rsqrt(spread + norm_eps) * norm_gain + norm_offset


def time_features(time_values):
    half_count = TFREQ // 2
    frequency = jnp.exp(jnp.arange(half_count, dtype=f32) * (-math.log(10000.0) / half_count))
    angles = (1000.0 * time_values)[:, None] * frequency[None, :]
    return jnp.concatenate([jnp.sin(angles), jnp.cos(angles)], axis=1)


def all_scattered(arrays):
    return [lax.psum_scatter(array.astype(f32), ("grp", "dev"), scatter_dimension=0, tiled=True) for array in arrays]


def shards(
    sizes,
    atoms,
    positions,
    segment,
    item_time,
    time_weight,
    norm1_gain,
    norm1_bias,
    qkv_weight,
    out_weight,
    norm2_gain,
    norm2_bias,
    ffn_in,
    ffn_in_bias,
    ffn_out,
    ffn_out_bias,
    pair_weight,
    kernel_mean,
    kernel_width,
    cotangent,
):
    axes = ("grp", "dev")
    own_rows, own_hidden = norm1_gain.shape[0], ffn_in_bias.shape[0]
    mean, width, weight_t = kernel_mean[None], kernel_width[None], pair_weight.T
    vectors = [v[None] for v in (norm1_gain, norm1_bias, norm2_gain, norm2_bias, ffn_out_bias, ffn_in_bias)]
    dist, phi, bias, (small, w_qkv, w_out, w_in, w_back) = pair_call(
        sizes,
        positions,
        segment.astype(f32)[None],
        mean,
        width,
        weight_t,
        time_weight,
        vectors,
        (qkv_weight, out_weight, ffn_in, ffn_out),
        1,
    )
    tables = spread_tables()
    w_qkv, w_out, w_in, w_back = (full.reshape(-1, full.shape[2]) for full in (w_qkv, w_out, w_in, w_back))
    w_time_t = small[:, :own_rows].reshape(-1, TFREQ)
    vectors = small[:, own_rows:].astype(f32).transpose(1, 0, 2)
    gain_one, shift_one, gain_two, shift_two, bias_back = (vectors[at, :, :own_rows].reshape(-1) for at in range(5))
    bias_in = vectors[5, :, :own_hidden].reshape(-1)

    features = time_features(item_time).astype(bf16)
    stream_zero = atoms.astype(f32) + lanes_dot(features, w_time_t)
    normed = layer_norm(stream_zero, gain_one, shift_one).astype(bf16)
    packed_t = lax.dot_general(w_qkv, normed, (((0,), (1,)), ((), ())), preferred_element_type=f32).astype(bf16)
    q_t = packed_t[:D]
    mixed_t, prob, kv_t = forward_call(sizes, q_t, packed_t[D:], bias, tables, 5)

    stream_one = stream_zero + lax.dot_general(mixed_t, w_out, (((0,), (0,)), ((), ())), preferred_element_type=f32)
    second = layer_norm(stream_one, gain_two, shift_two).astype(bf16)
    hidden_pre = dot(second, w_in) + bias_in
    hidden_act = jax.nn.gelu(hidden_pre, approximate=False).astype(bf16)
    output = (stream_one + dot(hidden_act, w_back) + bias_back).astype(bf16)

    grad_output = cotangent.astype(f32)
    grad_branch = cotangent
    grad_back = rows_dot(hidden_act, grad_branch).astype(bf16)
    grad_bias_back = jnp.sum(grad_output, axis=0)
    grad_act = lanes_dot(grad_branch, w_back)
    _, gelu_pull = jax.vjp(lambda pre: jax.nn.gelu(pre, approximate=False), hidden_pre)
    grad_pre = gelu_pull(grad_act)[0].astype(bf16)
    grad_in = rows_dot(second, grad_pre).astype(bf16)
    grad_bias_in = jnp.sum(grad_pre.astype(f32), axis=0)
    grad_second = lanes_dot(grad_pre, w_in)
    _, norm_two_pull = jax.vjp(layer_norm, stream_one, gain_two, shift_two)
    grad_stream_part, grad_gain_two, grad_shift_two = norm_two_pull(grad_second)
    grad_stream_one = grad_output + grad_stream_part
    grad_attn = grad_stream_one.astype(bf16)
    grad_out_weight = dot(mixed_t, grad_attn).astype(bf16)
    grad_mixed_t = lanes_dot(w_out, grad_attn).astype(bf16)

    own_sums = own_rows % 8 == 0
    early = (grad_back,) if own_sums else ()
    gs, grad_query_t, own, *early_sums = backward_call(sizes, q_t, grad_mixed_t, kv_t, prob, tables, early, 2)
    grad_packed_t = jnp.concatenate([grad_query_t, own], axis=0)
    grad_qkv = lax.dot_general(normed, grad_packed_t, (((0,), (1,)), ((), ())), preferred_element_type=f32).astype(bf16)
    grad_normed = lax.dot_general(grad_packed_t, w_qkv, (((0,), (1,)), ((), ())), preferred_element_type=f32)
    _, norm_one_pull = jax.vjp(layer_norm, stream_zero, gain_one, shift_one)
    grad_zero_part, grad_gain_one, grad_shift_one = norm_one_pull(grad_normed)
    grad_input = grad_stream_one + grad_zero_part
    grad_time_t = rows_dot(grad_input.astype(bf16), features).astype(bf16)

    vectors = jnp.stack([grad_gain_one, grad_shift_one, grad_gain_two, grad_shift_two, grad_bias_back], axis=1)
    vectors = jnp.concatenate([vectors, grad_bias_in.reshape(D // own_rows, -1, own_rows).transpose(0, 2, 1).reshape(D, -1)], axis=1)
    vectors = jnp.pad(vectors, ((0, 0), (0, 128 - vectors.shape[1]))).astype(bf16)
    grad_small = jnp.concatenate([grad_time_t, vectors], axis=1)
    late = (grad_in, grad_out_weight, grad_qkv, grad_small) if own_sums else ()
    sums, *late_sums = pair_grad_call(sizes, gs, dist, phi, late, 3)
    if own_sums:
        grad_small, weight_sums = late_sums[3], (*early_sums, *late_sums[:3])
    else:
        *weight_sums, grad_small = all_scattered((grad_back, grad_in, grad_out_weight, grad_qkv, grad_small))
        sums = lax.psum(sums, axes)
    (grad_pair, grad_mean, grad_width), small_grads, weight_sums = settle_call(
        sums, weight_t, mean, width, grad_small, weight_sums, own_hidden
    )
    grad_back, grad_in, grad_out_weight, grad_qkv = weight_sums
    grad_time, *vector_grads, grad_hidden = small_grads
    grad_gain_one, grad_shift_one, grad_gain_two, grad_shift_two, grad_bias_back = (row[0] for row in vector_grads)
    return (
        output,
        grad_input,
        grad_time,
        grad_gain_one,
        grad_shift_one,
        grad_qkv,
        grad_out_weight,
        grad_gain_two,
        grad_shift_two,
        grad_in,
        grad_hidden.reshape(-1),
        grad_back,
        grad_bias_back,
        grad_pair,
        grad_mean[0],
        grad_width[0],
    )


def solution(mesh):
    in_specs = (
        P(("grp", "dev"), None),
        P(None, ("grp", "dev")),
        P(("grp", "dev")),
        P(("grp", "dev")),
        P(None, ("grp", "dev")),
        P(("grp", "dev")),
        P(("grp", "dev")),
        P(("grp", "dev"), None),
        P(("grp", "dev"), None),
        P(("grp", "dev")),
        P(("grp", "dev")),
        P(("grp", "dev"), None),
        P(("grp", "dev")),
        P(("grp", "dev"), None),
        P(("grp", "dev")),
        P(),
        P(),
        P(),
        P(("grp", "dev"), None),
    )
    out_specs = (
        P(("grp", "dev"), None),
        P(("grp", "dev"), None),
        P(None, ("grp", "dev")),
        P(("grp", "dev")),
        P(("grp", "dev")),
        P(("grp", "dev"), None),
        P(("grp", "dev"), None),
        P(("grp", "dev")),
        P(("grp", "dev")),
        P(("grp", "dev"), None),
        P(("grp", "dev")),
        P(("grp", "dev"), None),
        P(("grp", "dev")),
        P(),
        P(),
        P(),
    )
    return jax.shard_map(partial(shards, grid_of_mesh(mesh)), mesh=mesh, in_specs=in_specs, out_specs=out_specs, check_vma=False)
```

```python
from functools import partial
import itertools
import math

import jax
import jax.numpy as jnp
from jax import lax
from jax.experimental import pallas as pl
from jax.experimental.pallas import tpu as pltpu
from jax.sharding import PartitionSpec as P
import ml_dtypes
import numpy as np

D = 768
HEADS = 32
HDIM = 24
KERN = 128
TFREQ = 128
BIN = 1024
GROUPS = 4
GHEADS = HEADS // GROUPS
GWIDTH = GHEADS * HDIM
PAIR_ROWS = 16
GRAD_ROWS = 32
ATT_ROWS = 128
UNIT_LANES = 768
UNIT_ROWS = 32
FEED_LANES = 512
SLACK = 2
LAST_TURNS = 5
VECTORS = 6

norm_eps = 1e-05
mask_fill = -1e30
log2e = math.log2(math.e)
center = 6.0
f32 = jnp.float32
bf16 = jnp.bfloat16
VMEM_LIMIT = 58 * 1024 * 1024
MESH = pl.DeviceIdType.MESH


def dot(left, right):
    return jnp.dot(left, right, preferred_element_type=f32)


def lanes_dot(left, right):
    return lax.dot_general(left, right, (((1,), (1,)), ((), ())), preferred_element_type=f32)


def rows_dot(left, right):
    return lax.dot_general(left, right, (((0,), (0,)), ((), ())), preferred_element_type=f32)


def grid_of_mesh(mesh):
    count = mesh.shape["dev"] // 2
    wide = 1
    while wide * wide < count:
        wide *= 2
    return mesh.shape["grp"], count // wide, wide, 2


def my_place(sizes):
    _, _, wide, cores = sizes
    dev = lax.axis_index("dev")
    return (lax.axis_index("grp"), dev // (wide * cores), lax.rem(dev // cores, wide), lax.rem(dev, cores))


def device_at(place, sizes):
    _, _, wide, cores = sizes
    return (place[0], (place[1] * wide + place[2]) * cores + place[3])


def other_place(place, axis, shift, sizes):
    moved = list(place)
    moved[axis] = lax.rem(place[axis] + shift, sizes[axis])
    return tuple(moved)


def block_partners(place):
    _, _, x, core = place
    beside, across = 1 - core, x + 1 - 2 * lax.rem(x, 2)
    return (
        place[:3] + (beside,),
        place[:2] + (across, core),
        place[:2] + (across, beside),
    )


def axis_partners(place, sizes):
    return [other_place(place, axis, shift, sizes) for axis in range(4) for shift in range(1, sizes[axis])]


def meet(partners, sizes):
    barrier = pltpu.get_barrier_semaphore()
    for partner in partners:
        pl.semaphore_signal(barrier, inc=1, device_id=device_at(partner, sizes), device_id_type=MESH)
    pl.semaphore_wait(barrier, len(partners))


def send(source, goal, sems, at, partner, sizes):
    return pltpu.make_async_remote_copy(
        src_ref=source,
        dst_ref=goal,
        send_sem=sems[0].at[at],
        recv_sem=sems[1].at[at],
        device_id=device_at(partner, sizes),
        device_id_type=MESH,
    )


class Staged:
    def place_stages(self, order, place, sizes):
        self.order, self.place, self.sizes = order, place, sizes
        self.base = [0]
        for axis in order:
            self.base.append(self.base[-1] + sizes[axis] - 1)

    def copies(self, stage):
        found = []
        for shift in range(1, self.sizes[self.order[stage]]):
            target = other_place(self.place, self.order[stage], shift, self.sizes)
            source, goal = self.ends(stage, shift, target)
            sem = self.base[stage] + shift - 1
            found.append(
                pltpu.make_async_remote_copy(
                    src_ref=source,
                    dst_ref=goal,
                    send_sem=self.send_sem.at[self.at, sem],
                    recv_sem=self.recv_sem.at[self.at, sem],
                    device_id=device_at(target, self.sizes),
                    device_id_type=MESH,
                )
            )
        return found

    def start(self, stage):
        for copy in self.copies(stage):
            copy.start()

    def arrive(self, stage):
        for copy in self.copies(stage):
            copy.wait_recv()

    def finish(self):
        for stage in range(len(self.order)):
            for copy in self.copies(stage):
                copy.wait_send()


class GatherPart(Staged):
    def __init__(self, source, full, rows, lanes, order, at, send_sem, recv_sem, place, sizes):
        self.source, self.full, self.rows, self.lanes = source, full, rows, lanes
        self.at, self.send_sem, self.recv_sem = at, send_sem, recv_sem
        self.place_stages(order, place, sizes)

    def ends(self, stage, shift, target):
        done = self.order[:stage]
        where = tuple(slice(None) if axis in done else self.place[axis] for axis in range(4))
        held = self.full.at[where + (self.rows, self.lanes)]
        return (self.source.at[self.rows, self.lanes] if stage == 0 else held), held


class ScatterPart(Staged):
    def __init__(self, source, result, rows, lanes, order, buffers, at, send_sem, recv_sem, own_sem, place, sizes):
        self.source, self.result, self.rows, self.lanes = source, result, rows, lanes
        self.first, self.slots = buffers[0], buffers[1:]
        self.at, self.send_sem, self.recv_sem, self.own_sem = at, send_sem, recv_sem, own_sem
        self.place_stages(order, place, sizes)

    def pick(self, stage, index):
        if stage == 0:
            where = tuple(index if axis == self.order[0] else slice(None) for axis in range(4))
            return self.source.at[where + (self.rows, self.lanes)]
        holder = self.first if stage == 1 else self.slots[stage - 1].at[0]
        left = [axis for axis in range(4) if axis not in self.order[:stage]]
        return holder.at[tuple(index if axis == self.order[stage] else slice(None) for axis in left)]

    def own_copy(self):
        return pltpu.make_async_copy(self.pick(0, self.place[self.order[0]]), self.first, self.own_sem.at[self.at])

    def ends(self, stage, shift, target):
        return self.pick(stage, target[self.order[stage]]), self.slots[stage].at[shift - 1]

    def start(self, stage):
        if stage == 0:
            self.own_copy().start()
        super().start(stage)

    def arrive(self, stage):
        if stage == 0:
            self.own_copy().wait()
        super().arrive(stage)
        slots = self.slots[stage]
        count = self.sizes[self.order[stage]] - 1
        mine = self.first if stage == 0 else self.pick(stage, self.place[self.order[stage]])
        lead = slots.shape[1:-2]
        if not lead:
            total = mine[...].astype(f32)
            for slot in range(count):
                total = total + slots[slot].astype(f32)
            self.result[self.rows, self.lanes] = total
            return

        def add(outer, carry):
            for inner in itertools.product(*map(range, lead[1:])):
                where = (outer,) + inner
                total = mine[where].astype(f32)
                for slot in range(count):
                    total = total + slots[(slot,) + where].astype(f32)
                if stage == 0:
                    self.first[where] = total.astype(bf16)
                else:
                    slots[(0,) + where] = total.astype(bf16)
            return carry

        lax.fori_loop(0, lead[0], add, 0)


class TotalPart(Staged):
    def __init__(self, source, result, slots, send_sem, recv_sem, place, sizes):
        self.source, self.result, self.slots = source, result, slots
        self.at, self.send_sem, self.recv_sem = 0, send_sem, recv_sem
        self.place_stages((3, 2, 1, 0), place, sizes)

    def ends(self, stage, shift, target):
        mine = self.slots[stage].at[self.place[self.order[stage]]]
        return mine, mine

    def start(self, stage):
        if stage == 0:
            self.slots[0][self.place[3]] = self.source[...]
        super().start(stage)

    def arrive(self, stage):
        super().arrive(stage)
        total = self.slots[stage][0]
        for at in range(1, self.sizes[self.order[stage]]):
            total = total + self.slots[stage][at]
        if stage == 3:
            self.result[...] = total
        else:
            self.slots[stage + 1][self.place[self.order[stage + 1]]] = total


def stage_turns(groups, stages=4, slack=SLACK):
    def opening():
        for group in groups[:slack]:
            for part in group:
                part.start(0)

    def turn(at):
        if at + slack < len(groups):
            for part in groups[at + slack]:
                part.start(0)
        for stage in range(stages - 1, -1, -1):
            index = at - slack * stage
            if 0 <= index < len(groups):
                for part in groups[index]:
                    part.arrive(stage)
                    if stage + 1 < stages:
                        part.start(stage + 1)

    def closing():
        for group in groups:
            for part in group:
                part.finish()

    return opening, [partial(turn, at) for at in range(len(groups) + slack * (stages - 1))], closing


def spread_turns(step, steps, turns, phase=0, phases=1):
    span = steps * phases - 1
    for at in range(steps):
        point = at * phases + phase - 1
        todo = turns[point * len(turns) // span : (point + 1) * len(turns) // span] if point >= 0 else []
        if todo:

            @pl.when(step == at)
            def _():
                for turn in todo:
                    turn()


def pieces(rows, lanes):
    if rows > UNIT_ROWS and rows % UNIT_ROWS == 0:
        return [(at, UNIT_ROWS, 0, lanes) for at in range(0, rows, UNIT_ROWS)]
    if lanes > UNIT_LANES and lanes % UNIT_LANES == 0:
        return [(0, rows, at, UNIT_LANES) for at in range(0, lanes, UNIT_LANES)]
    return [(0, rows, 0, lanes)]


def make_plan(shapes, first_order, second_order):
    plan = []
    for at, (rows, lanes) in enumerate(shapes):
        for row, height, lane, width in pieces(rows, lanes):
            half = width // 256 * 128
            group = [(at, (row, height), (lane + half, width - half), second_order)]
            if half:
                group.insert(0, (at, (row, height), (lane, half), first_order))
            plan.append(group)
    return plan


def part_count(plan):
    return sum(map(len, plan))


def slot_count(sizes):
    return sum(size - 1 for size in sizes)


def gather_plan(shapes):
    return make_plan(shapes, (0, 2, 1, 3), (0, 1, 2, 3))


def gather_groups(plan, sources, fulls, send_sem, recv_sem, place, sizes):
    groups, index = [], 0
    for group in plan:
        groups.append([])
        for at, rows, lanes, order in group:
            groups[-1].append(
                GatherPart(
                    sources[at], fulls[at], pl.ds(*rows), pl.ds(*lanes), order, index, send_sem, recv_sem, place, sizes
                )
            )
            index += 1
    return groups


def scatter_plan(shapes):
    return make_plan(shapes, (3, 2, 1, 0), (3, 1, 2, 0))


def scatter_scratch(sizes, plan):
    parts, slots = part_count(plan), slot_count(sizes)
    scratch = [
        pltpu.SemaphoreType.DMA((parts, slots)),
        pltpu.SemaphoreType.DMA((parts, slots)),
        pltpu.SemaphoreType.DMA((parts,)),
    ]
    for at, rows, lanes, order in sum(plan, []):
        block = (rows[1], lanes[1])
        left = [0, 1, 2, 3]
        for stage, axis in enumerate(order):
            left.remove(axis)
            lead = tuple(sizes[other] for other in left)
            if stage == 0:
                scratch.append(pltpu.VMEM(lead + block, bf16))
            scratch.append(pltpu.VMEM((sizes[axis] - 1,) + lead + block, bf16))
    return scratch


def scatter_groups(plan, sources, results, scratch, place, sizes):
    send_sem, recv_sem, own_sem = scratch[:3]
    groups, index = [], 0
    for group in plan:
        groups.append([])
        for at, rows, lanes, order in group:
            held = scratch[3 + 5 * index : 8 + 5 * index]
            groups[-1].append(
                ScatterPart(
                    sources[at],
                    results[at],
                    pl.ds(*rows),
                    pl.ds(*lanes),
                    order,
                    held,
                    index,
                    send_sem,
                    recv_sem,
                    own_sem,
                    place,
                    sizes,
                )
            )
            index += 1
    return groups


def scatter_shapes(sizes, arrays):
    return [(array.shape[0] // math.prod(sizes), array.shape[1]) for array in arrays]


anywhere = pl.BlockSpec(memory_space=pl.ANY)
in_vmem = pl.BlockSpec(memory_space=pltpu.VMEM)


def pair_block(places_i, keys, coef, weight_t, dist_ref, phi_ref, bias_ref, mask_scr, between):
    square = None
    for axis in range(3):
        gap = places_i[:, axis : axis + 1] - keys[axis : axis + 1, :]
        square = gap * gap if square is None else square + gap * gap
    dist_ref[...] = jnp.sqrt(square)
    mask_scr[...] = jnp.where(places_i[:, 3:4] == keys[3:4, :], 0.0, mask_fill).astype(f32)
    for u in range(PAIR_ROWS):
        if u == PAIR_ROWS // 2:
            between()
        for kg in range(KERN // 16):
            rows = slice(kg * 16, kg * 16 + 16)
            mean, inv, shift = coef[0, rows, :], coef[1, rows, :], coef[2, rows, :]
            for jv in range(BIN // 128):
                z = (dist_ref[u : u + 1, jv * 128 : jv * 128 + 128] - mean) * inv
                lanes = slice(u * BIN + jv * 128, u * BIN + jv * 128 + 128)
                phi_ref[rows, lanes] = jnp.exp2(shift - z * z).astype(bf16)
    bias = dot(weight_t[...], phi_ref[...])
    for u in range(PAIR_ROWS):
        part = bias[:, u * BIN : u * BIN + BIN] * log2e + mask_scr[u : u + 1, :]
        for g in range(GROUPS):
            bias_ref[g, u * GHEADS : u * GHEADS + GHEADS, :] = part[g * GHEADS : g * GHEADS + GHEADS, :]


def pair_kernel(sizes, plan, count, steps, positions, items, mean, width, weight_t, time_weight, *refs):
    vectors, refs = refs[:VECTORS], refs[VECTORS:]
    sources, refs = (refs[-1],) + refs[: count - 1], refs[count - 1 : -1]
    (dist_ref, phi_ref, bias_ref), refs = refs[:3], refs[3:]
    fulls, refs = refs[:count], refs[count:]
    mask_scr, keys, columns, coef, send_sem, recv_sem, own_sem, place_send, place_recv = refs
    step = pl.program_id(0)
    place = my_place(sizes)
    rows = positions.shape[1]
    opening, turns, closing = stage_turns(gather_groups(plan, sources, fulls, send_sem, recv_sem, place, sizes))
    own = [pltpu.make_async_copy(sources[at], fulls[at].at[place], own_sem.at[at]) for at in range(count)]
    shared = [
        send(
            keys.at[:, pl.ds(0, rows)],
            keys.at[:, pl.ds((at + 1) * rows, rows)],
            (place_send, place_recv),
            at,
            partner,
            sizes,
        )
        for at, partner in enumerate(block_partners(place))
    ]

    @pl.when(step == 0)
    def _():
        here = jnp.concatenate([positions[...], items[...], jnp.zeros((4, rows), f32)], axis=0)
        keys[:, pl.ds(0, rows)] = here
        columns[...] = here.T
        square = lambda values: jnp.broadcast_to(values, (KERN, KERN)).T
        coef[0] = square(mean[...])
        coef[1] = square(math.sqrt(0.5 * log2e) / width[...])
        coef[2] = square(-log2e * jnp.log(math.sqrt(2.0 * math.pi) * width[...]))
        mask_scr[...] = jnp.zeros_like(mask_scr)
        for at, vector in enumerate(vectors):
            mask_scr[at : at + 1, pl.ds(0, vector.shape[1])] = vector[...].astype(f32)
        rest = mask_scr[0 : sources[0].shape[0] - time_weight.shape[1], pl.ds(0, TFREQ)]
        sources[0][...] = jnp.concatenate([time_weight[...].astype(f32).T, rest], axis=0).astype(bf16)
        meet(axis_partners(place, sizes) + [block_partners(place)[2]], sizes)
        for copy in own:
            copy.start()
        for copy in shared:
            copy.start()
        opening()
        for copy in own:
            copy.wait()
        for copy in shared:
            copy.wait()

    spread_turns(step, steps, turns, 0, 2)
    pair_block(
        columns[pl.ds(pl.multiple_of(step * PAIR_ROWS, PAIR_ROWS), PAIR_ROWS), :],
        keys,
        coef,
        weight_t,
        dist_ref,
        phi_ref.at[0],
        bias_ref,
        mask_scr,
        lambda: spread_turns(step, steps, turns, 1, 2),
    )

    @pl.when(step == steps - 1)
    def _():
        closing()


def pair_call(sizes, positions, items, mean, width, weight_t, time_weight, vectors, arrays, collective):
    rows = positions.shape[1]
    count = 1 + len(arrays)
    steps = rows // PAIR_ROWS
    own = time_weight.shape[1]
    small = jax.ShapeDtypeStruct((own + 8, TFREQ), bf16)
    plan = gather_plan([array.shape for array in (small, *arrays)])
    parts, slots = part_count(plan), slot_count(sizes)
    outs = pl.pallas_call(
        partial(pair_kernel, sizes, plan, count, steps),
        grid=(steps,),
        in_specs=[in_vmem] * (6 + VECTORS) + [anywhere] * len(arrays),
        out_specs=[
            pl.BlockSpec((PAIR_ROWS, BIN), lambda i: (i, 0)),
            pl.BlockSpec((1, KERN, PAIR_ROWS * BIN), lambda i: (i, 0, 0)),
            pl.BlockSpec((GROUPS, PAIR_ROWS * GHEADS, BIN), lambda i: (0, i, 0)),
        ]
        + [anywhere] * count,
        out_shape=[
            jax.ShapeDtypeStruct((rows, BIN), f32),
            jax.ShapeDtypeStruct((steps, KERN, PAIR_ROWS * BIN), bf16),
            jax.ShapeDtypeStruct((GROUPS, rows * GHEADS, BIN), f32),
        ]
        + [jax.ShapeDtypeStruct(sizes + array.shape, array.dtype) for array in (small, *arrays)],
        scratch_shapes=[
            pltpu.VMEM((PAIR_ROWS, BIN), f32),
            pltpu.VMEM((8, BIN), f32),
            pltpu.VMEM((rows, 8), f32),
            pltpu.VMEM((3, KERN, KERN), f32),
            pltpu.SemaphoreType.DMA((parts, slots)),
            pltpu.SemaphoreType.DMA((parts, slots)),
            pltpu.SemaphoreType.DMA((count,)),
            pltpu.SemaphoreType.DMA((3,)),
            pltpu.SemaphoreType.DMA((3,)),
            pltpu.VMEM(small.shape, bf16),
        ],
        compiler_params=pltpu.CompilerParams(
            collective_id=collective, has_side_effects=True, vmem_limit_bytes=VMEM_LIMIT
        ),
        name="pair_bias_and_gather",
    )(positions, items, mean, width, weight_t, time_weight, *vectors, *arrays)
    return outs[0], outs[1], outs[2], [full.reshape((-1,) + full.shape[4:]) for full in outs[3:]]


def spread_tables():
    row = np.arange(ATT_ROWS * GHEADS)
    spread = row[:, None] // GHEADS == np.arange(ATT_ROWS)[None, :]
    head = row[:, None] % GHEADS == np.arange(GWIDTH)[None, :] // HDIM
    return tuple(jnp.asarray(table.astype(ml_dtypes.bfloat16)) for table in (spread, spread.T, head, head.T))


table_specs = [in_vmem] * 4


class BlockShare:
    def __init__(self, own, full, far, near, forward, place, sizes):
        self.own, self.full, self.sizes = own, full, sizes
        self.far_sems, self.near_sems, self.forward_sems = far, near, forward
        self.beside, self.across, _ = block_partners(place)
        self.width = own.shape[1]

    def rows(self, g, which):
        return pl.ds(which * D + g * GWIDTH, GWIDTH)

    def lanes(self, at):
        return pl.ds(at * self.width, self.width)

    def far(self, g):
        return [
            send(
                self.own.at[self.rows(g, which)],
                self.full.at[self.rows(g, which), self.lanes(2)],
                self.far_sems,
                g * 2 + which,
                self.across,
                self.sizes,
            )
            for which in range(2)
        ]

    def near(self, g):
        return [
            send(
                self.own.at[self.rows(g, which)],
                self.full.at[self.rows(g, which), self.lanes(1)],
                self.near_sems,
                g * 2 + which,
                self.beside,
                self.sizes,
            )
            for which in range(2)
        ]

    def forward(self, g):
        return [
            send(
                self.full.at[self.rows(g, which), self.lanes(2)],
                self.full.at[self.rows(g, which), self.lanes(3)],
                self.forward_sems,
                g * 2 + which,
                self.beside,
                self.sizes,
            )
            for which in range(2)
        ]

    def open(self):
        for copy in self.far(0) + self.far(1):
            copy.start()
        for g in range(GROUPS):
            for copy in self.near(g):
                copy.start()

    def pass_on(self, g):
        for copy in self.far(g):
            copy.wait_recv()
        for copy in self.forward(g) + (self.far(g + 2) if g + 2 < GROUPS else []):
            copy.start()

    def ready(self, g):
        for copy in self.near(g) + self.forward(g):
            copy.wait_recv()

    def close(self):
        for g in range(GROUPS):
            for copy in self.far(g) + self.near(g) + self.forward(g):
                copy.wait_send()


def forward_kernel(
    sizes, plan, count, parts, q_ref, own_ref, bias_ref, spread, gather, head, head_t, *refs
):
    sources, refs = refs[:count], refs[count:]
    (out_ref, prob_ref, kv_out), refs = refs[:3], refs[3:]
    fulls, refs = refs[:count], refs[count:]
    (kv_ref, out_sems), sems, (send_sem, recv_sem, own_sem) = refs[:2], refs[2:8], refs[8:]
    group, part = pl.program_id(0), pl.program_id(1)
    step, steps = group * parts + part, GROUPS * parts
    place = my_place(sizes)
    share = BlockShare(own_ref, kv_ref, sems[0:2], sems[2:4], sems[4:6], place, sizes)
    opening, turns, closing = stage_turns(gather_groups(plan, sources, fulls, send_sem, recv_sem, place, sizes))
    held = [pltpu.make_async_copy(sources[at], fulls[at].at[place], own_sem.at[at]) for at in range(count)]
    kept = [
        pltpu.make_async_copy(kv_ref.at[share.rows(g, which)], kv_out.at[share.rows(g, which)], out_sems.at[g * 2 + which])
        for g in range(GROUPS)
        for which in range(2)
    ]
    for g in range(GROUPS):

        @pl.when((group == g) & (part == 0))
        def _():
            if g == 0:
                kv_ref[:, pl.ds(0, share.width)] = own_ref[...]
                meet(axis_partners(place, sizes), sizes)
                share.open()
                for copy in held:
                    copy.start()
                opening()
                for copy in held:
                    copy.wait()
                share.pass_on(0)
            share.ready(g)
            for copy in kept[2 * g : 2 * g + 2]:
                copy.start()

        if g + 1 < GROUPS:

            @pl.when((group == g) & (part == parts - 1))
            def _():
                share.pass_on(g + 1)

    spread_turns(step, steps, turns, 0, 2)
    first_row = pl.multiple_of(group * GWIDTH, GWIDTH)
    key_rows, value_rows = pl.ds(first_row, GWIDTH), pl.ds(pl.multiple_of(D + first_row, GWIDTH), GWIDTH)
    wide = ATT_ROWS * GHEADS
    query = lanes_dot(spread[...], q_ref[...]).astype(bf16) * head[...]
    chunk = 256
    for first in range(0, wide, chunk):
        at = slice(first, first + chunk)
        score = dot(query[at], kv_ref[key_rows, :]) * (HDIM**-0.5 * log2e) + bias_ref[0, at, :]
        top = jnp.max(score, axis=-1, keepdims=True)
        weight = jnp.exp2(score - top)
        total = jnp.sum(weight, axis=-1, keepdims=True)
        prob_ref[0, at, :] = (weight * (1.0 / total)).astype(bf16)
    spread_turns(step, steps, turns, 1, 2)
    mixed = lanes_dot(kv_ref[value_rows, :], prob_ref[0]).astype(bf16) * head_t[...]
    out_ref[...] = lanes_dot(mixed, gather[...]).astype(bf16)

    @pl.when((group == GROUPS - 1) & (part == parts - 1))
    def _():
        closing()
        share.close()
        for copy in kept:
            copy.wait()


def forward_call(sizes, q_t, kv_t, bias, tables, arrays, collective):
    rows = q_t.shape[1]
    wide = ATT_ROWS * GHEADS
    parts = rows // ATT_ROWS
    count = len(arrays)
    plan = gather_plan([array.shape for array in arrays])
    pieces_held, slots = part_count(plan), slot_count(sizes)
    outs = pl.pallas_call(
        partial(forward_kernel, sizes, plan, count, parts),
        grid=(GROUPS, parts),
        in_specs=[
            pl.BlockSpec((GWIDTH, ATT_ROWS), lambda g, i: (g, i)),
            in_vmem,
            pl.BlockSpec((1, wide, BIN), lambda g, i: (g, i, 0)),
        ]
        + table_specs
        + [anywhere] * count,
        out_specs=[
            pl.BlockSpec((GWIDTH, ATT_ROWS), lambda g, i: (g, i)),
            pl.BlockSpec((1, wide, BIN), lambda g, i: (g, i, 0)),
            anywhere,
        ]
        + [anywhere] * count,
        out_shape=[
            jax.ShapeDtypeStruct((D, rows), bf16),
            jax.ShapeDtypeStruct((GROUPS, rows * GHEADS, BIN), bf16),
            jax.ShapeDtypeStruct((2 * D, BIN), bf16),
        ]
        + [jax.ShapeDtypeStruct(sizes + array.shape, array.dtype) for array in arrays],
        scratch_shapes=[pltpu.VMEM((2 * D, BIN), bf16)]
        + [pltpu.SemaphoreType.DMA((2 * GROUPS,))] * 7
        + [pltpu.SemaphoreType.DMA((pieces_held, slots))] * 2
        + [pltpu.SemaphoreType.DMA((count,))],
        compiler_params=pltpu.CompilerParams(
            collective_id=collective, has_side_effects=True, vmem_limit_bytes=VMEM_LIMIT
        ),
        name="attention_forward",
    )(q_t, kv_t, bias, *tables, *arrays)
    return outs[0], outs[1], outs[2], [full.reshape((-1, full.shape[-1])) for full in outs[3:]]


class BlockSum:
    def __init__(self, outbox, near, far, result, near_sems, far_sems, place, sizes):
        self.outbox, self.near, self.far, self.result = outbox, near, far, result
        self.near_sems, self.far_sems = near_sems, far_sems
        self.sizes = sizes
        self.beside, self.across, _ = block_partners(place)
        self.width = result.shape[1]

    def block(self, g, which, at):
        return self.outbox.at[g, which, :, pl.ds(at * self.width, self.width)]

    def near_copies(self, g):
        return [
            send(
                self.block(g, which, 2 * slot + 1),
                self.near.at[g, which, slot],
                self.near_sems,
                g * 4 + which * 2 + slot,
                self.beside,
                self.sizes,
            )
            for which in range(2)
            for slot in range(2)
        ]

    def far_copies(self, g):
        return [
            send(self.block(g, which, 2), self.far.at[g, which], self.far_sems, g * 2 + which, self.across, self.sizes)
            for which in range(2)
        ]

    def open(self, g):
        for copy in self.near_copies(g):
            copy.start()

    def middle(self, g):
        for copy in self.near_copies(g):
            copy.wait_recv()
        for which in range(2):
            here = self.block(g, which, 2)
            here[...] = (here[...].astype(f32) + self.near[g, which, 1].astype(f32)).astype(bf16)
        for copy in self.far_copies(g):
            copy.start()

    def close(self, g):
        for copy in self.far_copies(g):
            copy.wait_recv()
        for which in range(2):
            total = self.block(g, which, 0)[...].astype(f32) + self.near[g, which, 0].astype(f32)
            total = total + self.far[g, which].astype(f32)
            self.result[pl.ds(which * D + g * GWIDTH, GWIDTH), :] = total.astype(bf16)

    def finish(self):
        for g in range(GROUPS):
            for copy in self.near_copies(g) + self.far_copies(g):
                copy.wait_send()


def backward_kernel(
    sizes, plan, count, steps, q_ref, go_ref, k_ref, v_ref, prob_ref, spread, gather, head, head_t, *refs
):
    sources, refs = refs[:count], refs[count:]
    (gs_ref, gq_ref, own_ref), refs = refs[:3], refs[3:]
    results, refs = refs[:count], refs[count:]
    (key_sum, value_sum, outbox, near, far), refs = refs[:5], refs[5:]
    near_sems, far_sems, scratch = refs[:2], refs[2:4], refs[4:]
    group, part, parts = pl.program_id(0), pl.program_id(1), steps // GROUPS
    step = group * parts + part
    place = my_place(sizes)
    block = BlockSum(outbox, near, far, own_ref, near_sems, far_sems, place, sizes)
    if count:
        opening, turns, closing = stage_turns(scatter_groups(plan, sources, results, scratch, place, sizes))

    @pl.when(step == 0)
    def _():
        partners = axis_partners(place, sizes) if count else [block.beside, block.across]
        meet(partners, sizes)
        if count:
            opening()

    for g in range(1, GROUPS):

        @pl.when((group == g) & (part == 0))
        def _():
            block.middle(g - 1)
            if g >= 2:
                block.close(g - 2)

    if count:
        spread_turns(step, steps, turns, 0, 2)

    wide = ATT_ROWS * GHEADS
    grad_out = lanes_dot(spread[...], go_ref[...]).astype(bf16) * head[...]
    chunk = 256
    for first in range(0, wide, chunk):
        at = slice(first, first + chunk)
        prob = prob_ref[0, at, :].astype(f32)
        grad_prob = dot(grad_out[at], v_ref[...])
        inner = jnp.sum(prob * grad_prob, axis=-1, keepdims=True)
        gs_ref[0, at, :] = (prob * (grad_prob - inner)).astype(bf16)
    if count:
        spread_turns(step, steps, turns, 1, 2)

    grad_query = lanes_dot(k_ref[...], gs_ref[0]) * (HDIM**-0.5)
    gq_ref[...] = lanes_dot(grad_query.astype(bf16) * head_t[...], gather[...]).astype(bf16)
    query_t = lanes_dot(q_ref[...], spread[...]).astype(bf16) * head_t[...]
    grad_out_t = lanes_dot(go_ref[...], spread[...]).astype(bf16) * head_t[...]
    grad_key = dot(query_t, gs_ref[0])
    grad_value = dot(grad_out_t, prob_ref[0])

    @pl.when(part == 0)
    def _():
        key_sum[...] = grad_key
        value_sum[...] = grad_value

    @pl.when(part > 0)
    def _():
        key_sum[...] += grad_key
        value_sum[...] += grad_value

    for g in range(GROUPS):

        @pl.when((group == g) & (part == parts - 1))
        def _():
            outbox[g, 0] = (key_sum[...] * (HDIM**-0.5)).astype(bf16)
            outbox[g, 1] = value_sum[...].astype(bf16)
            block.open(g)

    @pl.when(step == steps - 1)
    def _():
        block.middle(GROUPS - 1)
        block.close(GROUPS - 2)
        if count:
            closing()
        block.close(GROUPS - 1)
        block.finish()


def backward_call(sizes, q_t, go_t, kv_t, prob, tables, arrays, collective):
    rows = q_t.shape[1]
    wide = ATT_ROWS * GHEADS
    parts = rows // ATT_ROWS
    count = len(arrays)
    shapes = scatter_shapes(sizes, arrays)
    plan = scatter_plan(shapes)
    return pl.pallas_call(
        partial(backward_kernel, sizes, plan, count, GROUPS * parts),
        grid=(GROUPS, parts),
        in_specs=[
            pl.BlockSpec((GWIDTH, ATT_ROWS), lambda g, i: (g, i)),
            pl.BlockSpec((GWIDTH, ATT_ROWS), lambda g, i: (g, i)),
            pl.BlockSpec((GWIDTH, BIN), lambda g, i: (g, 0)),
            pl.BlockSpec((GWIDTH, BIN), lambda g, i: (g + GROUPS, 0)),
            pl.BlockSpec((1, wide, BIN), lambda g, i: (g, i, 0)),
        ]
        + table_specs
        + [anywhere] * count,
        out_specs=[
            pl.BlockSpec((1, wide, BIN), lambda g, i: (g, i, 0)),
            pl.BlockSpec((GWIDTH, ATT_ROWS), lambda g, i: (g, i)),
            in_vmem,
        ]
        + [in_vmem] * count,
        out_shape=[
            jax.ShapeDtypeStruct((GROUPS, rows * GHEADS, BIN), bf16),
            jax.ShapeDtypeStruct((D, rows), bf16),
            jax.ShapeDtypeStruct((2 * D, rows), bf16),
        ]
        + [jax.ShapeDtypeStruct(shape, f32) for shape in shapes],
        scratch_shapes=[
            pltpu.VMEM((GWIDTH, BIN), f32),
            pltpu.VMEM((GWIDTH, BIN), f32),
            pltpu.VMEM((GROUPS, 2, GWIDTH, BIN), bf16),
            pltpu.VMEM((GROUPS, 2, 2, GWIDTH, rows), bf16),
            pltpu.VMEM((GROUPS, 2, GWIDTH, rows), bf16),
            pltpu.SemaphoreType.DMA((4 * GROUPS,)),
            pltpu.SemaphoreType.DMA((4 * GROUPS,)),
            pltpu.SemaphoreType.DMA((2 * GROUPS,)),
            pltpu.SemaphoreType.DMA((2 * GROUPS,)),
        ]
        + (scatter_scratch(sizes, plan) if count else []),
        compiler_params=pltpu.CompilerParams(
            collective_id=collective, has_side_effects=True, vmem_limit_bytes=VMEM_LIMIT
        ),
        name="attention_backward",
    )(q_t, go_t, kv_t, kv_t, prob, *tables, *[array.reshape(sizes + shape) for array, shape in zip(arrays, shapes)])


def norm_parts(values):
    middle = values - jnp.mean(values, axis=-1, keepdims=True)
    scale = lax.rsqrt(jnp.mean(middle * middle, axis=-1, keepdims=True) + norm_eps)
    return middle * scale, scale


def norm_back(grad, gain, normal, scale):
    inner = grad * gain
    mean = jnp.mean(inner, axis=-1, keepdims=True)
    along = jnp.mean(inner * normal, axis=-1, keepdims=True)
    return scale * (inner - mean - normal * along)


def column_sums(values):
    return jnp.sum(values, axis=0, keepdims=True)


def feed_kernel(
    steps,
    stream_ref,
    mixed_ref,
    w_out,
    gain,
    shift,
    bias_back,
    cotangent,
    w_in,
    bias_in,
    w_back,
    output_ref,
    grad_in_ref,
    grad_back_ref,
    grad_bias_in_ref,
    grad_stream_ref,
    grad_out_ref,
    grad_mixed_ref,
    grad_gain_ref,
    grad_shift_ref,
    grad_bias_back_ref,
    normal_scr,
    scale_scr,
    second_scr,
    second_t,
    total_scr,
    grad_scr,
):
    step = pl.program_id(0)

    @pl.when(step == 0)
    def _():
        stream = stream_ref[...] + rows_dot(mixed_ref[...], w_out[...])
        normal, scale = norm_parts(stream)
        normal_scr[...] = normal
        scale_scr[...] = jnp.broadcast_to(scale, scale_scr.shape)
        second = (normal * gain[...] + shift[...]).astype(bf16)
        second_scr[...] = second
        second_t[...] = second.T
        total_scr[...] = stream + bias_back[...]
        grad_scr[...] = jnp.zeros_like(grad_scr)

    grad_branch = cotangent[...]
    pre = dot(second_scr[...], w_in[...]) + bias_in[...]
    share = 0.5 * (1.0 + lax.erf(pre * (0.5**0.5)))
    slope = share + pre * (jnp.exp(-0.5 * pre * pre) * (1.0 / math.sqrt(2.0 * math.pi)))
    act = (pre * share).astype(bf16)
    grad_pre = (lanes_dot(grad_branch, w_back[...]) * slope).astype(bf16)
    total_scr[...] += dot(act, w_back[...])
    grad_scr[...] += lanes_dot(grad_pre, w_in[...])
    grad_in_ref[...] = dot(second_t[...], grad_pre).astype(bf16)
    grad_back_ref[...] = rows_dot(act, grad_branch).astype(bf16)
    grad_bias_in_ref[...] = column_sums(grad_pre.astype(f32))

    @pl.when(step == steps - 1)
    def _():
        output_ref[...] = total_scr[...].astype(bf16)
        grad_output = grad_branch.astype(f32)
        grad_second, normal = grad_scr[...], normal_scr[...]
        grad_stream = grad_output + norm_back(grad_second, gain[...], normal, scale_scr[:, 0:1])
        grad_stream_ref[...] = grad_stream
        grad_attn = grad_stream.astype(bf16)
        grad_out_ref[...] = dot(mixed_ref[...], grad_attn).astype(bf16)
        grad_mixed_ref[...] = lanes_dot(w_out[...], grad_attn).astype(bf16)
        grad_gain_ref[...] = column_sums(grad_second * normal)
        grad_shift_ref[...] = column_sums(grad_second)
        grad_bias_back_ref[...] = column_sums(grad_output)


def feed_call(stream_zero, mixed_t, w_out, gain, shift, bias_back, cotangent, w_in, bias_in, w_back):
    rows, hidden = stream_zero.shape[0], w_in.shape[1]
    steps = hidden // FEED_LANES
    row = jax.ShapeDtypeStruct((1, D), f32)
    return pl.pallas_call(
        partial(feed_kernel, steps),
        grid=(steps,),
        in_specs=[in_vmem] * 7
        + [
            pl.BlockSpec((D, FEED_LANES), lambda i: (0, i)),
            pl.BlockSpec((1, FEED_LANES), lambda i: (0, i)),
            pl.BlockSpec((FEED_LANES, D), lambda i: (i, 0)),
        ],
        out_specs=[
            in_vmem,
            pl.BlockSpec((D, FEED_LANES), lambda i: (0, i)),
            pl.BlockSpec((FEED_LANES, D), lambda i: (i, 0)),
            pl.BlockSpec((1, FEED_LANES), lambda i: (0, i)),
        ]
        + [in_vmem] * 6,
        out_shape=[
            jax.ShapeDtypeStruct((rows, D), bf16),
            jax.ShapeDtypeStruct((D, hidden), bf16),
            jax.ShapeDtypeStruct((hidden, D), bf16),
            jax.ShapeDtypeStruct((1, hidden), f32),
            jax.ShapeDtypeStruct((rows, D), f32),
            jax.ShapeDtypeStruct((D, D), bf16),
            jax.ShapeDtypeStruct((D, rows), bf16),
            row,
            row,
            row,
        ],
        scratch_shapes=[
            pltpu.VMEM((rows, D), f32),
            pltpu.VMEM((rows, 128), f32),
            pltpu.VMEM((rows, D), bf16),
            pltpu.VMEM((D, rows), bf16),
            pltpu.VMEM((rows, D), f32),
            pltpu.VMEM((rows, D), f32),
        ],
        compiler_params=pltpu.CompilerParams(vmem_limit_bytes=VMEM_LIMIT),
        name="feed_forward",
    )(stream_zero, mixed_t, w_out, gain, shift, bias_back, cotangent, w_in, bias_in, w_back)


def kernel_gradients(sums, weight_t, mean, width):
    weight_t = weight_t.astype(f32)
    shifted = mean - center
    zeroth, once, twice = (
        jnp.sum(weight_t * sums[at * HEADS : at * HEADS + HEADS], axis=0, keepdims=True) for at in range(3)
    )
    grad_mean = (once - shifted * zeroth) / (width * width)
    grad_width = (twice - 2.0 * shifted * once + shifted * shifted * zeroth) / (width * width * width) - zeroth / width
    return sums[:HEADS], grad_mean, grad_width


def split_small(small, own_hidden):
    rows = small.shape[0]
    vectors = small[:, TFREQ:].T
    return (small[:, :TFREQ].T, *(vectors[at : at + 1] for at in range(5)), vectors[5 : 5 + own_hidden // rows])


def pair_grad_kernel(sizes, plan, count, steps, gs_ref, dist_ref, phi_ref, *refs):
    sources, refs = refs[:count], refs[count:]
    sum_ref, refs = refs[0], refs[1:]
    results, refs = refs[:count], refs[count:]
    (terms, sums), refs = refs[:2], refs[2:]
    step = pl.program_id(0)
    place = my_place(sizes)
    if count:
        total_slots, total_send, total_recv, scratch = refs[:4], refs[4], refs[5], refs[6:]
        total = TotalPart(sums, sum_ref, total_slots, total_send, total_recv, place, sizes)
        opening, turns, closing = stage_turns(scatter_groups(plan, sources, results, scratch, place, sizes))
        tail = min(LAST_TURNS, len(turns))

    @pl.when(step == 0)
    def _():
        sums[...] = jnp.zeros_like(sums)
        if count:
            meet(axis_partners(place, sizes), sizes)
            opening()

    if count:
        spread_turns(step, steps, turns[: len(turns) - tail], 0, 2)

    for u in range(GRAD_ROWS):
        lanes = slice(u * BIN, u * BIN + BIN)
        dist = dist_ref[u : u + 1, :] - center
        for g in range(0, GROUPS, 2):
            low = gs_ref[g, u * GHEADS : u * GHEADS + GHEADS, :].astype(f32)
            high = gs_ref[g + 1, u * GHEADS : u * GHEADS + GHEADS, :].astype(f32)
            grad = jnp.concatenate([low, high], axis=0)
            once = grad * dist
            twice = once * dist
            once_top = once.astype(bf16)
            twice_top = twice.astype(bf16)
            kinds = (
                grad.astype(bf16),
                once_top,
                (once - once_top.astype(f32)).astype(bf16),
                twice_top,
                (twice - twice_top.astype(f32)).astype(bf16),
            )
            for at, kind in enumerate(kinds):
                terms[at * HEADS + g * GHEADS : at * HEADS + (g + 2) * GHEADS, lanes] = kind
    if count:
        spread_turns(step, steps, turns[: len(turns) - tail], 1, 2)

    found = None
    for half in range(GRAD_ROWS // PAIR_ROWS):
        wide = PAIR_ROWS * BIN
        more = lanes_dot(terms[:, half * wide : half * wide + wide], phi_ref[half])
        found = more if found is None else found + more
    sums[:HEADS] += found[:HEADS]
    sums[HEADS : 2 * HEADS] += found[HEADS : 2 * HEADS] + found[2 * HEADS : 3 * HEADS]
    sums[2 * HEADS :] += found[3 * HEADS : 4 * HEADS] + found[4 * HEADS :]

    @pl.when(step == steps - 1)
    def _():
        if not count:
            sum_ref[...] = sums[...]
            return
        total.start(0)
        for at in range(max(tail, 4)):
            if at < tail:
                turns[len(turns) - tail + at]()
            if at < 4:
                total.arrive(at)
                if at < 3:
                    total.start(at + 1)
        closing()
        total.finish()


def pair_grad_call(sizes, gs, dist, phi, arrays, collective):
    rows = dist.shape[0]
    steps = rows // GRAD_ROWS
    count = len(arrays)
    shapes = scatter_shapes(sizes, arrays)
    plan = scatter_plan(shapes)
    total = (3 * HEADS, KERN)
    scratch = [pltpu.VMEM((5 * HEADS, GRAD_ROWS * BIN), bf16), pltpu.VMEM(total, f32)]
    remote = {}
    if count:
        scratch += [pltpu.VMEM((sizes[axis],) + total, f32) for axis in (3, 2, 1, 0)]
        scratch += [pltpu.SemaphoreType.DMA((1, slot_count(sizes)))] * 2
        scratch += scatter_scratch(sizes, plan)
        remote = dict(collective_id=collective, has_side_effects=True)
    return pl.pallas_call(
        partial(pair_grad_kernel, sizes, plan, count, steps),
        grid=(steps,),
        in_specs=[
            pl.BlockSpec((GROUPS, GRAD_ROWS * GHEADS, BIN), lambda i: (0, i, 0)),
            pl.BlockSpec((GRAD_ROWS, BIN), lambda i: (i, 0)),
            pl.BlockSpec((GRAD_ROWS // PAIR_ROWS, KERN, PAIR_ROWS * BIN), lambda i: (i, 0, 0)),
        ]
        + [anywhere] * count,
        out_specs=[in_vmem] * (count + 1),
        out_shape=[jax.ShapeDtypeStruct(total, f32)] + [jax.ShapeDtypeStruct(shape, f32) for shape in shapes],
        scratch_shapes=scratch,
        compiler_params=pltpu.CompilerParams(vmem_limit_bytes=VMEM_LIMIT, **remote),
        name="pair_gradient",
    )(gs, dist, phi, *[array.reshape(sizes + shape) for array, shape in zip(arrays, shapes)])


def settle_kernel(own_hidden, count, sums, weight_t, mean, width, small, *refs):
    values = list(kernel_gradients(sums[...], weight_t[...], mean[...], width[...]))
    values[0] = values[0].T
    values += split_small(small[...], own_hidden)
    for ref, value in zip(refs[count : count + len(values)], values):
        ref[...] = value
    for source, goal in zip(refs[:count], refs[count + len(values) :]):
        goal[...] = source[...]


def settle_call(sums, weight_t, mean, width, small, arrays, own_hidden):
    own = small.shape[0]
    shapes = [(KERN, HEADS), (1, KERN), (1, KERN), (TFREQ, own)] + [(1, own)] * 5 + [(own_hidden // own, own)]
    shapes += [array.shape for array in arrays]
    found = pl.pallas_call(
        partial(settle_kernel, own_hidden, len(arrays)),
        in_specs=[in_vmem] * (5 + len(arrays)),
        out_specs=[in_vmem] * len(shapes),
        out_shape=[jax.ShapeDtypeStruct(shape, f32) for shape in shapes],
        compiler_params=pltpu.CompilerParams(vmem_limit_bytes=VMEM_LIMIT),
        name="settle_gradients",
    )(sums, weight_t, mean, width, small, *arrays)
    return found[:3], found[3:10], found[10:]


def layer_norm(values, norm_gain, norm_offset):
    middle = values - jnp.mean(values, axis=-1, keepdims=True)
    spread = jnp.mean(middle * middle, axis=-1, keepdims=True)
    return middle * lax.rsqrt(spread + norm_eps) * norm_gain + norm_offset


def time_features(time_values):
    half_count = TFREQ // 2
    frequency = jnp.exp(jnp.arange(half_count, dtype=f32) * (-math.log(10000.0) / half_count))
    angles = (1000.0 * time_values)[:, None] * frequency[None, :]
    return jnp.concatenate([jnp.sin(angles), jnp.cos(angles)], axis=1)


def all_scattered(arrays):
    return [lax.psum_scatter(array.astype(f32), ("grp", "dev"), scatter_dimension=0, tiled=True) for array in arrays]


def shards(
    sizes,
    atoms,
    positions,
    segment,
    item_time,
    time_weight,
    norm1_gain,
    norm1_bias,
    qkv_weight,
    out_weight,
    norm2_gain,
    norm2_bias,
    ffn_in,
    ffn_in_bias,
    ffn_out,
    ffn_out_bias,
    pair_weight,
    kernel_mean,
    kernel_width,
    cotangent,
):
    axes = ("grp", "dev")
    own_rows, own_hidden = norm1_gain.shape[0], ffn_in_bias.shape[0]
    mean, width, weight_t = kernel_mean[None], kernel_width[None], pair_weight.T
    vectors = [v[None] for v in (norm1_gain, norm1_bias, norm2_gain, norm2_bias, ffn_out_bias, ffn_in_bias)]
    dist, phi, bias, (small, w_qkv, w_in) = pair_call(
        sizes,
        positions,
        segment.astype(f32)[None],
        mean,
        width,
        weight_t,
        time_weight,
        vectors,
        (qkv_weight, ffn_in,),
        1,
    )
    tables = spread_tables()
    w_qkv, w_in = (full.reshape(-1, full.shape[2]) for full in (w_qkv, w_in))
    w_time_t = small[:, :own_rows].reshape(-1, TFREQ)
    vectors = small[:, own_rows:].astype(f32).transpose(1, 0, 2)
    gain_one, shift_one, gain_two, shift_two, bias_back = (vectors[at, :, :own_rows].reshape(-1) for at in range(5))
    bias_in = vectors[5, :, :own_hidden].reshape(-1)

    features = time_features(item_time).astype(bf16)
    stream_zero = atoms.astype(f32) + lanes_dot(features, w_time_t)
    normed = layer_norm(stream_zero, gain_one, shift_one).astype(bf16)
    packed_t = lax.dot_general(w_qkv, normed, (((0,), (1,)), ((), ())), preferred_element_type=f32).astype(bf16)
    q_t = packed_t[:D]
    mixed_t, prob, kv_t, (w_out, w_back) = forward_call(
        sizes, q_t, packed_t[D:], bias, tables, (out_weight, ffn_out), 5
    )

    (
        output,
        grad_in,
        grad_back,
        grad_bias_in,
        grad_stream_one,
        grad_out_weight,
        grad_mixed_t,
        grad_gain_two,
        grad_shift_two,
        grad_bias_back,
    ) = feed_call(
        stream_zero, mixed_t, w_out, gain_two[None], shift_two[None], bias_back[None], cotangent, w_in, bias_in[None], w_back
    )
    grad_gain_two, grad_shift_two, grad_bias_back = grad_gain_two[0], grad_shift_two[0], grad_bias_back[0]

    own_sums = own_rows % 8 == 0
    early = (grad_back,) if own_sums else ()
    gs, grad_query_t, own, *early_sums = backward_call(sizes, q_t, grad_mixed_t, kv_t, prob, tables, early, 2)
    grad_packed_t = jnp.concatenate([grad_query_t, own], axis=0)
    grad_qkv = lax.dot_general(normed, grad_packed_t, (((0,), (1,)), ((), ())), preferred_element_type=f32).astype(bf16)
    grad_normed = lax.dot_general(grad_packed_t, w_qkv, (((0,), (1,)), ((), ())), preferred_element_type=f32)
    _, norm_one_pull = jax.vjp(layer_norm, stream_zero, gain_one, shift_one)
    grad_zero_part, grad_gain_one, grad_shift_one = norm_one_pull(grad_normed)
    grad_input = grad_stream_one + grad_zero_part
    grad_time_t = rows_dot(grad_input.astype(bf16), features).astype(bf16)

    vectors = jnp.stack([grad_gain_one, grad_shift_one, grad_gain_two, grad_shift_two, grad_bias_back], axis=1)
    vectors = jnp.concatenate([vectors, grad_bias_in.reshape(D // own_rows, -1, own_rows).transpose(0, 2, 1).reshape(D, -1)], axis=1)
    vectors = jnp.pad(vectors, ((0, 0), (0, 128 - vectors.shape[1]))).astype(bf16)
    grad_small = jnp.concatenate([grad_time_t, vectors], axis=1)
    late = (grad_in, grad_out_weight, grad_qkv, grad_small) if own_sums else ()
    sums, *late_sums = pair_grad_call(sizes, gs, dist, phi, late, 3)
    if own_sums:
        grad_small, weight_sums = late_sums[3], (*early_sums, *late_sums[:3])
    else:
        *weight_sums, grad_small = all_scattered((grad_back, grad_in, grad_out_weight, grad_qkv, grad_small))
        sums = lax.psum(sums, axes)
    (grad_pair, grad_mean, grad_width), small_grads, weight_sums = settle_call(
        sums, weight_t, mean, width, grad_small, weight_sums, own_hidden
    )
    grad_back, grad_in, grad_out_weight, grad_qkv = weight_sums
    grad_time, *vector_grads, grad_hidden = small_grads
    grad_gain_one, grad_shift_one, grad_gain_two, grad_shift_two, grad_bias_back = (row[0] for row in vector_grads)
    return (
        output,
        grad_input,
        grad_time,
        grad_gain_one,
        grad_shift_one,
        grad_qkv,
        grad_out_weight,
        grad_gain_two,
        grad_shift_two,
        grad_in,
        grad_hidden.reshape(-1),
        grad_back,
        grad_bias_back,
        grad_pair,
        grad_mean[0],
        grad_width[0],
    )


def solution(mesh):
    in_specs = (
        P(("grp", "dev"), None),
        P(None, ("grp", "dev")),
        P(("grp", "dev")),
        P(("grp", "dev")),
        P(None, ("grp", "dev")),
        P(("grp", "dev")),
        P(("grp", "dev")),
        P(("grp", "dev"), None),
        P(("grp", "dev"), None),
        P(("grp", "dev")),
        P(("grp", "dev")),
        P(("grp", "dev"), None),
        P(("grp", "dev")),
        P(("grp", "dev"), None),
        P(("grp", "dev")),
        P(),
        P(),
        P(),
        P(("grp", "dev"), None),
    )
    out_specs = (
        P(("grp", "dev"), None),
        P(("grp", "dev"), None),
        P(None, ("grp", "dev")),
        P(("grp", "dev")),
        P(("grp", "dev")),
        P(("grp", "dev"), None),
        P(("grp", "dev"), None),
        P(("grp", "dev")),
        P(("grp", "dev")),
        P(("grp", "dev"), None),
        P(("grp", "dev")),
        P(("grp", "dev"), None),
        P(("grp", "dev")),
        P(),
        P(),
        P(),
    )
    return jax.shard_map(partial(shards, grid_of_mesh(mesh)), mesh=mesh, in_specs=in_specs, out_specs=out_specs, check_vma=False)
```

```python
from functools import partial
import itertools
import math

import jax
import jax.numpy as jnp
from jax import lax
from jax.experimental import pallas as pl
from jax.experimental.pallas import tpu as pltpu
from jax.sharding import PartitionSpec as P
import ml_dtypes
import numpy as np

D = 768
HEADS = 32
HDIM = 24
KERN = 128
TFREQ = 128
BIN = 1024
GROUPS = 4
GHEADS = HEADS // GROUPS
GWIDTH = GHEADS * HDIM
PAIR_ROWS = 16
GRAD_ROWS = 32
ATT_ROWS = 128
UNIT_LANES = 768
UNIT_ROWS = 32
FEED_LANES = 512
SLACK = 2
LAST_TURNS = 5
VECTORS = 6

norm_eps = 1e-05
mask_fill = -1e30
log2e = math.log2(math.e)
center = 6.0
f32 = jnp.float32
bf16 = jnp.bfloat16
VMEM_LIMIT = 58 * 1024 * 1024
MESH = pl.DeviceIdType.MESH


def dot(left, right):
    return jnp.dot(left, right, preferred_element_type=f32)


def lanes_dot(left, right):
    return lax.dot_general(left, right, (((1,), (1,)), ((), ())), preferred_element_type=f32)


def rows_dot(left, right):
    return lax.dot_general(left, right, (((0,), (0,)), ((), ())), preferred_element_type=f32)


def grid_of_mesh(mesh):
    count = mesh.shape["dev"] // 2
    wide = 1
    while wide * wide < count:
        wide *= 2
    return mesh.shape["grp"], count // wide, wide, 2


def my_place(sizes):
    _, _, wide, cores = sizes
    dev = lax.axis_index("dev")
    return (lax.axis_index("grp"), dev // (wide * cores), lax.rem(dev // cores, wide), lax.rem(dev, cores))


def device_at(place, sizes):
    _, _, wide, cores = sizes
    return (place[0], (place[1] * wide + place[2]) * cores + place[3])


def other_place(place, axis, shift, sizes):
    moved = list(place)
    moved[axis] = lax.rem(place[axis] + shift, sizes[axis])
    return tuple(moved)


def block_partners(place):
    _, _, x, core = place
    beside, across = 1 - core, x + 1 - 2 * lax.rem(x, 2)
    return (
        place[:3] + (beside,),
        place[:2] + (across, core),
        place[:2] + (across, beside),
    )


def axis_partners(place, sizes):
    return [other_place(place, axis, shift, sizes) for axis in range(4) for shift in range(1, sizes[axis])]


def meet(partners, sizes):
    barrier = pltpu.get_barrier_semaphore()
    for partner in partners:
        pl.semaphore_signal(barrier, inc=1, device_id=device_at(partner, sizes), device_id_type=MESH)
    pl.semaphore_wait(barrier, len(partners))


def send(source, goal, sems, at, partner, sizes):
    return pltpu.make_async_remote_copy(
        src_ref=source,
        dst_ref=goal,
        send_sem=sems[0].at[at],
        recv_sem=sems[1].at[at],
        device_id=device_at(partner, sizes),
        device_id_type=MESH,
    )


class Staged:
    def place_stages(self, order, place, sizes):
        self.order, self.place, self.sizes = order, place, sizes
        self.base = [0]
        for axis in order:
            self.base.append(self.base[-1] + sizes[axis] - 1)

    def copies(self, stage):
        found = []
        for shift in range(1, self.sizes[self.order[stage]]):
            target = other_place(self.place, self.order[stage], shift, self.sizes)
            source, goal = self.ends(stage, shift, target)
            sem = self.base[stage] + shift - 1
            found.append(
                pltpu.make_async_remote_copy(
                    src_ref=source,
                    dst_ref=goal,
                    send_sem=self.send_sem.at[self.at, sem],
                    recv_sem=self.recv_sem.at[self.at, sem],
                    device_id=device_at(target, self.sizes),
                    device_id_type=MESH,
                )
            )
        return found

    def start(self, stage):
        for copy in self.copies(stage):
            copy.start()

    def arrive(self, stage):
        for copy in self.copies(stage):
            copy.wait_recv()

    def finish(self):
        for stage in range(len(self.order)):
            for copy in self.copies(stage):
                copy.wait_send()


class GatherPart(Staged):
    def __init__(self, source, full, rows, lanes, order, at, send_sem, recv_sem, place, sizes):
        self.source, self.full, self.rows, self.lanes = source, full, rows, lanes
        self.at, self.send_sem, self.recv_sem = at, send_sem, recv_sem
        self.place_stages(order, place, sizes)

    def ends(self, stage, shift, target):
        done = self.order[:stage]
        where = tuple(slice(None) if axis in done else self.place[axis] for axis in range(4))
        held = self.full.at[where + (self.rows, self.lanes)]
        return (self.source.at[self.rows, self.lanes] if stage == 0 else held), held


class ScatterPart(Staged):
    def __init__(self, source, result, rows, lanes, order, buffers, at, send_sem, recv_sem, own_sem, place, sizes):
        self.source, self.result, self.rows, self.lanes = source, result, rows, lanes
        self.first, self.slots = buffers[0], buffers[1:]
        self.at, self.send_sem, self.recv_sem, self.own_sem = at, send_sem, recv_sem, own_sem
        self.place_stages(order, place, sizes)

    def pick(self, stage, index):
        if stage == 0:
            where = tuple(index if axis == self.order[0] else slice(None) for axis in range(4))
            return self.source.at[where + (self.rows, self.lanes)]
        holder = self.first if stage == 1 else self.slots[stage - 1].at[0]
        left = [axis for axis in range(4) if axis not in self.order[:stage]]
        return holder.at[tuple(index if axis == self.order[stage] else slice(None) for axis in left)]

    def own_copy(self):
        return pltpu.make_async_copy(self.pick(0, self.place[self.order[0]]), self.first, self.own_sem.at[self.at])

    def ends(self, stage, shift, target):
        return self.pick(stage, target[self.order[stage]]), self.slots[stage].at[shift - 1]

    def start(self, stage):
        if stage == 0:
            self.own_copy().start()
        super().start(stage)

    def arrive(self, stage):
        if stage == 0:
            self.own_copy().wait()
        super().arrive(stage)
        slots = self.slots[stage]
        count = self.sizes[self.order[stage]] - 1
        mine = self.first if stage == 0 else self.pick(stage, self.place[self.order[stage]])
        lead = slots.shape[1:-2]
        if not lead:
            total = mine[...].astype(f32)
            for slot in range(count):
                total = total + slots[slot].astype(f32)
            self.result[self.rows, self.lanes] = total
            return

        def add(outer, carry):
            for inner in itertools.product(*map(range, lead[1:])):
                where = (outer,) + inner
                total = mine[where].astype(f32)
                for slot in range(count):
                    total = total + slots[(slot,) + where].astype(f32)
                if stage == 0:
                    self.first[where] = total.astype(bf16)
                else:
                    slots[(0,) + where] = total.astype(bf16)
            return carry

        lax.fori_loop(0, lead[0], add, 0)


class TotalPart(Staged):
    def __init__(self, source, result, slots, send_sem, recv_sem, place, sizes):
        self.source, self.result, self.slots = source, result, slots
        self.at, self.send_sem, self.recv_sem = 0, send_sem, recv_sem
        self.place_stages((3, 2, 1, 0), place, sizes)

    def ends(self, stage, shift, target):
        mine = self.slots[stage].at[self.place[self.order[stage]]]
        return mine, mine

    def start(self, stage):
        if stage == 0:
            self.slots[0][self.place[3]] = self.source[...]
        super().start(stage)

    def arrive(self, stage):
        super().arrive(stage)
        total = self.slots[stage][0]
        for at in range(1, self.sizes[self.order[stage]]):
            total = total + self.slots[stage][at]
        if stage == 3:
            self.result[...] = total
        else:
            self.slots[stage + 1][self.place[self.order[stage + 1]]] = total


def stage_turns(groups, stages=4, slack=SLACK):
    def opening():
        for group in groups[:slack]:
            for part in group:
                part.start(0)

    def turn(at):
        if at + slack < len(groups):
            for part in groups[at + slack]:
                part.start(0)
        for stage in range(stages - 1, -1, -1):
            index = at - slack * stage
            if 0 <= index < len(groups):
                for part in groups[index]:
                    part.arrive(stage)
                    if stage + 1 < stages:
                        part.start(stage + 1)

    def closing():
        for group in groups:
            for part in group:
                part.finish()

    return opening, [partial(turn, at) for at in range(len(groups) + slack * (stages - 1))], closing


def spread_turns(step, steps, turns, phase=0, phases=1):
    span = steps * phases - 1
    for at in range(steps):
        point = at * phases + phase - 1
        todo = turns[point * len(turns) // span : (point + 1) * len(turns) // span] if point >= 0 else []
        if todo:

            @pl.when(step == at)
            def _():
                for turn in todo:
                    turn()


def pieces(rows, lanes):
    if rows > UNIT_ROWS and rows % UNIT_ROWS == 0:
        return [(at, UNIT_ROWS, 0, lanes) for at in range(0, rows, UNIT_ROWS)]
    if lanes > UNIT_LANES and lanes % UNIT_LANES == 0:
        return [(0, rows, at, UNIT_LANES) for at in range(0, lanes, UNIT_LANES)]
    return [(0, rows, 0, lanes)]


def make_plan(shapes, first_order, second_order):
    plan = []
    for at, (rows, lanes) in enumerate(shapes):
        for row, height, lane, width in pieces(rows, lanes):
            half = width // 256 * 128
            group = [(at, (row, height), (lane + half, width - half), second_order)]
            if half:
                group.insert(0, (at, (row, height), (lane, half), first_order))
            plan.append(group)
    return plan


def part_count(plan):
    return sum(map(len, plan))


def slot_count(sizes):
    return sum(size - 1 for size in sizes)


def gather_plan(shapes):
    return make_plan(shapes, (0, 2, 1, 3), (0, 1, 2, 3))


def gather_groups(plan, sources, fulls, send_sem, recv_sem, place, sizes):
    groups, index = [], 0
    for group in plan:
        groups.append([])
        for at, rows, lanes, order in group:
            groups[-1].append(
                GatherPart(
                    sources[at], fulls[at], pl.ds(*rows), pl.ds(*lanes), order, index, send_sem, recv_sem, place, sizes
                )
            )
            index += 1
    return groups


def scatter_plan(shapes):
    return make_plan(shapes, (3, 2, 1, 0), (3, 1, 2, 0))


def scatter_scratch(sizes, plan):
    parts, slots = part_count(plan), slot_count(sizes)
    scratch = [
        pltpu.SemaphoreType.DMA((parts, slots)),
        pltpu.SemaphoreType.DMA((parts, slots)),
        pltpu.SemaphoreType.DMA((parts,)),
    ]
    for at, rows, lanes, order in sum(plan, []):
        block = (rows[1], lanes[1])
        left = [0, 1, 2, 3]
        for stage, axis in enumerate(order):
            left.remove(axis)
            lead = tuple(sizes[other] for other in left)
            if stage == 0:
                scratch.append(pltpu.VMEM(lead + block, bf16))
            scratch.append(pltpu.VMEM((sizes[axis] - 1,) + lead + block, bf16))
    return scratch


def scatter_groups(plan, sources, results, scratch, place, sizes):
    send_sem, recv_sem, own_sem = scratch[:3]
    groups, index = [], 0
    for group in plan:
        groups.append([])
        for at, rows, lanes, order in group:
            held = scratch[3 + 5 * index : 8 + 5 * index]
            groups[-1].append(
                ScatterPart(
                    sources[at],
                    results[at],
                    pl.ds(*rows),
                    pl.ds(*lanes),
                    order,
                    held,
                    index,
                    send_sem,
                    recv_sem,
                    own_sem,
                    place,
                    sizes,
                )
            )
            index += 1
    return groups


def scatter_shapes(sizes, arrays):
    return [(array.shape[0] // math.prod(sizes), array.shape[1]) for array in arrays]


anywhere = pl.BlockSpec(memory_space=pl.ANY)
in_vmem = pl.BlockSpec(memory_space=pltpu.VMEM)


def pair_block(places_i, keys, coef, weight_t, dist_ref, phi_ref, bias_ref, mask_scr, between):
    square = None
    for axis in range(3):
        gap = places_i[:, axis : axis + 1] - keys[axis : axis + 1, :]
        square = gap * gap if square is None else square + gap * gap
    dist_ref[...] = jnp.sqrt(square)
    mask_scr[...] = jnp.where(places_i[:, 3:4] == keys[3:4, :], 0.0, mask_fill).astype(f32)
    for u in range(PAIR_ROWS):
        if u == PAIR_ROWS // 2:
            between()
        for kg in range(KERN // 16):
            rows = slice(kg * 16, kg * 16 + 16)
            mean, inv, shift = coef[0, rows, :], coef[1, rows, :], coef[2, rows, :]
            for jv in range(BIN // 128):
                z = (dist_ref[u : u + 1, jv * 128 : jv * 128 + 128] - mean) * inv
                lanes = slice(u * BIN + jv * 128, u * BIN + jv * 128 + 128)
                phi_ref[rows, lanes] = jnp.exp2(shift - z * z).astype(bf16)
    bias = dot(weight_t[...], phi_ref[...])
    for u in range(PAIR_ROWS):
        part = bias[:, u * BIN : u * BIN + BIN] * log2e + mask_scr[u : u + 1, :]
        for g in range(GROUPS):
            bias_ref[g, u * GHEADS : u * GHEADS + GHEADS, :] = part[g * GHEADS : g * GHEADS + GHEADS, :]


def pair_kernel(sizes, plan, count, steps, positions, items, mean, width, weight_t, time_weight, *refs):
    vectors, refs = refs[:VECTORS], refs[VECTORS:]
    sources, refs = (refs[-1],) + refs[: count - 1], refs[count - 1 : -1]
    (dist_ref, phi_ref, bias_ref), refs = refs[:3], refs[3:]
    fulls, refs = refs[:count], refs[count:]
    mask_scr, keys, columns, coef, send_sem, recv_sem, own_sem, place_send, place_recv = refs
    step = pl.program_id(0)
    place = my_place(sizes)
    rows = positions.shape[1]
    opening, turns, closing = stage_turns(gather_groups(plan, sources, fulls, send_sem, recv_sem, place, sizes))
    own = [pltpu.make_async_copy(sources[at], fulls[at].at[place], own_sem.at[at]) for at in range(count)]
    shared = [
        send(
            keys.at[:, pl.ds(0, rows)],
            keys.at[:, pl.ds((at + 1) * rows, rows)],
            (place_send, place_recv),
            at,
            partner,
            sizes,
        )
        for at, partner in enumerate(block_partners(place))
    ]

    @pl.when(step == 0)
    def _():
        here = jnp.concatenate([positions[...], items[...], jnp.zeros((4, rows), f32)], axis=0)
        keys[:, pl.ds(0, rows)] = here
        columns[...] = here.T
        square = lambda values: jnp.broadcast_to(values, (KERN, KERN)).T
        coef[0] = square(mean[...])
        coef[1] = square(math.sqrt(0.5 * log2e) / width[...])
        coef[2] = square(-log2e * jnp.log(math.sqrt(2.0 * math.pi) * width[...]))
        mask_scr[...] = jnp.zeros_like(mask_scr)
        for at, vector in enumerate(vectors):
            mask_scr[at : at + 1, pl.ds(0, vector.shape[1])] = vector[...].astype(f32)
        rest = mask_scr[0 : sources[0].shape[0] - time_weight.shape[0], pl.ds(0, TFREQ)]
        sources[0][...] = jnp.concatenate([time_weight[...].astype(f32), rest], axis=0).astype(bf16)
        meet(axis_partners(place, sizes) + [block_partners(place)[2]], sizes)
        for copy in own:
            copy.start()
        for copy in shared:
            copy.start()
        opening()
        for copy in own:
            copy.wait()
        for copy in shared:
            copy.wait()

    spread_turns(step, steps, turns, 0, 2)
    pair_block(
        columns[pl.ds(pl.multiple_of(step * PAIR_ROWS, PAIR_ROWS), PAIR_ROWS), :],
        keys,
        coef,
        weight_t,
        dist_ref,
        phi_ref.at[0],
        bias_ref,
        mask_scr,
        lambda: spread_turns(step, steps, turns, 1, 2),
    )

    @pl.when(step == steps - 1)
    def _():
        closing()


def pair_call(sizes, positions, items, mean, width, weight_t, time_weight, vectors, arrays, collective):
    rows = positions.shape[1]
    count = 1 + len(arrays)
    steps = rows // PAIR_ROWS
    own = time_weight.shape[0]
    small = jax.ShapeDtypeStruct((own + 8, TFREQ), bf16)
    plan = gather_plan([array.shape for array in (small, *arrays)])
    parts, slots = part_count(plan), slot_count(sizes)
    outs = pl.pallas_call(
        partial(pair_kernel, sizes, plan, count, steps),
        grid=(steps,),
        in_specs=[in_vmem] * (6 + VECTORS) + [anywhere] * len(arrays),
        out_specs=[
            pl.BlockSpec((PAIR_ROWS, BIN), lambda i: (i, 0)),
            pl.BlockSpec((1, KERN, PAIR_ROWS * BIN), lambda i: (i, 0, 0)),
            pl.BlockSpec((GROUPS, PAIR_ROWS * GHEADS, BIN), lambda i: (0, i, 0)),
        ]
        + [anywhere] * count,
        out_shape=[
            jax.ShapeDtypeStruct((rows, BIN), f32),
            jax.ShapeDtypeStruct((steps, KERN, PAIR_ROWS * BIN), bf16),
            jax.ShapeDtypeStruct((GROUPS, rows * GHEADS, BIN), f32),
        ]
        + [jax.ShapeDtypeStruct(sizes + array.shape, array.dtype) for array in (small, *arrays)],
        scratch_shapes=[
            pltpu.VMEM((PAIR_ROWS, BIN), f32),
            pltpu.VMEM((8, BIN), f32),
            pltpu.VMEM((rows, 8), f32),
            pltpu.VMEM((3, KERN, KERN), f32),
            pltpu.SemaphoreType.DMA((parts, slots)),
            pltpu.SemaphoreType.DMA((parts, slots)),
            pltpu.SemaphoreType.DMA((count,)),
            pltpu.SemaphoreType.DMA((3,)),
            pltpu.SemaphoreType.DMA((3,)),
            pltpu.VMEM(small.shape, bf16),
        ],
        compiler_params=pltpu.CompilerParams(
            collective_id=collective, has_side_effects=True, vmem_limit_bytes=VMEM_LIMIT
        ),
        name="pair_bias_and_gather",
    )(positions, items, mean, width, weight_t, time_weight, *vectors, *arrays)
    return outs[0], outs[1], outs[2], [full.reshape((-1,) + full.shape[4:]) for full in outs[3:]]


def spread_tables():
    row = np.arange(ATT_ROWS * GHEADS)
    spread = row[:, None] // GHEADS == np.arange(ATT_ROWS)[None, :]
    head = row[:, None] % GHEADS == np.arange(GWIDTH)[None, :] // HDIM
    return tuple(jnp.asarray(table.astype(ml_dtypes.bfloat16)) for table in (spread, spread.T, head, head.T))


table_specs = [in_vmem] * 4


class BlockShare:
    def __init__(self, own, full, far, near, forward, place, sizes):
        self.own, self.full, self.sizes = own, full, sizes
        self.far_sems, self.near_sems, self.forward_sems = far, near, forward
        self.beside, self.across, _ = block_partners(place)
        self.width = own.shape[1]

    def rows(self, g, which):
        return pl.ds(which * D + g * GWIDTH, GWIDTH)

    def own_rows(self, g, which):
        return pl.ds((1 + which) * D + g * GWIDTH, GWIDTH)

    def lanes(self, at):
        return pl.ds(at * self.width, self.width)

    def far(self, g):
        return [
            send(
                self.own.at[self.own_rows(g, which)],
                self.full.at[self.rows(g, which), self.lanes(2)],
                self.far_sems,
                g * 2 + which,
                self.across,
                self.sizes,
            )
            for which in range(2)
        ]

    def near(self, g):
        return [
            send(
                self.own.at[self.own_rows(g, which)],
                self.full.at[self.rows(g, which), self.lanes(1)],
                self.near_sems,
                g * 2 + which,
                self.beside,
                self.sizes,
            )
            for which in range(2)
        ]

    def forward(self, g):
        return [
            send(
                self.full.at[self.rows(g, which), self.lanes(2)],
                self.full.at[self.rows(g, which), self.lanes(3)],
                self.forward_sems,
                g * 2 + which,
                self.beside,
                self.sizes,
            )
            for which in range(2)
        ]

    def open(self):
        for copy in self.far(0) + self.far(1):
            copy.start()
        for g in range(GROUPS):
            for copy in self.near(g):
                copy.start()

    def pass_on(self, g):
        for copy in self.far(g):
            copy.wait_recv()
        for copy in self.forward(g) + (self.far(g + 2) if g + 2 < GROUPS else []):
            copy.start()

    def ready(self, g):
        for copy in self.near(g) + self.forward(g):
            copy.wait_recv()

    def close(self):
        for g in range(GROUPS):
            for copy in self.far(g) + self.near(g) + self.forward(g):
                copy.wait_send()


def forward_kernel(
    sizes, plan, count, parts, q_ref, own_ref, bias_ref, spread, gather, head, head_t, *refs
):
    sources, refs = refs[:count], refs[count:]
    (out_ref, prob_ref, kv_out), refs = refs[:3], refs[3:]
    fulls, refs = refs[:count], refs[count:]
    (kv_ref, out_sems), sems, (send_sem, recv_sem, own_sem) = refs[:2], refs[2:8], refs[8:]
    group, part = pl.program_id(0), pl.program_id(1)
    step, steps = group * parts + part, GROUPS * parts
    place = my_place(sizes)
    share = BlockShare(own_ref, kv_ref, sems[0:2], sems[2:4], sems[4:6], place, sizes)
    opening, turns, closing = stage_turns(gather_groups(plan, sources, fulls, send_sem, recv_sem, place, sizes))
    held = [pltpu.make_async_copy(sources[at], fulls[at].at[place], own_sem.at[at]) for at in range(count)]
    kept = [
        pltpu.make_async_copy(kv_ref.at[share.rows(g, which)], kv_out.at[share.rows(g, which)], out_sems.at[g * 2 + which])
        for g in range(GROUPS)
        for which in range(2)
    ]
    for g in range(GROUPS):

        @pl.when((group == g) & (part == 0))
        def _():
            if g == 0:
                kv_ref[:, pl.ds(0, share.width)] = own_ref[pl.ds(D, 2 * D), :]
                meet(axis_partners(place, sizes), sizes)
                share.open()
                for copy in held:
                    copy.start()
                opening()
                for copy in held:
                    copy.wait()
                share.pass_on(0)
            share.ready(g)
            for copy in kept[2 * g : 2 * g + 2]:
                copy.start()

        if g + 1 < GROUPS:

            @pl.when((group == g) & (part == parts - 1))
            def _():
                share.pass_on(g + 1)

    spread_turns(step, steps, turns, 0, 2)
    first_row = pl.multiple_of(group * GWIDTH, GWIDTH)
    key_rows, value_rows = pl.ds(first_row, GWIDTH), pl.ds(pl.multiple_of(D + first_row, GWIDTH), GWIDTH)
    wide = ATT_ROWS * GHEADS
    query = lanes_dot(spread[...], q_ref[...]).astype(bf16) * head[...]
    chunk = 256
    for first in range(0, wide, chunk):
        at = slice(first, first + chunk)
        score = dot(query[at], kv_ref[key_rows, :]) * (HDIM**-0.5 * log2e) + bias_ref[0, at, :]
        top = jnp.max(score, axis=-1, keepdims=True)
        weight = jnp.exp2(score - top)
        total = jnp.sum(weight, axis=-1, keepdims=True)
        prob_ref[0, at, :] = (weight * (1.0 / total)).astype(bf16)
    spread_turns(step, steps, turns, 1, 2)
    mixed = lanes_dot(kv_ref[value_rows, :], prob_ref[0]).astype(bf16) * head_t[...]
    out_ref[...] = lanes_dot(mixed, gather[...]).astype(bf16)

    @pl.when((group == GROUPS - 1) & (part == parts - 1))
    def _():
        closing()
        share.close()
        for copy in kept:
            copy.wait()


def forward_call(sizes, packed_t, bias, tables, arrays, collective):
    rows = packed_t.shape[1]
    wide = ATT_ROWS * GHEADS
    parts = rows // ATT_ROWS
    count = len(arrays)
    plan = gather_plan([array.shape for array in arrays])
    pieces_held, slots = part_count(plan), slot_count(sizes)
    outs = pl.pallas_call(
        partial(forward_kernel, sizes, plan, count, parts),
        grid=(GROUPS, parts),
        in_specs=[
            pl.BlockSpec((GWIDTH, ATT_ROWS), lambda g, i: (g, i)),
            in_vmem,
            pl.BlockSpec((1, wide, BIN), lambda g, i: (g, i, 0)),
        ]
        + table_specs
        + [anywhere] * count,
        out_specs=[
            pl.BlockSpec((GWIDTH, ATT_ROWS), lambda g, i: (g, i)),
            pl.BlockSpec((1, wide, BIN), lambda g, i: (g, i, 0)),
            anywhere,
        ]
        + [anywhere] * count,
        out_shape=[
            jax.ShapeDtypeStruct((D, rows), bf16),
            jax.ShapeDtypeStruct((GROUPS, rows * GHEADS, BIN), bf16),
            jax.ShapeDtypeStruct((2 * D, BIN), bf16),
        ]
        + [jax.ShapeDtypeStruct(sizes + array.shape, array.dtype) for array in arrays],
        scratch_shapes=[pltpu.VMEM((2 * D, BIN), bf16)]
        + [pltpu.SemaphoreType.DMA((2 * GROUPS,))] * 7
        + [pltpu.SemaphoreType.DMA((pieces_held, slots))] * 2
        + [pltpu.SemaphoreType.DMA((count,))],
        compiler_params=pltpu.CompilerParams(
            collective_id=collective, has_side_effects=True, vmem_limit_bytes=VMEM_LIMIT
        ),
        name="attention_forward",
    )(packed_t, packed_t, bias, *tables, *arrays)
    return outs[0], outs[1], outs[2], [full.reshape((-1, full.shape[-1])) for full in outs[3:]]


class BlockSum:
    def __init__(self, outbox, near, far, result, near_sems, far_sems, place, sizes):
        self.outbox, self.near, self.far, self.result = outbox, near, far, result
        self.near_sems, self.far_sems = near_sems, far_sems
        self.sizes = sizes
        self.beside, self.across, _ = block_partners(place)
        self.width = result.shape[1]

    def block(self, g, which, at):
        return self.outbox.at[g, which, :, pl.ds(at * self.width, self.width)]

    def near_copies(self, g):
        return [
            send(
                self.block(g, which, 2 * slot + 1),
                self.near.at[g, which, slot],
                self.near_sems,
                g * 4 + which * 2 + slot,
                self.beside,
                self.sizes,
            )
            for which in range(2)
            for slot in range(2)
        ]

    def far_copies(self, g):
        return [
            send(self.block(g, which, 2), self.far.at[g, which], self.far_sems, g * 2 + which, self.across, self.sizes)
            for which in range(2)
        ]

    def open(self, g):
        for copy in self.near_copies(g):
            copy.start()

    def middle(self, g):
        for copy in self.near_copies(g):
            copy.wait_recv()
        for which in range(2):
            here = self.block(g, which, 2)
            here[...] = (here[...].astype(f32) + self.near[g, which, 1].astype(f32)).astype(bf16)
        for copy in self.far_copies(g):
            copy.start()

    def close(self, g):
        for copy in self.far_copies(g):
            copy.wait_recv()
        for which in range(2):
            total = self.block(g, which, 0)[...].astype(f32) + self.near[g, which, 0].astype(f32)
            total = total + self.far[g, which].astype(f32)
            self.result[pl.ds((1 + which) * D + g * GWIDTH, GWIDTH), :] = total.astype(bf16)

    def finish(self):
        for g in range(GROUPS):
            for copy in self.near_copies(g) + self.far_copies(g):
                copy.wait_send()


def backward_kernel(
    sizes, plan, count, steps, q_ref, go_ref, k_ref, v_ref, prob_ref, spread, gather, head, head_t, *refs
):
    sources, refs = refs[:count], refs[count:]
    (gs_ref, own_ref), refs = refs[:2], refs[2:]
    results, refs = refs[:count], refs[count:]
    (key_sum, value_sum, outbox, near, far), refs = refs[:5], refs[5:]
    near_sems, far_sems, scratch = refs[:2], refs[2:4], refs[4:]
    group, part, parts = pl.program_id(0), pl.program_id(1), steps // GROUPS
    step = group * parts + part
    place = my_place(sizes)
    block = BlockSum(outbox, near, far, own_ref, near_sems, far_sems, place, sizes)
    if count:
        opening, turns, closing = stage_turns(scatter_groups(plan, sources, results, scratch, place, sizes))

    @pl.when(step == 0)
    def _():
        partners = axis_partners(place, sizes) if count else [block.beside, block.across]
        meet(partners, sizes)
        if count:
            opening()

    for g in range(1, GROUPS):

        @pl.when((group == g) & (part == 0))
        def _():
            block.middle(g - 1)
            if g >= 2:
                block.close(g - 2)

    if count:
        spread_turns(step, steps, turns, 0, 2)

    wide = ATT_ROWS * GHEADS
    grad_out = lanes_dot(spread[...], go_ref[...]).astype(bf16) * head[...]
    chunk = 256
    for first in range(0, wide, chunk):
        at = slice(first, first + chunk)
        prob = prob_ref[0, at, :].astype(f32)
        grad_prob = dot(grad_out[at], v_ref[...])
        inner = jnp.sum(prob * grad_prob, axis=-1, keepdims=True)
        gs_ref[0, at, :] = (prob * (grad_prob - inner)).astype(bf16)
    if count:
        spread_turns(step, steps, turns, 1, 2)

    grad_query = lanes_dot(k_ref[...], gs_ref[0]) * (HDIM**-0.5)
    rows, lanes = pl.multiple_of(group * GWIDTH, GWIDTH), pl.multiple_of(part * ATT_ROWS, ATT_ROWS)
    own_ref[pl.ds(rows, GWIDTH), pl.ds(lanes, ATT_ROWS)] = lanes_dot(
        grad_query.astype(bf16) * head_t[...], gather[...]
    ).astype(bf16)
    query_t = lanes_dot(q_ref[...], spread[...]).astype(bf16) * head_t[...]
    grad_out_t = lanes_dot(go_ref[...], spread[...]).astype(bf16) * head_t[...]
    grad_key = dot(query_t, gs_ref[0])
    grad_value = dot(grad_out_t, prob_ref[0])

    @pl.when(part == 0)
    def _():
        key_sum[...] = grad_key
        value_sum[...] = grad_value

    @pl.when(part > 0)
    def _():
        key_sum[...] += grad_key
        value_sum[...] += grad_value

    for g in range(GROUPS):

        @pl.when((group == g) & (part == parts - 1))
        def _():
            outbox[g, 0] = (key_sum[...] * (HDIM**-0.5)).astype(bf16)
            outbox[g, 1] = value_sum[...].astype(bf16)
            block.open(g)

    @pl.when(step == steps - 1)
    def _():
        block.middle(GROUPS - 1)
        block.close(GROUPS - 2)
        if count:
            closing()
        block.close(GROUPS - 1)
        block.finish()


def backward_call(sizes, q_t, go_t, kv_t, prob, tables, arrays, collective):
    rows = q_t.shape[1]
    wide = ATT_ROWS * GHEADS
    parts = rows // ATT_ROWS
    count = len(arrays)
    shapes = scatter_shapes(sizes, arrays)
    plan = scatter_plan(shapes)
    return pl.pallas_call(
        partial(backward_kernel, sizes, plan, count, GROUPS * parts),
        grid=(GROUPS, parts),
        in_specs=[
            pl.BlockSpec((GWIDTH, ATT_ROWS), lambda g, i: (g, i)),
            pl.BlockSpec((GWIDTH, ATT_ROWS), lambda g, i: (g, i)),
            pl.BlockSpec((GWIDTH, BIN), lambda g, i: (g, 0)),
            pl.BlockSpec((GWIDTH, BIN), lambda g, i: (g + GROUPS, 0)),
            pl.BlockSpec((1, wide, BIN), lambda g, i: (g, i, 0)),
        ]
        + table_specs
        + [anywhere] * count,
        out_specs=[
            pl.BlockSpec((1, wide, BIN), lambda g, i: (g, i, 0)),
            in_vmem,
        ]
        + [in_vmem] * count,
        out_shape=[
            jax.ShapeDtypeStruct((GROUPS, rows * GHEADS, BIN), bf16),
            jax.ShapeDtypeStruct((3 * D, rows), bf16),
        ]
        + [jax.ShapeDtypeStruct(shape, f32) for shape in shapes],
        scratch_shapes=[
            pltpu.VMEM((GWIDTH, BIN), f32),
            pltpu.VMEM((GWIDTH, BIN), f32),
            pltpu.VMEM((GROUPS, 2, GWIDTH, BIN), bf16),
            pltpu.VMEM((GROUPS, 2, 2, GWIDTH, rows), bf16),
            pltpu.VMEM((GROUPS, 2, GWIDTH, rows), bf16),
            pltpu.SemaphoreType.DMA((4 * GROUPS,)),
            pltpu.SemaphoreType.DMA((4 * GROUPS,)),
            pltpu.SemaphoreType.DMA((2 * GROUPS,)),
            pltpu.SemaphoreType.DMA((2 * GROUPS,)),
        ]
        + (scatter_scratch(sizes, plan) if count else []),
        compiler_params=pltpu.CompilerParams(
            collective_id=collective, has_side_effects=True, vmem_limit_bytes=VMEM_LIMIT
        ),
        name="attention_backward",
    )(q_t, go_t, kv_t, kv_t, prob, *tables, *[array.reshape(sizes + shape) for array, shape in zip(arrays, shapes)])


def norm_parts(values):
    middle = values - jnp.mean(values, axis=-1, keepdims=True)
    scale = lax.rsqrt(jnp.mean(middle * middle, axis=-1, keepdims=True) + norm_eps)
    return middle * scale, scale


def norm_back(grad, gain, normal, scale):
    inner = grad * gain
    mean = jnp.mean(inner, axis=-1, keepdims=True)
    along = jnp.mean(inner * normal, axis=-1, keepdims=True)
    return scale * (inner - mean - normal * along)


def column_sums(values):
    return jnp.sum(values, axis=0, keepdims=True)


def feed_kernel(
    steps,
    stream_ref,
    mixed_ref,
    w_out,
    vectors,
    cotangent,
    w_in,
    bias_in,
    w_back,
    output_ref,
    grad_in_ref,
    grad_back_ref,
    grad_bias_in_ref,
    grad_stream_ref,
    grad_out_ref,
    grad_mixed_ref,
    grad_gain_ref,
    grad_shift_ref,
    grad_bias_back_ref,
    normal_scr,
    scale_scr,
    second_scr,
    second_t,
    total_scr,
    grad_scr,
):
    step = pl.program_id(0)
    gain, shift, bias_back = (vectors.at[pl.ds(at, 1)] for at in range(3))

    @pl.when(step == 0)
    def _():
        stream = stream_ref[...] + rows_dot(mixed_ref[...], w_out[...])
        normal, scale = norm_parts(stream)
        normal_scr[...] = normal
        scale_scr[...] = jnp.broadcast_to(scale, scale_scr.shape)
        second = (normal * gain[...] + shift[...]).astype(bf16)
        second_scr[...] = second
        second_t[...] = second.T
        total_scr[...] = stream + bias_back[...]
        grad_scr[...] = jnp.zeros_like(grad_scr)

    grad_branch = cotangent[...]
    pre = dot(second_scr[...], w_in[...]) + bias_in[...]
    share = 0.5 * (1.0 + lax.erf(pre * (0.5**0.5)))
    slope = share + pre * (jnp.exp(-0.5 * pre * pre) * (1.0 / math.sqrt(2.0 * math.pi)))
    act = (pre * share).astype(bf16)
    grad_pre = (lanes_dot(grad_branch, w_back[...]) * slope).astype(bf16)
    total_scr[...] += dot(act, w_back[...])
    grad_scr[...] += lanes_dot(grad_pre, w_in[...])
    grad_in_ref[...] = dot(second_t[...], grad_pre).astype(bf16)
    grad_back_ref[...] = rows_dot(act, grad_branch).astype(bf16)
    grad_bias_in_ref[...] = column_sums(grad_pre.astype(f32))

    @pl.when(step == steps - 1)
    def _():
        output_ref[...] = total_scr[...].astype(bf16)
        grad_output = grad_branch.astype(f32)
        grad_second, normal = grad_scr[...], normal_scr[...]
        grad_stream = grad_output + norm_back(grad_second, gain[...], normal, scale_scr[:, 0:1])
        grad_stream_ref[...] = grad_stream
        grad_attn = grad_stream.astype(bf16)
        grad_out_ref[...] = dot(mixed_ref[...], grad_attn).astype(bf16)
        grad_mixed_ref[...] = lanes_dot(w_out[...], grad_attn).astype(bf16)
        grad_gain_ref[...] = column_sums(grad_second * normal)
        grad_shift_ref[...] = column_sums(grad_second)
        grad_bias_back_ref[...] = column_sums(grad_output)


def feed_call(stream_zero, mixed_t, w_out, vectors, cotangent, w_in, bias_in, w_back):
    rows, hidden = stream_zero.shape[0], w_in.shape[1]
    steps = hidden // FEED_LANES
    row = jax.ShapeDtypeStruct((1, D), f32)
    return pl.pallas_call(
        partial(feed_kernel, steps),
        grid=(steps,),
        in_specs=[in_vmem] * 5
        + [
            pl.BlockSpec((D, FEED_LANES), lambda i: (0, i)),
            pl.BlockSpec((1, FEED_LANES), lambda i: (0, i)),
            pl.BlockSpec((FEED_LANES, D), lambda i: (i, 0)),
        ],
        out_specs=[
            in_vmem,
            pl.BlockSpec((D, FEED_LANES), lambda i: (0, i)),
            pl.BlockSpec((FEED_LANES, D), lambda i: (i, 0)),
            pl.BlockSpec((1, FEED_LANES), lambda i: (0, i)),
        ]
        + [in_vmem] * 6,
        out_shape=[
            jax.ShapeDtypeStruct((rows, D), bf16),
            jax.ShapeDtypeStruct((D, hidden), bf16),
            jax.ShapeDtypeStruct((hidden, D), bf16),
            jax.ShapeDtypeStruct((1, hidden), f32),
            jax.ShapeDtypeStruct((rows, D), f32),
            jax.ShapeDtypeStruct((D, D), bf16),
            jax.ShapeDtypeStruct((D, rows), bf16),
            row,
            row,
            row,
        ],
        scratch_shapes=[
            pltpu.VMEM((rows, D), f32),
            pltpu.VMEM((rows, 128), f32),
            pltpu.VMEM((rows, D), bf16),
            pltpu.VMEM((D, rows), bf16),
            pltpu.VMEM((rows, D), f32),
            pltpu.VMEM((rows, D), f32),
        ],
        compiler_params=pltpu.CompilerParams(vmem_limit_bytes=VMEM_LIMIT),
        name="feed_forward",
    )(stream_zero, mixed_t, w_out, vectors, cotangent, w_in, bias_in, w_back)


def kernel_gradients(sums, weight_t, mean, width):
    weight_t = weight_t.astype(f32)
    shifted = mean - center
    zeroth, once, twice = (
        jnp.sum(weight_t * sums[at * HEADS : at * HEADS + HEADS], axis=0, keepdims=True) for at in range(3)
    )
    grad_mean = (once - shifted * zeroth) / (width * width)
    grad_width = (twice - 2.0 * shifted * once + shifted * shifted * zeroth) / (width * width * width) - zeroth / width
    return sums[:HEADS], grad_mean, grad_width


def split_small(small, own_hidden):
    rows = small.shape[0]
    vectors = small[:, TFREQ:].T
    return (small[:, :TFREQ], *(vectors[at : at + 1] for at in range(5)), vectors[5 : 5 + own_hidden // rows])


def pair_grad_kernel(sizes, plan, count, steps, gs_ref, dist_ref, phi_ref, *refs):
    sources, refs = refs[:count], refs[count:]
    sum_ref, refs = refs[0], refs[1:]
    results, refs = refs[:count], refs[count:]
    (terms, sums), refs = refs[:2], refs[2:]
    step = pl.program_id(0)
    place = my_place(sizes)
    if count:
        total_slots, total_send, total_recv, scratch = refs[:4], refs[4], refs[5], refs[6:]
        total = TotalPart(sums, sum_ref, total_slots, total_send, total_recv, place, sizes)
        opening, turns, closing = stage_turns(scatter_groups(plan, sources, results, scratch, place, sizes))
        tail = min(LAST_TURNS, len(turns))

    @pl.when(step == 0)
    def _():
        sums[...] = jnp.zeros_like(sums)
        if count:
            meet(axis_partners(place, sizes), sizes)
            opening()

    if count:
        spread_turns(step, steps, turns[: len(turns) - tail], 0, 2)

    for u in range(GRAD_ROWS):
        lanes = slice(u * BIN, u * BIN + BIN)
        dist = dist_ref[u : u + 1, :] - center
        for g in range(0, GROUPS, 2):
            low = gs_ref[g, u * GHEADS : u * GHEADS + GHEADS, :].astype(f32)
            high = gs_ref[g + 1, u * GHEADS : u * GHEADS + GHEADS, :].astype(f32)
            grad = jnp.concatenate([low, high], axis=0)
            once = grad * dist
            twice = once * dist
            once_top = once.astype(bf16)
            twice_top = twice.astype(bf16)
            kinds = (
                grad.astype(bf16),
                once_top,
                (once - once_top.astype(f32)).astype(bf16),
                twice_top,
                (twice - twice_top.astype(f32)).astype(bf16),
            )
            for at, kind in enumerate(kinds):
                terms[at * HEADS + g * GHEADS : at * HEADS + (g + 2) * GHEADS, lanes] = kind
    if count:
        spread_turns(step, steps, turns[: len(turns) - tail], 1, 2)

    found = None
    for half in range(GRAD_ROWS // PAIR_ROWS):
        wide = PAIR_ROWS * BIN
        more = lanes_dot(terms[:, half * wide : half * wide + wide], phi_ref[half])
        found = more if found is None else found + more
    sums[:HEADS] += found[:HEADS]
    sums[HEADS : 2 * HEADS] += found[HEADS : 2 * HEADS] + found[2 * HEADS : 3 * HEADS]
    sums[2 * HEADS :] += found[3 * HEADS : 4 * HEADS] + found[4 * HEADS :]

    @pl.when(step == steps - 1)
    def _():
        if not count:
            sum_ref[...] = sums[...]
            return
        total.start(0)
        for at in range(max(tail, 4)):
            if at < tail:
                turns[len(turns) - tail + at]()
            if at < 4:
                total.arrive(at)
                if at < 3:
                    total.start(at + 1)
        closing()
        total.finish()


def pair_grad_call(sizes, gs, dist, phi, arrays, collective):
    rows = dist.shape[0]
    steps = rows // GRAD_ROWS
    count = len(arrays)
    shapes = scatter_shapes(sizes, arrays)
    plan = scatter_plan(shapes)
    total = (3 * HEADS, KERN)
    scratch = [pltpu.VMEM((5 * HEADS, GRAD_ROWS * BIN), bf16), pltpu.VMEM(total, f32)]
    remote = {}
    if count:
        scratch += [pltpu.VMEM((sizes[axis],) + total, f32) for axis in (3, 2, 1, 0)]
        scratch += [pltpu.SemaphoreType.DMA((1, slot_count(sizes)))] * 2
        scratch += scatter_scratch(sizes, plan)
        remote = dict(collective_id=collective, has_side_effects=True)
    return pl.pallas_call(
        partial(pair_grad_kernel, sizes, plan, count, steps),
        grid=(steps,),
        in_specs=[
            pl.BlockSpec((GROUPS, GRAD_ROWS * GHEADS, BIN), lambda i: (0, i, 0)),
            pl.BlockSpec((GRAD_ROWS, BIN), lambda i: (i, 0)),
            pl.BlockSpec((GRAD_ROWS // PAIR_ROWS, KERN, PAIR_ROWS * BIN), lambda i: (i, 0, 0)),
        ]
        + [anywhere] * count,
        out_specs=[in_vmem] * (count + 1),
        out_shape=[jax.ShapeDtypeStruct(total, f32)] + [jax.ShapeDtypeStruct(shape, f32) for shape in shapes],
        scratch_shapes=scratch,
        compiler_params=pltpu.CompilerParams(vmem_limit_bytes=VMEM_LIMIT, **remote),
        name="pair_gradient",
    )(gs, dist, phi, *[array.reshape(sizes + shape) for array, shape in zip(arrays, shapes)])


def settle_kernel(own_hidden, count, sums, weight_t, mean, width, small, *refs):
    values = list(kernel_gradients(sums[...], weight_t[...], mean[...], width[...]))
    values += split_small(small[...], own_hidden)
    for ref, value in zip(refs[count : count + len(values)], values):
        ref[...] = value
    for source, goal in zip(refs[:count], refs[count + len(values) :]):
        goal[...] = source[...]


def settle_call(sums, weight_t, mean, width, small, arrays, own_hidden):
    own = small.shape[0]
    shapes = [(HEADS, KERN), (1, KERN), (1, KERN), (own, TFREQ)] + [(1, own)] * 5 + [(own_hidden // own, own)]
    shapes += [array.shape for array in arrays]
    found = pl.pallas_call(
        partial(settle_kernel, own_hidden, len(arrays)),
        in_specs=[in_vmem] * (5 + len(arrays)),
        out_specs=[in_vmem] * len(shapes),
        out_shape=[jax.ShapeDtypeStruct(shape, f32) for shape in shapes],
        compiler_params=pltpu.CompilerParams(vmem_limit_bytes=VMEM_LIMIT),
        name="settle_gradients",
    )(sums, weight_t, mean, width, small, *arrays)
    return found[:3], found[3:10], found[10:]


def layer_norm(values, norm_gain, norm_offset):
    middle = values - jnp.mean(values, axis=-1, keepdims=True)
    spread = jnp.mean(middle * middle, axis=-1, keepdims=True)
    return middle * lax.rsqrt(spread + norm_eps) * norm_gain + norm_offset


def time_features(time_values):
    half_count = TFREQ // 2
    frequency = jnp.exp(jnp.arange(half_count, dtype=f32) * (-math.log(10000.0) / half_count))
    angles = (1000.0 * time_values)[:, None] * frequency[None, :]
    return jnp.concatenate([jnp.sin(angles), jnp.cos(angles)], axis=1)


def all_scattered(arrays):
    return [lax.psum_scatter(array.astype(f32), ("grp", "dev"), scatter_dimension=0, tiled=True) for array in arrays]


def shards(
    sizes,
    atoms,
    positions,
    segment,
    item_time,
    time_weight,
    norm1_gain,
    norm1_bias,
    qkv_weight,
    out_weight,
    norm2_gain,
    norm2_bias,
    ffn_in,
    ffn_in_bias,
    ffn_out,
    ffn_out_bias,
    pair_weight,
    kernel_mean,
    kernel_width,
    cotangent,
):
    axes = ("grp", "dev")
    own_rows, own_hidden = norm1_gain.shape[0], ffn_in_bias.shape[0]
    mean, width, weight_t = kernel_mean[None], kernel_width[None], pair_weight.T
    vectors = [v[None] for v in (norm1_gain, norm1_bias, norm2_gain, norm2_bias, ffn_out_bias, ffn_in_bias)]
    dist, phi, bias, (small, w_qkv, w_in) = pair_call(
        sizes,
        positions,
        segment.astype(f32)[None],
        mean,
        width,
        weight_t,
        time_weight.T,
        vectors,
        (qkv_weight, ffn_in,),
        1,
    )
    tables = spread_tables()
    w_qkv, w_in = (full.reshape(-1, full.shape[2]) for full in (w_qkv, w_in))
    w_time_t = small[:, :own_rows].reshape(-1, TFREQ)
    vectors = small[:, own_rows:].astype(f32).transpose(1, 0, 2)
    gain_one, shift_one = (vectors[at, :, :own_rows].reshape(-1) for at in range(2))
    vectors_two = vectors[2:5, :, :own_rows].reshape(3, -1)
    bias_in = vectors[5, :, :own_hidden].reshape(-1)

    features = time_features(item_time).astype(bf16)
    stream_zero = atoms.astype(f32) + lanes_dot(features, w_time_t)
    normed = layer_norm(stream_zero, gain_one, shift_one).astype(bf16)
    packed_t = lax.dot_general(w_qkv, normed, (((0,), (1,)), ((), ())), preferred_element_type=f32).astype(bf16)
    mixed_t, prob, kv_t, (w_out, w_back) = forward_call(
        sizes, packed_t, bias, tables, (out_weight, ffn_out), 5
    )

    (
        output,
        grad_in,
        grad_back,
        grad_bias_in,
        grad_stream_one,
        grad_out_weight,
        grad_mixed_t,
        grad_gain_two,
        grad_shift_two,
        grad_bias_back,
    ) = feed_call(
        stream_zero, mixed_t, w_out, vectors_two, cotangent, w_in, bias_in[None], w_back
    )
    grad_gain_two, grad_shift_two, grad_bias_back = grad_gain_two[0], grad_shift_two[0], grad_bias_back[0]

    own_sums = own_rows % 8 == 0
    early = (grad_back,) if own_sums else ()
    gs, grad_packed_t, *early_sums = backward_call(sizes, packed_t, grad_mixed_t, kv_t, prob, tables, early, 2)
    grad_qkv = lax.dot_general(normed, grad_packed_t, (((0,), (1,)), ((), ())), preferred_element_type=f32).astype(bf16)
    grad_normed = lax.dot_general(grad_packed_t, w_qkv, (((0,), (1,)), ((), ())), preferred_element_type=f32)
    _, norm_one_pull = jax.vjp(layer_norm, stream_zero, gain_one, shift_one)
    grad_zero_part, grad_gain_one, grad_shift_one = norm_one_pull(grad_normed)
    grad_input = grad_stream_one + grad_zero_part
    grad_time_rows = rows_dot(grad_input.astype(bf16), features).astype(bf16)

    vectors = jnp.stack([grad_gain_one, grad_shift_one, grad_gain_two, grad_shift_two, grad_bias_back], axis=1)
    vectors = jnp.concatenate([vectors, grad_bias_in.reshape(D // own_rows, -1, own_rows).transpose(0, 2, 1).reshape(D, -1)], axis=1)
    vectors = jnp.pad(vectors, ((0, 0), (0, 128 - vectors.shape[1]))).astype(bf16)
    grad_small = jnp.concatenate([grad_time_rows, vectors], axis=1)
    late = (grad_in, grad_out_weight, grad_qkv, grad_small) if own_sums else ()
    sums, *late_sums = pair_grad_call(sizes, gs, dist, phi, late, 3)
    if own_sums:
        grad_small, weight_sums = late_sums[3], (*early_sums, *late_sums[:3])
    else:
        *weight_sums, grad_small = all_scattered((grad_back, grad_in, grad_out_weight, grad_qkv, grad_small))
        sums = lax.psum(sums, axes)
    (grad_pair_t, grad_mean, grad_width), small_grads, weight_sums = settle_call(
        sums, weight_t, mean, width, grad_small, weight_sums, own_hidden
    )
    grad_back, grad_in, grad_out_weight, grad_qkv = weight_sums
    grad_time_t, *vector_grads, grad_hidden = small_grads
    grad_gain_one, grad_shift_one, grad_gain_two, grad_shift_two, grad_bias_back = (row[0] for row in vector_grads)
    return (
        output,
        grad_input,
        grad_time_t.T,
        grad_gain_one,
        grad_shift_one,
        grad_qkv,
        grad_out_weight,
        grad_gain_two,
        grad_shift_two,
        grad_in,
        grad_hidden.reshape(-1),
        grad_back,
        grad_bias_back,
        grad_pair_t.T,
        grad_mean[0],
        grad_width[0],
    )


def solution(mesh):
    in_specs = (
        P(("grp", "dev"), None),
        P(None, ("grp", "dev")),
        P(("grp", "dev")),
        P(("grp", "dev")),
        P(None, ("grp", "dev")),
        P(("grp", "dev")),
        P(("grp", "dev")),
        P(("grp", "dev"), None),
        P(("grp", "dev"), None),
        P(("grp", "dev")),
        P(("grp", "dev")),
        P(("grp", "dev"), None),
        P(("grp", "dev")),
        P(("grp", "dev"), None),
        P(("grp", "dev")),
        P(),
        P(),
        P(),
        P(("grp", "dev"), None),
    )
    out_specs = (
        P(("grp", "dev"), None),
        P(("grp", "dev"), None),
        P(None, ("grp", "dev")),
        P(("grp", "dev")),
        P(("grp", "dev")),
        P(("grp", "dev"), None),
        P(("grp", "dev"), None),
        P(("grp", "dev")),
        P(("grp", "dev")),
        P(("grp", "dev"), None),
        P(("grp", "dev")),
        P(("grp", "dev"), None),
        P(("grp", "dev")),
        P(),
        P(),
        P(),
    )
    return jax.shard_map(partial(shards, grid_of_mesh(mesh)), mesh=mesh, in_specs=in_specs, out_specs=out_specs, check_vma=False)
```

```python
from functools import partial
import itertools
import math

import jax
import jax.numpy as jnp
from jax import lax
from jax.experimental import pallas as pl
from jax.experimental.pallas import tpu as pltpu
from jax.sharding import PartitionSpec as P
import ml_dtypes
import numpy as np

D = 768
HEADS = 32
HDIM = 24
KERN = 128
TFREQ = 128
BIN = 1024
GROUPS = 4
GHEADS = HEADS // GROUPS
GWIDTH = GHEADS * HDIM
PAIR_ROWS = 16
GRAD_ROWS = 32
ATT_ROWS = 128
UNIT_LANES = 768
UNIT_ROWS = 32
FEED_LANES = 1024
SLACK = 2
LAST_TURNS = 5
VECTORS = 6

norm_eps = 1e-05
mask_fill = -1e30
log2e = math.log2(math.e)
center = 6.0
f32 = jnp.float32
bf16 = jnp.bfloat16
VMEM_LIMIT = 58 * 1024 * 1024
MESH = pl.DeviceIdType.MESH


def dot(left, right):
    return jnp.dot(left, right, preferred_element_type=f32)


def lanes_dot(left, right):
    return lax.dot_general(left, right, (((1,), (1,)), ((), ())), preferred_element_type=f32)


def rows_dot(left, right):
    return lax.dot_general(left, right, (((0,), (0,)), ((), ())), preferred_element_type=f32)


def grid_of_mesh(mesh):
    count = mesh.shape["dev"] // 2
    wide = 1
    while wide * wide < count:
        wide *= 2
    return mesh.shape["grp"], count // wide, wide, 2


def my_place(sizes):
    _, _, wide, cores = sizes
    dev = lax.axis_index("dev")
    return (lax.axis_index("grp"), dev // (wide * cores), lax.rem(dev // cores, wide), lax.rem(dev, cores))


def device_at(place, sizes):
    _, _, wide, cores = sizes
    return (place[0], (place[1] * wide + place[2]) * cores + place[3])


def other_place(place, axis, shift, sizes):
    moved = list(place)
    moved[axis] = lax.rem(place[axis] + shift, sizes[axis])
    return tuple(moved)


def block_partners(place):
    _, _, x, core = place
    beside, across = 1 - core, x + 1 - 2 * lax.rem(x, 2)
    return (
        place[:3] + (beside,),
        place[:2] + (across, core),
        place[:2] + (across, beside),
    )


def axis_partners(place, sizes):
    return [other_place(place, axis, shift, sizes) for axis in range(4) for shift in range(1, sizes[axis])]


def meet(partners, sizes):
    barrier = pltpu.get_barrier_semaphore()
    for partner in partners:
        pl.semaphore_signal(barrier, inc=1, device_id=device_at(partner, sizes), device_id_type=MESH)
    pl.semaphore_wait(barrier, len(partners))


def send(source, goal, sems, at, partner, sizes):
    return pltpu.make_async_remote_copy(
        src_ref=source,
        dst_ref=goal,
        send_sem=sems[0].at[at],
        recv_sem=sems[1].at[at],
        device_id=device_at(partner, sizes),
        device_id_type=MESH,
    )


class Staged:
    def place_stages(self, order, place, sizes):
        self.order, self.place, self.sizes = order, place, sizes
        self.base = [0]
        for axis in order:
            self.base.append(self.base[-1] + sizes[axis] - 1)

    def copies(self, stage):
        found = []
        for shift in range(1, self.sizes[self.order[stage]]):
            target = other_place(self.place, self.order[stage], shift, self.sizes)
            source, goal = self.ends(stage, shift, target)
            sem = self.base[stage] + shift - 1
            found.append(
                pltpu.make_async_remote_copy(
                    src_ref=source,
                    dst_ref=goal,
                    send_sem=self.send_sem.at[self.at, sem],
                    recv_sem=self.recv_sem.at[self.at, sem],
                    device_id=device_at(target, self.sizes),
                    device_id_type=MESH,
                )
            )
        return found

    def start(self, stage):
        for copy in self.copies(stage):
            copy.start()

    def arrive(self, stage):
        for copy in self.copies(stage):
            copy.wait_recv()

    def finish(self):
        for stage in range(len(self.order)):
            for copy in self.copies(stage):
                copy.wait_send()


class GatherPart(Staged):
    def __init__(self, source, full, rows, lanes, order, at, send_sem, recv_sem, place, sizes):
        self.source, self.full, self.rows, self.lanes = source, full, rows, lanes
        self.at, self.send_sem, self.recv_sem = at, send_sem, recv_sem
        self.place_stages(order, place, sizes)

    def ends(self, stage, shift, target):
        done = self.order[:stage]
        where = tuple(slice(None) if axis in done else self.place[axis] for axis in range(4))
        held = self.full.at[where + (self.rows, self.lanes)]
        return (self.source.at[self.rows, self.lanes] if stage == 0 else held), held


class ScatterPart(Staged):
    def __init__(self, source, result, rows, lanes, order, buffers, at, send_sem, recv_sem, own_sem, place, sizes):
        self.source, self.result, self.rows, self.lanes = source, result, rows, lanes
        self.first, self.slots = buffers[0], buffers[1:]
        self.at, self.send_sem, self.recv_sem, self.own_sem = at, send_sem, recv_sem, own_sem
        self.place_stages(order, place, sizes)

    def pick(self, stage, index):
        if stage == 0:
            where = tuple(index if axis == self.order[0] else slice(None) for axis in range(4))
            return self.source.at[where + (self.rows, self.lanes)]
        holder = self.first if stage == 1 else self.slots[stage - 1].at[0]
        left = [axis for axis in range(4) if axis not in self.order[:stage]]
        return holder.at[tuple(index if axis == self.order[stage] else slice(None) for axis in left)]

    def own_copy(self):
        return pltpu.make_async_copy(self.pick(0, self.place[self.order[0]]), self.first, self.own_sem.at[self.at])

    def ends(self, stage, shift, target):
        return self.pick(stage, target[self.order[stage]]), self.slots[stage].at[shift - 1]

    def start(self, stage):
        if stage == 0:
            self.own_copy().start()
        super().start(stage)

    def arrive(self, stage):
        if stage == 0:
            self.own_copy().wait()
        super().arrive(stage)
        slots = self.slots[stage]
        count = self.sizes[self.order[stage]] - 1
        mine = self.first if stage == 0 else self.pick(stage, self.place[self.order[stage]])
        lead = slots.shape[1:-2]
        if not lead:
            total = mine[...].astype(f32)
            for slot in range(count):
                total = total + slots[slot].astype(f32)
            self.result[self.rows, self.lanes] = total
            return

        def add(outer, carry):
            for inner in itertools.product(*map(range, lead[1:])):
                where = (outer,) + inner
                total = mine[where].astype(f32)
                for slot in range(count):
                    total = total + slots[(slot,) + where].astype(f32)
                if stage == 0:
                    self.first[where] = total.astype(bf16)
                else:
                    slots[(0,) + where] = total.astype(bf16)
            return carry

        lax.fori_loop(0, lead[0], add, 0)


class TotalPart(Staged):
    def __init__(self, source, result, slots, send_sem, recv_sem, place, sizes):
        self.source, self.result, self.slots = source, result, slots
        self.at, self.send_sem, self.recv_sem = 0, send_sem, recv_sem
        self.place_stages((3, 2, 1, 0), place, sizes)

    def ends(self, stage, shift, target):
        mine = self.slots[stage].at[self.place[self.order[stage]]]
        return mine, mine

    def start(self, stage):
        if stage == 0:
            self.slots[0][self.place[3]] = self.source[...]
        super().start(stage)

    def arrive(self, stage):
        super().arrive(stage)
        total = self.slots[stage][0]
        for at in range(1, self.sizes[self.order[stage]]):
            total = total + self.slots[stage][at]
        if stage == 3:
            self.result[...] = total
        else:
            self.slots[stage + 1][self.place[self.order[stage + 1]]] = total


def stage_turns(groups, stages=4, slack=SLACK):
    def opening():
        for group in groups[:slack]:
            for part in group:
                part.start(0)

    def turn(at):
        if at + slack < len(groups):
            for part in groups[at + slack]:
                part.start(0)
        for stage in range(stages - 1, -1, -1):
            index = at - slack * stage
            if 0 <= index < len(groups):
                for part in groups[index]:
                    part.arrive(stage)
                    if stage + 1 < stages:
                        part.start(stage + 1)

    def closing():
        for group in groups:
            for part in group:
                part.finish()

    return opening, [partial(turn, at) for at in range(len(groups) + slack * (stages - 1))], closing


def spread_turns(step, steps, turns, phase=0, phases=1):
    span = steps * phases - 1
    for at in range(steps):
        point = at * phases + phase - 1
        todo = turns[point * len(turns) // span : (point + 1) * len(turns) // span] if point >= 0 else []
        if todo:

            @pl.when(step == at)
            def _():
                for turn in todo:
                    turn()


def pieces(rows, lanes):
    if rows > UNIT_ROWS and rows % UNIT_ROWS == 0:
        return [(at, UNIT_ROWS, 0, lanes) for at in range(0, rows, UNIT_ROWS)]
    if lanes > UNIT_LANES and lanes % UNIT_LANES == 0:
        return [(0, rows, at, UNIT_LANES) for at in range(0, lanes, UNIT_LANES)]
    return [(0, rows, 0, lanes)]


def make_plan(shapes, first_order, second_order):
    plan = []
    for at, (rows, lanes) in enumerate(shapes):
        for row, height, lane, width in pieces(rows, lanes):
            half = width // 256 * 128
            group = [(at, (row, height), (lane + half, width - half), second_order)]
            if half:
                group.insert(0, (at, (row, height), (lane, half), first_order))
            plan.append(group)
    return plan


def part_count(plan):
    return sum(map(len, plan))


def slot_count(sizes):
    return sum(size - 1 for size in sizes)


def gather_plan(shapes):
    return make_plan(shapes, (0, 2, 1, 3), (0, 1, 2, 3))


def gather_groups(plan, sources, fulls, send_sem, recv_sem, place, sizes):
    groups, index = [], 0
    for group in plan:
        groups.append([])
        for at, rows, lanes, order in group:
            groups[-1].append(
                GatherPart(
                    sources[at], fulls[at], pl.ds(*rows), pl.ds(*lanes), order, index, send_sem, recv_sem, place, sizes
                )
            )
            index += 1
    return groups


def scatter_plan(shapes):
    return make_plan(shapes, (3, 2, 1, 0), (3, 1, 2, 0))


def scatter_scratch(sizes, plan):
    parts, slots = part_count(plan), slot_count(sizes)
    scratch = [
        pltpu.SemaphoreType.DMA((parts, slots)),
        pltpu.SemaphoreType.DMA((parts, slots)),
        pltpu.SemaphoreType.DMA((parts,)),
    ]
    for at, rows, lanes, order in sum(plan, []):
        block = (rows[1], lanes[1])
        left = [0, 1, 2, 3]
        for stage, axis in enumerate(order):
            left.remove(axis)
            lead = tuple(sizes[other] for other in left)
            if stage == 0:
                scratch.append(pltpu.VMEM(lead + block, bf16))
            scratch.append(pltpu.VMEM((sizes[axis] - 1,) + lead + block, bf16))
    return scratch


def scatter_groups(plan, sources, results, scratch, place, sizes):
    send_sem, recv_sem, own_sem = scratch[:3]
    groups, index = [], 0
    for group in plan:
        groups.append([])
        for at, rows, lanes, order in group:
            held = scratch[3 + 5 * index : 8 + 5 * index]
            groups[-1].append(
                ScatterPart(
                    sources[at],
                    results[at],
                    pl.ds(*rows),
                    pl.ds(*lanes),
                    order,
                    held,
                    index,
                    send_sem,
                    recv_sem,
                    own_sem,
                    place,
                    sizes,
                )
            )
            index += 1
    return groups


def scatter_shapes(sizes, arrays):
    return [(array.shape[0] // math.prod(sizes), array.shape[1]) for array in arrays]


anywhere = pl.BlockSpec(memory_space=pl.ANY)
in_vmem = pl.BlockSpec(memory_space=pltpu.VMEM)


def pair_block(places_i, keys, coef, weight_t, dist_ref, phi_ref, bias_ref, mask_scr, between):
    square = None
    for axis in range(3):
        gap = places_i[:, axis : axis + 1] - keys[axis : axis + 1, :]
        square = gap * gap if square is None else square + gap * gap
    dist_ref[...] = jnp.sqrt(square)
    mask_scr[...] = jnp.where(places_i[:, 3:4] == keys[3:4, :], 0.0, mask_fill).astype(f32)
    for u in range(PAIR_ROWS):
        if u == PAIR_ROWS // 2:
            between()
        for kg in range(KERN // 16):
            rows = slice(kg * 16, kg * 16 + 16)
            mean, inv, shift = coef[0, rows, :], coef[1, rows, :], coef[2, rows, :]
            for jv in range(BIN // 128):
                z = (dist_ref[u : u + 1, jv * 128 : jv * 128 + 128] - mean) * inv
                lanes = slice(u * BIN + jv * 128, u * BIN + jv * 128 + 128)
                phi_ref[rows, lanes] = jnp.exp2(shift - z * z).astype(bf16)
    bias = dot(weight_t[...], phi_ref[...])
    for u in range(PAIR_ROWS):
        part = bias[:, u * BIN : u * BIN + BIN] * log2e + mask_scr[u : u + 1, :]
        for g in range(GROUPS):
            bias_ref[g, u * GHEADS : u * GHEADS + GHEADS, :] = part[g * GHEADS : g * GHEADS + GHEADS, :]


def pair_kernel(sizes, plan, count, steps, positions, items, mean, width, weight_t, time_weight, *refs):
    vectors, refs = refs[:VECTORS], refs[VECTORS:]
    sources, refs = (refs[-1],) + refs[: count - 1], refs[count - 1 : -1]
    (dist_ref, phi_ref, bias_ref), refs = refs[:3], refs[3:]
    fulls, refs = refs[:count], refs[count:]
    mask_scr, keys, columns, coef, send_sem, recv_sem, own_sem, place_send, place_recv = refs
    step = pl.program_id(0)
    place = my_place(sizes)
    rows = positions.shape[1]
    opening, turns, closing = stage_turns(gather_groups(plan, sources, fulls, send_sem, recv_sem, place, sizes))
    own = [pltpu.make_async_copy(sources[at], fulls[at].at[place], own_sem.at[at]) for at in range(count)]
    shared = [
        send(
            keys.at[:, pl.ds(0, rows)],
            keys.at[:, pl.ds((at + 1) * rows, rows)],
            (place_send, place_recv),
            at,
            partner,
            sizes,
        )
        for at, partner in enumerate(block_partners(place))
    ]

    @pl.when(step == 0)
    def _():
        here = jnp.concatenate([positions[...], items[...], jnp.zeros((4, rows), f32)], axis=0)
        keys[:, pl.ds(0, rows)] = here
        columns[...] = here.T
        square = lambda values: jnp.broadcast_to(values, (KERN, KERN)).T
        coef[0] = square(mean[...])
        coef[1] = square(math.sqrt(0.5 * log2e) / width[...])
        coef[2] = square(-log2e * jnp.log(math.sqrt(2.0 * math.pi) * width[...]))
        mask_scr[...] = jnp.zeros_like(mask_scr)
        for at, vector in enumerate(vectors):
            mask_scr[at : at + 1, pl.ds(0, vector.shape[1])] = vector[...].astype(f32)
        rest = mask_scr[0 : sources[0].shape[0] - time_weight.shape[0], pl.ds(0, TFREQ)]
        sources[0][...] = jnp.concatenate([time_weight[...].astype(f32), rest], axis=0).astype(bf16)
        meet(axis_partners(place, sizes) + [block_partners(place)[2]], sizes)
        for copy in own:
            copy.start()
        for copy in shared:
            copy.start()
        opening()
        for copy in own:
            copy.wait()
        for copy in shared:
            copy.wait()

    spread_turns(step, steps, turns, 0, 2)
    pair_block(
        columns[pl.ds(pl.multiple_of(step * PAIR_ROWS, PAIR_ROWS), PAIR_ROWS), :],
        keys,
        coef,
        weight_t,
        dist_ref,
        phi_ref.at[0],
        bias_ref,
        mask_scr,
        lambda: spread_turns(step, steps, turns, 1, 2),
    )

    @pl.when(step == steps - 1)
    def _():
        closing()


def pair_call(sizes, positions, items, mean, width, weight_t, time_weight, vectors, arrays, collective):
    rows = positions.shape[1]
    count = 1 + len(arrays)
    steps = rows // PAIR_ROWS
    own = time_weight.shape[0]
    small = jax.ShapeDtypeStruct((own + 8, TFREQ), bf16)
    plan = gather_plan([array.shape for array in (small, *arrays)])
    parts, slots = part_count(plan), slot_count(sizes)
    outs = pl.pallas_call(
        partial(pair_kernel, sizes, plan, count, steps),
        grid=(steps,),
        in_specs=[in_vmem] * (6 + VECTORS) + [anywhere] * len(arrays),
        out_specs=[
            pl.BlockSpec((PAIR_ROWS, BIN), lambda i: (i, 0)),
            pl.BlockSpec((1, KERN, PAIR_ROWS * BIN), lambda i: (i, 0, 0)),
            pl.BlockSpec((GROUPS, PAIR_ROWS * GHEADS, BIN), lambda i: (0, i, 0)),
        ]
        + [anywhere] * count,
        out_shape=[
            jax.ShapeDtypeStruct((rows, BIN), f32),
            jax.ShapeDtypeStruct((steps, KERN, PAIR_ROWS * BIN), bf16),
            jax.ShapeDtypeStruct((GROUPS, rows * GHEADS, BIN), f32),
        ]
        + [jax.ShapeDtypeStruct(sizes + array.shape, array.dtype) for array in (small, *arrays)],
        scratch_shapes=[
            pltpu.VMEM((PAIR_ROWS, BIN), f32),
            pltpu.VMEM((8, BIN), f32),
            pltpu.VMEM((rows, 8), f32),
            pltpu.VMEM((3, KERN, KERN), f32),
            pltpu.SemaphoreType.DMA((parts, slots)),
            pltpu.SemaphoreType.DMA((parts, slots)),
            pltpu.SemaphoreType.DMA((count,)),
            pltpu.SemaphoreType.DMA((3,)),
            pltpu.SemaphoreType.DMA((3,)),
            pltpu.VMEM(small.shape, bf16),
        ],
        compiler_params=pltpu.CompilerParams(
            collective_id=collective, has_side_effects=True, vmem_limit_bytes=VMEM_LIMIT
        ),
        name="pair_bias_and_gather",
    )(positions, items, mean, width, weight_t, time_weight, *vectors, *arrays)
    return outs[0], outs[1], outs[2], [full.reshape((-1,) + full.shape[4:]) for full in outs[3:]]


def spread_tables():
    row = np.arange(ATT_ROWS * GHEADS)
    spread = row[:, None] // GHEADS == np.arange(ATT_ROWS)[None, :]
    head = row[:, None] % GHEADS == np.arange(GWIDTH)[None, :] // HDIM
    return tuple(jnp.asarray(table.astype(ml_dtypes.bfloat16)) for table in (spread, spread.T, head, head.T))


table_specs = [in_vmem] * 4


class BlockShare:
    def __init__(self, own, full, far, near, forward, place, sizes):
        self.own, self.full, self.sizes = own, full, sizes
        self.far_sems, self.near_sems, self.forward_sems = far, near, forward
        self.beside, self.across, _ = block_partners(place)
        self.width = own.shape[1]

    def rows(self, g, which):
        return pl.ds(which * D + g * GWIDTH, GWIDTH)

    def own_rows(self, g, which):
        return pl.ds((1 + which) * D + g * GWIDTH, GWIDTH)

    def lanes(self, at):
        return pl.ds(at * self.width, self.width)

    def far(self, g):
        return [
            send(
                self.own.at[self.own_rows(g, which)],
                self.full.at[self.rows(g, which), self.lanes(2)],
                self.far_sems,
                g * 2 + which,
                self.across,
                self.sizes,
            )
            for which in range(2)
        ]

    def near(self, g):
        return [
            send(
                self.own.at[self.own_rows(g, which)],
                self.full.at[self.rows(g, which), self.lanes(1)],
                self.near_sems,
                g * 2 + which,
                self.beside,
                self.sizes,
            )
            for which in range(2)
        ]

    def forward(self, g):
        return [
            send(
                self.full.at[self.rows(g, which), self.lanes(2)],
                self.full.at[self.rows(g, which), self.lanes(3)],
                self.forward_sems,
                g * 2 + which,
                self.beside,
                self.sizes,
            )
            for which in range(2)
        ]

    def open(self):
        for copy in self.far(0) + self.far(1):
            copy.start()
        for g in range(GROUPS):
            for copy in self.near(g):
                copy.start()

    def pass_on(self, g):
        for copy in self.far(g):
            copy.wait_recv()
        for copy in self.forward(g) + (self.far(g + 2) if g + 2 < GROUPS else []):
            copy.start()

    def ready(self, g):
        for copy in self.near(g) + self.forward(g):
            copy.wait_recv()

    def close(self):
        for g in range(GROUPS):
            for copy in self.far(g) + self.near(g) + self.forward(g):
                copy.wait_send()


def forward_kernel(
    sizes, plan, count, parts, q_ref, own_ref, bias_ref, spread, gather, head, head_t, *refs
):
    sources, refs = refs[:count], refs[count:]
    (out_ref, prob_ref, kv_out), refs = refs[:3], refs[3:]
    fulls, refs = refs[:count], refs[count:]
    (kv_ref, out_sems), sems, (send_sem, recv_sem, own_sem) = refs[:2], refs[2:8], refs[8:]
    group, part = pl.program_id(0), pl.program_id(1)
    step, steps = group * parts + part, GROUPS * parts
    place = my_place(sizes)
    share = BlockShare(own_ref, kv_ref, sems[0:2], sems[2:4], sems[4:6], place, sizes)
    opening, turns, closing = stage_turns(gather_groups(plan, sources, fulls, send_sem, recv_sem, place, sizes))
    held = [pltpu.make_async_copy(sources[at], fulls[at].at[place], own_sem.at[at]) for at in range(count)]
    kept = [
        pltpu.make_async_copy(kv_ref.at[share.rows(g, which)], kv_out.at[share.rows(g, which)], out_sems.at[g * 2 + which])
        for g in range(GROUPS)
        for which in range(2)
    ]
    for g in range(GROUPS):

        @pl.when((group == g) & (part == 0))
        def _():
            if g == 0:
                kv_ref[:, pl.ds(0, share.width)] = own_ref[pl.ds(D, 2 * D), :]
                meet(axis_partners(place, sizes), sizes)
                share.open()
                for copy in held:
                    copy.start()
                opening()
                for copy in held:
                    copy.wait()
                share.pass_on(0)
            share.ready(g)
            for copy in kept[2 * g : 2 * g + 2]:
                copy.start()

        if g + 1 < GROUPS:

            @pl.when((group == g) & (part == parts - 1))
            def _():
                share.pass_on(g + 1)

    spread_turns(step, steps, turns, 0, 2)
    first_row = pl.multiple_of(group * GWIDTH, GWIDTH)
    key_rows, value_rows = pl.ds(first_row, GWIDTH), pl.ds(pl.multiple_of(D + first_row, GWIDTH), GWIDTH)
    wide = ATT_ROWS * GHEADS
    query = lanes_dot(spread[...], q_ref[...]).astype(bf16) * head[...]
    chunk = 256
    for first in range(0, wide, chunk):
        at = slice(first, first + chunk)
        score = dot(query[at], kv_ref[key_rows, :]) * (HDIM**-0.5 * log2e) + bias_ref[0, at, :]
        top = jnp.max(score, axis=-1, keepdims=True)
        weight = jnp.exp2(score - top)
        total = jnp.sum(weight, axis=-1, keepdims=True)
        prob_ref[0, at, :] = (weight * (1.0 / total)).astype(bf16)
    spread_turns(step, steps, turns, 1, 2)
    mixed = lanes_dot(kv_ref[value_rows, :], prob_ref[0]).astype(bf16) * head_t[...]
    out_ref[...] = lanes_dot(mixed, gather[...]).astype(bf16)

    @pl.when((group == GROUPS - 1) & (part == parts - 1))
    def _():
        closing()
        share.close()
        for copy in kept:
            copy.wait()


def forward_call(sizes, packed_t, bias, tables, arrays, collective):
    rows = packed_t.shape[1]
    wide = ATT_ROWS * GHEADS
    parts = rows // ATT_ROWS
    count = len(arrays)
    plan = gather_plan([array.shape for array in arrays])
    pieces_held, slots = part_count(plan), slot_count(sizes)
    outs = pl.pallas_call(
        partial(forward_kernel, sizes, plan, count, parts),
        grid=(GROUPS, parts),
        in_specs=[
            pl.BlockSpec((GWIDTH, ATT_ROWS), lambda g, i: (g, i)),
            in_vmem,
            pl.BlockSpec((1, wide, BIN), lambda g, i: (g, i, 0)),
        ]
        + table_specs
        + [anywhere] * count,
        out_specs=[
            pl.BlockSpec((GWIDTH, ATT_ROWS), lambda g, i: (g, i)),
            pl.BlockSpec((1, wide, BIN), lambda g, i: (g, i, 0)),
            anywhere,
        ]
        + [anywhere] * count,
        out_shape=[
            jax.ShapeDtypeStruct((D, rows), bf16),
            jax.ShapeDtypeStruct((GROUPS, rows * GHEADS, BIN), bf16),
            jax.ShapeDtypeStruct((2 * D, BIN), bf16),
        ]
        + [jax.ShapeDtypeStruct(sizes + array.shape, array.dtype) for array in arrays],
        scratch_shapes=[pltpu.VMEM((2 * D, BIN), bf16)]
        + [pltpu.SemaphoreType.DMA((2 * GROUPS,))] * 7
        + [pltpu.SemaphoreType.DMA((pieces_held, slots))] * 2
        + [pltpu.SemaphoreType.DMA((count,))],
        compiler_params=pltpu.CompilerParams(
            collective_id=collective, has_side_effects=True, vmem_limit_bytes=VMEM_LIMIT
        ),
        name="attention_forward",
    )(packed_t, packed_t, bias, *tables, *arrays)
    return outs[0], outs[1], outs[2], [full.reshape((-1, full.shape[-1])) for full in outs[3:]]


class BlockSum:
    def __init__(self, outbox, near, far, result, near_sems, far_sems, place, sizes):
        self.outbox, self.near, self.far, self.result = outbox, near, far, result
        self.near_sems, self.far_sems = near_sems, far_sems
        self.sizes = sizes
        self.beside, self.across, _ = block_partners(place)
        self.width = result.shape[1]

    def block(self, g, which, at):
        return self.outbox.at[g, which, :, pl.ds(at * self.width, self.width)]

    def near_copies(self, g):
        return [
            send(
                self.block(g, which, 2 * slot + 1),
                self.near.at[g, which, slot],
                self.near_sems,
                g * 4 + which * 2 + slot,
                self.beside,
                self.sizes,
            )
            for which in range(2)
            for slot in range(2)
        ]

    def far_copies(self, g):
        return [
            send(self.block(g, which, 2), self.far.at[g, which], self.far_sems, g * 2 + which, self.across, self.sizes)
            for which in range(2)
        ]

    def open(self, g):
        for copy in self.near_copies(g):
            copy.start()

    def middle(self, g):
        for copy in self.near_copies(g):
            copy.wait_recv()
        for which in range(2):
            here = self.block(g, which, 2)
            here[...] = (here[...].astype(f32) + self.near[g, which, 1].astype(f32)).astype(bf16)
        for copy in self.far_copies(g):
            copy.start()

    def close(self, g):
        for copy in self.far_copies(g):
            copy.wait_recv()
        for which in range(2):
            total = self.block(g, which, 0)[...].astype(f32) + self.near[g, which, 0].astype(f32)
            total = total + self.far[g, which].astype(f32)
            self.result[pl.ds((1 + which) * D + g * GWIDTH, GWIDTH), :] = total.astype(bf16)

    def finish(self):
        for g in range(GROUPS):
            for copy in self.near_copies(g) + self.far_copies(g):
                copy.wait_send()


def backward_kernel(
    sizes, plan, count, steps, q_ref, go_ref, k_ref, v_ref, prob_ref, spread, gather, head, head_t, *refs
):
    sources, refs = refs[:count], refs[count:]
    (gs_ref, own_ref), refs = refs[:2], refs[2:]
    results, refs = refs[:count], refs[count:]
    (key_sum, value_sum, outbox, near, far), refs = refs[:5], refs[5:]
    near_sems, far_sems, scratch = refs[:2], refs[2:4], refs[4:]
    group, part, parts = pl.program_id(0), pl.program_id(1), steps // GROUPS
    step = group * parts + part
    place = my_place(sizes)
    block = BlockSum(outbox, near, far, own_ref, near_sems, far_sems, place, sizes)
    if count:
        opening, turns, closing = stage_turns(scatter_groups(plan, sources, results, scratch, place, sizes), slack=3)

    @pl.when(step == 0)
    def _():
        partners = axis_partners(place, sizes) if count else [block.beside, block.across]
        meet(partners, sizes)
        if count:
            opening()

    for g in range(1, GROUPS):

        @pl.when((group == g) & (part == 0))
        def _():
            block.middle(g - 1)
            if g >= 2:
                block.close(g - 2)

    if count:
        spread_turns(step, steps, turns, 0, 2)

    wide = ATT_ROWS * GHEADS
    grad_out = lanes_dot(spread[...], go_ref[...]).astype(bf16) * head[...]
    chunk = 256
    for first in range(0, wide, chunk):
        at = slice(first, first + chunk)
        prob = prob_ref[0, at, :].astype(f32)
        grad_prob = dot(grad_out[at], v_ref[...])
        inner = jnp.sum(prob * grad_prob, axis=-1, keepdims=True)
        gs_ref[0, at, :] = (prob * (grad_prob - inner)).astype(bf16)
    if count:
        spread_turns(step, steps, turns, 1, 2)

    grad_query = lanes_dot(k_ref[...], gs_ref[0]) * (HDIM**-0.5)
    rows, lanes = pl.multiple_of(group * GWIDTH, GWIDTH), pl.multiple_of(part * ATT_ROWS, ATT_ROWS)
    own_ref[pl.ds(rows, GWIDTH), pl.ds(lanes, ATT_ROWS)] = lanes_dot(
        grad_query.astype(bf16) * head_t[...], gather[...]
    ).astype(bf16)
    query_t = lanes_dot(q_ref[...], spread[...]).astype(bf16) * head_t[...]
    grad_out_t = lanes_dot(go_ref[...], spread[...]).astype(bf16) * head_t[...]
    grad_key = dot(query_t, gs_ref[0])
    grad_value = dot(grad_out_t, prob_ref[0])

    @pl.when(part == 0)
    def _():
        key_sum[...] = grad_key
        value_sum[...] = grad_value

    @pl.when(part > 0)
    def _():
        key_sum[...] += grad_key
        value_sum[...] += grad_value

    for g in range(GROUPS):

        @pl.when((group == g) & (part == parts - 1))
        def _():
            outbox[g, 0] = (key_sum[...] * (HDIM**-0.5)).astype(bf16)
            outbox[g, 1] = value_sum[...].astype(bf16)
            block.open(g)

    @pl.when(step == steps - 1)
    def _():
        block.middle(GROUPS - 1)
        block.close(GROUPS - 2)
        if count:
            closing()
        block.close(GROUPS - 1)
        block.finish()


def backward_call(sizes, q_t, go_t, kv_t, prob, tables, arrays, collective):
    rows = q_t.shape[1]
    wide = ATT_ROWS * GHEADS
    parts = rows // ATT_ROWS
    count = len(arrays)
    shapes = scatter_shapes(sizes, arrays)
    plan = scatter_plan(shapes)
    return pl.pallas_call(
        partial(backward_kernel, sizes, plan, count, GROUPS * parts),
        grid=(GROUPS, parts),
        in_specs=[
            pl.BlockSpec((GWIDTH, ATT_ROWS), lambda g, i: (g, i)),
            pl.BlockSpec((GWIDTH, ATT_ROWS), lambda g, i: (g, i)),
            pl.BlockSpec((GWIDTH, BIN), lambda g, i: (g, 0)),
            pl.BlockSpec((GWIDTH, BIN), lambda g, i: (g + GROUPS, 0)),
            pl.BlockSpec((1, wide, BIN), lambda g, i: (g, i, 0)),
        ]
        + table_specs
        + [anywhere] * count,
        out_specs=[
            pl.BlockSpec((1, wide, BIN), lambda g, i: (g, i, 0)),
            in_vmem,
        ]
        + [in_vmem] * count,
        out_shape=[
            jax.ShapeDtypeStruct((GROUPS, rows * GHEADS, BIN), bf16),
            jax.ShapeDtypeStruct((3 * D, rows), bf16),
        ]
        + [jax.ShapeDtypeStruct(shape, f32) for shape in shapes],
        scratch_shapes=[
            pltpu.VMEM((GWIDTH, BIN), f32),
            pltpu.VMEM((GWIDTH, BIN), f32),
            pltpu.VMEM((GROUPS, 2, GWIDTH, BIN), bf16),
            pltpu.VMEM((GROUPS, 2, 2, GWIDTH, rows), bf16),
            pltpu.VMEM((GROUPS, 2, GWIDTH, rows), bf16),
            pltpu.SemaphoreType.DMA((4 * GROUPS,)),
            pltpu.SemaphoreType.DMA((4 * GROUPS,)),
            pltpu.SemaphoreType.DMA((2 * GROUPS,)),
            pltpu.SemaphoreType.DMA((2 * GROUPS,)),
        ]
        + (scatter_scratch(sizes, plan) if count else []),
        compiler_params=pltpu.CompilerParams(
            collective_id=collective, has_side_effects=True, vmem_limit_bytes=VMEM_LIMIT
        ),
        name="attention_backward",
    )(q_t, go_t, kv_t, kv_t, prob, *tables, *[array.reshape(sizes + shape) for array, shape in zip(arrays, shapes)])


def norm_parts(values):
    middle = values - jnp.mean(values, axis=-1, keepdims=True)
    scale = lax.rsqrt(jnp.mean(middle * middle, axis=-1, keepdims=True) + norm_eps)
    return middle * scale, scale


def norm_back(grad, gain, normal, scale):
    inner = grad * gain
    mean = jnp.mean(inner, axis=-1, keepdims=True)
    along = jnp.mean(inner * normal, axis=-1, keepdims=True)
    return scale * (inner - mean - normal * along)


def column_sums(values):
    return jnp.sum(values, axis=0, keepdims=True)


def feed_kernel(
    steps,
    stream_ref,
    mixed_ref,
    w_out,
    vectors,
    cotangent,
    w_in,
    bias_in,
    w_back,
    output_ref,
    grad_in_ref,
    grad_back_ref,
    grad_bias_in_ref,
    grad_stream_ref,
    grad_out_ref,
    grad_mixed_ref,
    grad_gain_ref,
    grad_shift_ref,
    grad_bias_back_ref,
    normal_scr,
    scale_scr,
    second_scr,
    second_t,
    total_scr,
    grad_scr,
):
    step = pl.program_id(0)
    gain, shift, bias_back = (vectors.at[pl.ds(at, 1)] for at in range(3))

    @pl.when(step == 0)
    def _():
        stream = stream_ref[...] + rows_dot(mixed_ref[...], w_out[...])
        normal, scale = norm_parts(stream)
        normal_scr[...] = normal
        scale_scr[...] = jnp.broadcast_to(scale, scale_scr.shape)
        second = (normal * gain[...] + shift[...]).astype(bf16)
        second_scr[...] = second
        second_t[...] = second.T
        total_scr[...] = stream + bias_back[...]
        grad_scr[...] = jnp.zeros_like(grad_scr)

    grad_branch = cotangent[...]
    pre = dot(second_scr[...], w_in[...]) + bias_in[...]
    share = 0.5 * (1.0 + lax.erf(pre * (0.5**0.5)))
    slope = share + pre * (jnp.exp(-0.5 * pre * pre) * (1.0 / math.sqrt(2.0 * math.pi)))
    act = (pre * share).astype(bf16)
    grad_pre = (lanes_dot(grad_branch, w_back[...]) * slope).astype(bf16)
    total_scr[...] += dot(act, w_back[...])
    grad_scr[...] += lanes_dot(grad_pre, w_in[...])
    grad_in_ref[...] = dot(second_t[...], grad_pre).astype(bf16)
    grad_back_ref[...] = rows_dot(act, grad_branch).astype(bf16)
    grad_bias_in_ref[...] = column_sums(grad_pre.astype(f32))

    @pl.when(step == steps - 1)
    def _():
        output_ref[...] = total_scr[...].astype(bf16)
        grad_output = grad_branch.astype(f32)
        grad_second, normal = grad_scr[...], normal_scr[...]
        grad_stream = grad_output + norm_back(grad_second, gain[...], normal, scale_scr[:, 0:1])
        grad_stream_ref[...] = grad_stream
        grad_attn = grad_stream.astype(bf16)
        grad_out_ref[...] = dot(mixed_ref[...], grad_attn).astype(bf16)
        grad_mixed_ref[...] = lanes_dot(w_out[...], grad_attn).astype(bf16)
        grad_gain_ref[...] = column_sums(grad_second * normal)
        grad_shift_ref[...] = column_sums(grad_second)
        grad_bias_back_ref[...] = column_sums(grad_output)


def feed_call(stream_zero, mixed_t, w_out, vectors, cotangent, w_in, bias_in, w_back):
    rows, hidden = stream_zero.shape[0], w_in.shape[1]
    steps = hidden // FEED_LANES
    row = jax.ShapeDtypeStruct((1, D), f32)
    return pl.pallas_call(
        partial(feed_kernel, steps),
        grid=(steps,),
        in_specs=[in_vmem] * 5
        + [
            pl.BlockSpec((D, FEED_LANES), lambda i: (0, i)),
            pl.BlockSpec((1, FEED_LANES), lambda i: (0, i)),
            pl.BlockSpec((FEED_LANES, D), lambda i: (i, 0)),
        ],
        out_specs=[
            in_vmem,
            pl.BlockSpec((D, FEED_LANES), lambda i: (0, i)),
            pl.BlockSpec((FEED_LANES, D), lambda i: (i, 0)),
            pl.BlockSpec((1, FEED_LANES), lambda i: (0, i)),
        ]
        + [in_vmem] * 6,
        out_shape=[
            jax.ShapeDtypeStruct((rows, D), bf16),
            jax.ShapeDtypeStruct((D, hidden), bf16),
            jax.ShapeDtypeStruct((hidden, D), bf16),
            jax.ShapeDtypeStruct((1, hidden), f32),
            jax.ShapeDtypeStruct((rows, D), f32),
            jax.ShapeDtypeStruct((D, D), bf16),
            jax.ShapeDtypeStruct((D, rows), bf16),
            row,
            row,
            row,
        ],
        scratch_shapes=[
            pltpu.VMEM((rows, D), f32),
            pltpu.VMEM((rows, 128), f32),
            pltpu.VMEM((rows, D), bf16),
            pltpu.VMEM((D, rows), bf16),
            pltpu.VMEM((rows, D), f32),
            pltpu.VMEM((rows, D), f32),
        ],
        compiler_params=pltpu.CompilerParams(vmem_limit_bytes=VMEM_LIMIT),
        name="feed_forward",
    )(stream_zero, mixed_t, w_out, vectors, cotangent, w_in, bias_in, w_back)


def kernel_gradients(sums, weight_t, mean, width):
    weight_t = weight_t.astype(f32)
    shifted = mean - center
    zeroth, once, twice = (
        jnp.sum(weight_t * sums[at * HEADS : at * HEADS + HEADS], axis=0, keepdims=True) for at in range(3)
    )
    grad_mean = (once - shifted * zeroth) / (width * width)
    grad_width = (twice - 2.0 * shifted * once + shifted * shifted * zeroth) / (width * width * width) - zeroth / width
    return sums[:HEADS], grad_mean, grad_width


def split_small(small, own_hidden):
    rows = small.shape[0]
    vectors = small[:, TFREQ:].T
    return (small[:, :TFREQ], *(vectors[at : at + 1] for at in range(5)), vectors[5 : 5 + own_hidden // rows])


def pair_grad_kernel(sizes, plan, count, steps, gs_ref, dist_ref, phi_ref, *refs):
    sources, refs = refs[:count], refs[count:]
    sum_ref, refs = refs[0], refs[1:]
    results, refs = refs[:count], refs[count:]
    (terms, sums), refs = refs[:2], refs[2:]
    step = pl.program_id(0)
    place = my_place(sizes)
    if count:
        total_slots, total_send, total_recv, scratch = refs[:4], refs[4], refs[5], refs[6:]
        total = TotalPart(sums, sum_ref, total_slots, total_send, total_recv, place, sizes)
        opening, turns, closing = stage_turns(scatter_groups(plan, sources, results, scratch, place, sizes))
        tail = min(LAST_TURNS, len(turns))

    @pl.when(step == 0)
    def _():
        sums[...] = jnp.zeros_like(sums)
        if count:
            meet(axis_partners(place, sizes), sizes)
            opening()

    if count:
        spread_turns(step, steps, turns[: len(turns) - tail], 0, 2)

    for u in range(GRAD_ROWS):
        lanes = slice(u * BIN, u * BIN + BIN)
        dist = dist_ref[u : u + 1, :] - center
        for g in range(0, GROUPS, 2):
            low = gs_ref[g, u * GHEADS : u * GHEADS + GHEADS, :].astype(f32)
            high = gs_ref[g + 1, u * GHEADS : u * GHEADS + GHEADS, :].astype(f32)
            grad = jnp.concatenate([low, high], axis=0)
            once = grad * dist
            twice = once * dist
            once_top = once.astype(bf16)
            twice_top = twice.astype(bf16)
            kinds = (
                grad.astype(bf16),
                once_top,
                (once - once_top.astype(f32)).astype(bf16),
                twice_top,
                (twice - twice_top.astype(f32)).astype(bf16),
            )
            for at, kind in enumerate(kinds):
                terms[at * HEADS + g * GHEADS : at * HEADS + (g + 2) * GHEADS, lanes] = kind
    if count:
        spread_turns(step, steps, turns[: len(turns) - tail], 1, 2)

    found = None
    for half in range(GRAD_ROWS // PAIR_ROWS):
        wide = PAIR_ROWS * BIN
        more = lanes_dot(terms[:, half * wide : half * wide + wide], phi_ref[half])
        found = more if found is None else found + more
    sums[:HEADS] += found[:HEADS]
    sums[HEADS : 2 * HEADS] += found[HEADS : 2 * HEADS] + found[2 * HEADS : 3 * HEADS]
    sums[2 * HEADS :] += found[3 * HEADS : 4 * HEADS] + found[4 * HEADS :]

    @pl.when(step == steps - 1)
    def _():
        if not count:
            sum_ref[...] = sums[...]
            return
        total.start(0)
        for at in range(max(tail, 4)):
            if at < tail:
                turns[len(turns) - tail + at]()
            if at < 4:
                total.arrive(at)
                if at < 3:
                    total.start(at + 1)
        closing()
        total.finish()


def pair_grad_call(sizes, gs, dist, phi, arrays, collective):
    rows = dist.shape[0]
    steps = rows // GRAD_ROWS
    count = len(arrays)
    shapes = scatter_shapes(sizes, arrays)
    plan = scatter_plan(shapes)
    total = (3 * HEADS, KERN)
    scratch = [pltpu.VMEM((5 * HEADS, GRAD_ROWS * BIN), bf16), pltpu.VMEM(total, f32)]
    remote = {}
    if count:
        scratch += [pltpu.VMEM((sizes[axis],) + total, f32) for axis in (3, 2, 1, 0)]
        scratch += [pltpu.SemaphoreType.DMA((1, slot_count(sizes)))] * 2
        scratch += scatter_scratch(sizes, plan)
        remote = dict(collective_id=collective, has_side_effects=True)
    return pl.pallas_call(
        partial(pair_grad_kernel, sizes, plan, count, steps),
        grid=(steps,),
        in_specs=[
            pl.BlockSpec((GROUPS, GRAD_ROWS * GHEADS, BIN), lambda i: (0, i, 0)),
            pl.BlockSpec((GRAD_ROWS, BIN), lambda i: (i, 0)),
            pl.BlockSpec((GRAD_ROWS // PAIR_ROWS, KERN, PAIR_ROWS * BIN), lambda i: (i, 0, 0)),
        ]
        + [anywhere] * count,
        out_specs=[in_vmem] * (count + 1),
        out_shape=[jax.ShapeDtypeStruct(total, f32)] + [jax.ShapeDtypeStruct(shape, f32) for shape in shapes],
        scratch_shapes=scratch,
        compiler_params=pltpu.CompilerParams(vmem_limit_bytes=VMEM_LIMIT, **remote),
        name="pair_gradient",
    )(gs, dist, phi, *[array.reshape(sizes + shape) for array, shape in zip(arrays, shapes)])


def settle_kernel(own_hidden, count, sums, weight_t, mean, width, small, *refs):
    values = list(kernel_gradients(sums[...], weight_t[...], mean[...], width[...]))
    values += split_small(small[...], own_hidden)
    for ref, value in zip(refs[count : count + len(values)], values):
        ref[...] = value
    for source, goal in zip(refs[:count], refs[count + len(values) :]):
        goal[...] = source[...]


def settle_call(sums, weight_t, mean, width, small, arrays, own_hidden):
    own = small.shape[0]
    shapes = [(HEADS, KERN), (1, KERN), (1, KERN), (own, TFREQ)] + [(1, own)] * 5 + [(own_hidden // own, own)]
    shapes += [array.shape for array in arrays]
    found = pl.pallas_call(
        partial(settle_kernel, own_hidden, len(arrays)),
        in_specs=[in_vmem] * (5 + len(arrays)),
        out_specs=[in_vmem] * len(shapes),
        out_shape=[jax.ShapeDtypeStruct(shape, f32) for shape in shapes],
        compiler_params=pltpu.CompilerParams(vmem_limit_bytes=VMEM_LIMIT),
        name="settle_gradients",
    )(sums, weight_t, mean, width, small, *arrays)
    return found[:3], found[3:10], found[10:]


def layer_norm(values, norm_gain, norm_offset):
    middle = values - jnp.mean(values, axis=-1, keepdims=True)
    spread = jnp.mean(middle * middle, axis=-1, keepdims=True)
    return middle * lax.rsqrt(spread + norm_eps) * norm_gain + norm_offset


def time_features(time_values):
    half_count = TFREQ // 2
    frequency = jnp.exp(jnp.arange(half_count, dtype=f32) * (-math.log(10000.0) / half_count))
    angles = (1000.0 * time_values)[:, None] * frequency[None, :]
    return jnp.concatenate([jnp.sin(angles), jnp.cos(angles)], axis=1)


def all_scattered(arrays):
    return [lax.psum_scatter(array.astype(f32), ("grp", "dev"), scatter_dimension=0, tiled=True) for array in arrays]


def shards(
    sizes,
    atoms,
    positions,
    segment,
    item_time,
    time_weight,
    norm1_gain,
    norm1_bias,
    qkv_weight,
    out_weight,
    norm2_gain,
    norm2_bias,
    ffn_in,
    ffn_in_bias,
    ffn_out,
    ffn_out_bias,
    pair_weight,
    kernel_mean,
    kernel_width,
    cotangent,
):
    axes = ("grp", "dev")
    own_rows, own_hidden = norm1_gain.shape[0], ffn_in_bias.shape[0]
    mean, width, weight_t = kernel_mean[None], kernel_width[None], pair_weight.T
    vectors = [v[None] for v in (norm1_gain, norm1_bias, norm2_gain, norm2_bias, ffn_out_bias, ffn_in_bias)]
    dist, phi, bias, (small, w_qkv, w_in) = pair_call(
        sizes,
        positions,
        segment.astype(f32)[None],
        mean,
        width,
        weight_t,
        time_weight.T,
        vectors,
        (qkv_weight, ffn_in,),
        1,
    )
    tables = spread_tables()
    w_qkv, w_in = (full.reshape(-1, full.shape[2]) for full in (w_qkv, w_in))
    w_time_t = small[:, :own_rows].reshape(-1, TFREQ)
    vectors = small[:, own_rows:].astype(f32).transpose(1, 0, 2)
    gain_one, shift_one = (vectors[at, :, :own_rows].reshape(-1) for at in range(2))
    vectors_two = vectors[2:5, :, :own_rows].reshape(3, -1)
    bias_in = vectors[5, :, :own_hidden].reshape(-1)

    features = time_features(item_time).astype(bf16)
    stream_zero = atoms.astype(f32) + lanes_dot(features, w_time_t)
    normed = layer_norm(stream_zero, gain_one, shift_one).astype(bf16)
    packed_t = lax.dot_general(w_qkv, normed, (((0,), (1,)), ((), ())), preferred_element_type=f32).astype(bf16)
    mixed_t, prob, kv_t, (w_out, w_back) = forward_call(
        sizes, packed_t, bias, tables, (out_weight, ffn_out), 5
    )

    (
        output,
        grad_in,
        grad_back,
        grad_bias_in,
        grad_stream_one,
        grad_out_weight,
        grad_mixed_t,
        grad_gain_two,
        grad_shift_two,
        grad_bias_back,
    ) = feed_call(
        stream_zero, mixed_t, w_out, vectors_two, cotangent, w_in, bias_in[None], w_back
    )
    grad_gain_two, grad_shift_two, grad_bias_back = grad_gain_two[0], grad_shift_two[0], grad_bias_back[0]

    own_sums = own_rows % 8 == 0
    early = (grad_back,) if own_sums else ()
    gs, grad_packed_t, *early_sums = backward_call(sizes, packed_t, grad_mixed_t, kv_t, prob, tables, early, 2)
    grad_qkv = lax.dot_general(normed, grad_packed_t, (((0,), (1,)), ((), ())), preferred_element_type=f32).astype(bf16)
    grad_normed = lax.dot_general(grad_packed_t, w_qkv, (((0,), (1,)), ((), ())), preferred_element_type=f32)
    _, norm_one_pull = jax.vjp(layer_norm, stream_zero, gain_one, shift_one)
    grad_zero_part, grad_gain_one, grad_shift_one = norm_one_pull(grad_normed)
    grad_input = grad_stream_one + grad_zero_part
    grad_time_rows = rows_dot(grad_input.astype(bf16), features).astype(bf16)

    vectors = jnp.stack([grad_gain_one, grad_shift_one, grad_gain_two, grad_shift_two, grad_bias_back], axis=1)
    vectors = jnp.concatenate([vectors, grad_bias_in.reshape(D // own_rows, -1, own_rows).transpose(0, 2, 1).reshape(D, -1)], axis=1)
    vectors = jnp.pad(vectors, ((0, 0), (0, 128 - vectors.shape[1]))).astype(bf16)
    grad_small = jnp.concatenate([grad_time_rows, vectors], axis=1)
    late = (grad_in, grad_out_weight, grad_qkv, grad_small) if own_sums else ()
    sums, *late_sums = pair_grad_call(sizes, gs, dist, phi, late, 3)
    if own_sums:
        grad_small, weight_sums = late_sums[3], (*early_sums, *late_sums[:3])
    else:
        *weight_sums, grad_small = all_scattered((grad_back, grad_in, grad_out_weight, grad_qkv, grad_small))
        sums = lax.psum(sums, axes)
    (grad_pair_t, grad_mean, grad_width), small_grads, weight_sums = settle_call(
        sums, weight_t, mean, width, grad_small, weight_sums, own_hidden
    )
    grad_back, grad_in, grad_out_weight, grad_qkv = weight_sums
    grad_time_t, *vector_grads, grad_hidden = small_grads
    grad_gain_one, grad_shift_one, grad_gain_two, grad_shift_two, grad_bias_back = (row[0] for row in vector_grads)
    return (
        output,
        grad_input,
        grad_time_t.T,
        grad_gain_one,
        grad_shift_one,
        grad_qkv,
        grad_out_weight,
        grad_gain_two,
        grad_shift_two,
        grad_in,
        grad_hidden.reshape(-1),
        grad_back,
        grad_bias_back,
        grad_pair_t.T,
        grad_mean[0],
        grad_width[0],
    )


def solution(mesh):
    in_specs = (
        P(("grp", "dev"), None),
        P(None, ("grp", "dev")),
        P(("grp", "dev")),
        P(("grp", "dev")),
        P(None, ("grp", "dev")),
        P(("grp", "dev")),
        P(("grp", "dev")),
        P(("grp", "dev"), None),
        P(("grp", "dev"), None),
        P(("grp", "dev")),
        P(("grp", "dev")),
        P(("grp", "dev"), None),
        P(("grp", "dev")),
        P(("grp", "dev"), None),
        P(("grp", "dev")),
        P(),
        P(),
        P(),
        P(("grp", "dev"), None),
    )
    out_specs = (
        P(("grp", "dev"), None),
        P(("grp", "dev"), None),
        P(None, ("grp", "dev")),
        P(("grp", "dev")),
        P(("grp", "dev")),
        P(("grp", "dev"), None),
        P(("grp", "dev"), None),
        P(("grp", "dev")),
        P(("grp", "dev")),
        P(("grp", "dev"), None),
        P(("grp", "dev")),
        P(("grp", "dev"), None),
        P(("grp", "dev")),
        P(),
        P(),
        P(),
    )
    return jax.shard_map(partial(shards, grid_of_mesh(mesh)), mesh=mesh, in_specs=in_specs, out_specs=out_specs, check_vma=False)
```
